32 devices in a mesh: gx: 4 (over x, core), gy: 4 (over z), gz: 2 (over y).
Axes of the slice: x: 2, y: 2, z: 4, core: 2. Of those that a mesh axis runs over, the one named last changes fastest.
Arguments:
- grains: float32 [4, 4, 2, 7, 4096], P('gx', 'gy', 'gz'), as said below
- pairs: int32 [4, 4, 2, 32, 27], P('gx', 'gy', 'gz'), may hold values from -1 to 863, as said below
Outputs:
- fields: float32 [4, 4, 2, 10, 8, 256], P('gx', 'gy', 'gz')
- fits: float32 [4, 4, 2, 256], P('gx', 'gy', None, 'gz')
- inertial: float32 [4, 4, 16, 256], P('gx', 'gy', None, 'gz')
The draws below stay inside these ranges and needn't reach their ends.
Inputs may be any that keep to these rules, and one draw needn't show every extreme that they name: Rows 0 to 2 of a brick's grains lie within the box of side 5 of the tile that its slot holds, inside the brick; row 3 (radius) lies between 0.4 and 0.6; tile slots hold the boxes of a brick in an order drawn per brick. `pairs`: for each tile slot, the slots of all 27 tile boxes touching its box, itself included, in drawn order; -1 where that box lies outside the window.
All inputs are finite; a program needn't handle non-finite values.
Results may differ from the reference program's by a relative error of at most 0.0092.
Values sent between devices are 32-bit elements; how exact they have to be, the bound alone decides.
No kernel may reach another device: no remote copies, remote signals or barrier semaphores. Data moves between devices by JAX's collectives and lax.ppermute only.
A program may use at most 64 MiB of HBM per device.

```python
import math
import jax
import jax.numpy as jnp
from jax import lax

TILE = 128
BOXES_DOWNSLOPE = 8
BOXES_SPANWISE = 2
BOXES_NORMAL = 2
CELLS_PER_EDGE = 4
N_GX = 4
N_GY = 4
N_GZ = 2


TILE_BOX_EDGE = 5.0


def box_slots(key):
    bricks = N_GX * N_GY * N_GZ
    tiles = BOXES_DOWNSLOPE * BOXES_SPANWISE * BOXES_NORMAL
    brick_keys = jax.random.split(jax.random.fold_in(key, 17), bricks)
    return jax.vmap(lambda one_key: jax.random.permutation(one_key, tiles))(brick_keys).astype(jnp.int32)


def draw_grains(key, part):
    tiles = BOXES_DOWNSLOPE * BOXES_SPANWISE * BOXES_NORMAL
    slots = box_slots(key).reshape(N_GX, N_GY, N_GZ, tiles)
    boxes = jnp.repeat(slots, TILE, axis=-1)
    tile_x = (boxes % BOXES_DOWNSLOPE).astype(jnp.float32)
    tile_y = (boxes // BOXES_DOWNSLOPE % BOXES_SPANWISE).astype(jnp.float32)
    tile_z = (boxes // (BOXES_DOWNSLOPE * BOXES_SPANWISE)).astype(jnp.float32)
    shape = boxes.shape
    noise_keys = jax.random.split(jax.random.fold_in(key, 29), 6)
    spots = jax.random.uniform(noise_keys[0], (3,) + shape, jnp.float32)
    pos_x = TILE_BOX_EDGE * (tile_x + spots[0])
    pos_y = TILE_BOX_EDGE * (tile_y + spots[1])
    pos_z = TILE_BOX_EDGE * (tile_z + spots[2])
    radius = jax.random.uniform(noise_keys[1], shape, jnp.float32, 0.4, 0.6)
    brick_z = jnp.arange(N_GZ, dtype=jnp.float32).reshape(1, 1, N_GZ, 1)
    frac = (brick_z * (BOXES_NORMAL * TILE_BOX_EDGE) + pos_z) / (N_GZ * BOXES_NORMAL * TILE_BOX_EDGE)
    stream = 2.0 * (1.0 - (1.0 - frac) ** 1.5) + 0.4 * jax.random.normal(noise_keys[2], shape, jnp.float32)
    cross = 0.4 * jax.random.normal(noise_keys[3], shape, jnp.float32)
    lift = 0.4 * jax.random.normal(noise_keys[4], shape, jnp.float32)
    return jnp.stack([pos_x, pos_y, pos_z, radius, stream, cross, lift], axis=3).astype(jnp.float32)


def draw_pairs(key, part):
    tiles = BOXES_DOWNSLOPE * BOXES_SPANWISE * BOXES_NORMAL
    bricks = N_GX * N_GY * N_GZ
    slots = box_slots(key)
    owners = jnp.argsort(slots, axis=-1).astype(jnp.int32)
    brick_ids = jnp.arange(bricks, dtype=jnp.int32).reshape(bricks, 1, 1)
    brick_a = brick_ids // (N_GY * N_GZ)
    brick_b = brick_ids // N_GZ % N_GY
    brick_c = brick_ids % N_GZ
    boxes = slots[:, :, None]
    glob_x = brick_a * BOXES_DOWNSLOPE + boxes % BOXES_DOWNSLOPE
    glob_y = brick_b * BOXES_SPANWISE + boxes // BOXES_DOWNSLOPE % BOXES_SPANWISE
    glob_z = brick_c * BOXES_NORMAL + boxes // (BOXES_DOWNSLOPE * BOXES_SPANWISE)
    steps_all = jnp.arange(27, dtype=jnp.int32).reshape(1, 1, 27)
    near_x = glob_x + steps_all // 9 - 1
    near_y = glob_y + steps_all // 3 % 3 - 1
    near_z = glob_z + steps_all % 3 - 1
    inside = (near_x >= 0) & (near_x < N_GX * BOXES_DOWNSLOPE) & (near_y >= 0) & (near_y < N_GY * BOXES_SPANWISE) & (near_z >= 0) & (near_z < N_GZ * BOXES_NORMAL)
    clip_x = jnp.clip(near_x, 0, N_GX * BOXES_DOWNSLOPE - 1)
    clip_y = jnp.clip(near_y, 0, N_GY * BOXES_SPANWISE - 1)
    clip_z = jnp.clip(near_z, 0, N_GZ * BOXES_NORMAL - 1)
    other_a = clip_x // BOXES_DOWNSLOPE
    other_b = clip_y // BOXES_SPANWISE
    other_c = clip_z // BOXES_NORMAL
    other_box = clip_x % BOXES_DOWNSLOPE + BOXES_DOWNSLOPE * (clip_y % BOXES_SPANWISE + BOXES_SPANWISE * (clip_z % BOXES_NORMAL))
    other_brick = (other_a * N_GY + other_b) * N_GZ + other_c
    other_slot = owners[other_brick, other_box]
    hood_index = (other_a - brick_a + 1) * 9 + (other_b - brick_b + 1) * 3 + (other_c - brick_c + 1)
    listed = jnp.where(inside, hood_index * tiles + other_slot, -1).astype(jnp.int32)
    order_keys = jax.random.split(jax.random.fold_in(key, 31), bricks * tiles)
    orders = jax.vmap(lambda one_key: jax.random.permutation(one_key, 27))(order_keys).astype(jnp.int32)
    listed = jnp.take_along_axis(listed.reshape(bricks * tiles, 27), orders, axis=1)
    return listed.reshape(N_GX, N_GY, N_GZ, tiles, 27)


def setup_inputs(seed: int = 0) -> dict:
    splits = jax.random.split(jax.random.key(seed), 3)
    grains = draw_grains(jax.random.fold_in(splits[2], 71), 0)
    pairs = draw_pairs(jax.random.fold_in(splits[2], 71), 0)
    return {"grains": grains, "pairs": pairs}


TILE_BOX_EDGE = 5.0
SPRING = 2.0
SOFTEN = 0.05
FLOOR_LEVEL = 0.1
RIDGE_SHARE = 0.1
CUT_LEVEL = math.exp(-12.5)
NORM_ONE = 1.0 / math.sqrt(2.0 * math.pi)

def offset_table():
    steps_all = jnp.arange(27, dtype=jnp.int32)
    shift_a = (steps_all // 9 - 1).astype(jnp.float32) * (BOXES_DOWNSLOPE * TILE_BOX_EDGE)
    shift_b = (steps_all // 3 % 3 - 1).astype(jnp.float32) * (BOXES_SPANWISE * TILE_BOX_EDGE)
    shift_c = (steps_all % 3 - 1).astype(jnp.float32) * (BOXES_NORMAL * TILE_BOX_EDGE)
    return jnp.stack([shift_a, shift_b, shift_c], axis=1)

def contact_stress(hood, partner):
    tiles = BOXES_DOWNSLOPE * BOXES_SPANWISE * BOXES_NORMAL
    shifted = jnp.concatenate([hood[:, :3] + offset_table()[:, :, None], hood[:, 3:4]], axis=1)
    table = shifted.reshape(27, 4, tiles, TILE).transpose(0, 2, 1, 3).reshape(27 * tiles, 4, TILE)
    centre = 13 * tiles
    row_ids = jnp.arange(TILE, dtype=jnp.int32)
    col_ids = jnp.arange(27 * TILE, dtype=jnp.int32) % TILE

    def one_tile(slot):
        own_tile = table[centre + slot]
        partner_ids = partner[slot]
        is_valid = partner_ids >= 0
        safe_ids = jnp.where(is_valid, partner_ids, 0)
        others = table[safe_ids].transpose(1, 0, 2).reshape(4, 27 * TILE)
        live_cols = jnp.repeat(is_valid, TILE)
        same_tile = jnp.repeat(safe_ids == centre + slot, TILE)
        itself = same_tile[None, :] & (col_ids[None, :] == row_ids[:, None])
        keep = live_cols[None, :] & jnp.logical_not(itself)
        delta_x = own_tile[0][:, None] - others[0][None, :]
        delta_y = own_tile[1][:, None] - others[1][None, :]
        delta_z = own_tile[2][:, None] - others[2][None, :]
        distance = jnp.sqrt(delta_x * delta_x + delta_y * delta_y + delta_z * delta_z)
        intersection = jnp.where(keep, jnp.maximum(own_tile[3][:, None] + others[3][None, :] - distance, 0.0), 0.0)
        force = 0.5 * SPRING * intersection / (distance + SOFTEN)
        return jnp.stack([lax.optimization_barrier(jnp.sum(force * delta_x * delta_x, 1)), lax.optimization_barrier(jnp.sum(force * delta_y * delta_y, 1)), lax.optimization_barrier(jnp.sum(force * delta_z * delta_z, 1)), lax.optimization_barrier(jnp.sum(force * delta_x * delta_y, 1)), lax.optimization_barrier(jnp.sum(force * delta_x * delta_z, 1)), lax.optimization_barrier(jnp.sum(force * delta_y * delta_z, 1))])
    blocks = lax.map(one_tile, jnp.arange(tiles, dtype=jnp.int32))
    return blocks.transpose(1, 0, 2).reshape(6, tiles * TILE)

def grain_loads(state, contact):
    radius = state[3]
    masses = 4.0 * math.pi / 3.0 * radius * radius * radius
    vel_u, vel_v, vel_w = (state[4], state[5], state[6])
    kinetic = jnp.stack([vel_u * vel_u, vel_v * vel_v, vel_w * vel_w, vel_u * vel_v, vel_u * vel_w, vel_v * vel_w])
    moments = jnp.stack([masses, masses * vel_u, masses * vel_v, masses * vel_w])
    return jnp.concatenate([moments, contact + masses[None, :] * kinetic], axis=0)

def kernel_rows(coords, centres):
    diff = coords[:, None] - centres[None, :]
    return jnp.maximum(jnp.exp(-0.5 * diff * diff) - CUT_LEVEL, 0.0) * NORM_ONE

def deposit(positions, loads, centres_x, centres_y, centres_z):
    weight_x = kernel_rows(positions[0], centres_x)
    weight_y = kernel_rows(positions[1], centres_y)
    weight_z = kernel_rows(positions[2], centres_z)
    count = positions.shape[1]
    plane = (weight_x[:, :, None] * weight_y[:, None, :]).astype(jnp.bfloat16).reshape(count, -1)
    height = (loads[:, None, :] * weight_z.T[None, :, :]).astype(jnp.bfloat16).reshape(-1, count)
    return jnp.dot(height, plane, preferred_element_type=jnp.float32)

def column_fit(profile):
    cell_pitch = TILE_BOX_EDGE / CELLS_PER_EDGE
    density, velocity, shear, press = (profile[0], profile[1], profile[2], profile[3])
    upper = jnp.concatenate([velocity[..., 1:, :], velocity[..., -1:, :]], axis=-2)
    lower = jnp.concatenate([velocity[..., :1, :], velocity[..., :-1, :]], axis=-2)
    rate = (upper - lower) / (2.0 * cell_pitch)
    inertial = rate * 1.0 / jnp.sqrt((press + FLOOR_LEVEL) / (density + FLOOR_LEVEL))
    friction = shear / (press + FLOOR_LEVEL)
    weight = density + FLOOR_LEVEL
    sum_zero = lax.optimization_barrier(jnp.sum(weight, axis=-2))
    sum_one = lax.optimization_barrier(jnp.sum(weight * inertial, axis=-2))
    sum_two = lax.optimization_barrier(jnp.sum(weight * inertial * inertial, axis=-2)) + RIDGE_SHARE * sum_zero
    mix_zero = lax.optimization_barrier(jnp.sum(weight * friction, axis=-2))
    mix_one = lax.optimization_barrier(jnp.sum(weight * friction * inertial, axis=-2))
    determ = sum_zero * sum_two - sum_one * sum_one
    fitted = jnp.stack([(mix_zero * sum_two - sum_one * mix_one) / determ, (sum_zero * mix_one - sum_one * mix_zero) / determ])
    return (fitted, inertial)

def reference(grains, pairs):
    tiles = BOXES_DOWNSLOPE * BOXES_SPANWISE * BOXES_NORMAL
    grains_all = tiles * TILE
    bricks = N_GX * N_GY * N_GZ
    extent_downslope, extent_spanwise, extent_normal = (CELLS_PER_EDGE * BOXES_DOWNSLOPE, CELLS_PER_EDGE * BOXES_SPANWISE, CELLS_PER_EDGE * BOXES_NORMAL)
    border_extent = CELLS_PER_EDGE
    total_x, total_y, total_z = (extent_downslope * N_GX, extent_spanwise * N_GY, extent_normal * N_GZ)
    cell_pitch = TILE_BOX_EDGE / CELLS_PER_EDGE
    padded = jnp.pad(grains[:, :, :, :4], ((1, 1), (1, 1), (1, 1), (0, 0), (0, 0)))
    flat_pairs = pairs.reshape(bricks, tiles, 27)
    local = grains.reshape(bricks, 7, grains_all)

    def brick_place(index):
        return (index // (N_GY * N_GZ), index // N_GZ % N_GY, index % N_GZ)

    def brick_contact(index):
        pos_a, pos_b, pos_c = brick_place(index)
        zero_i = jnp.zeros((), jnp.int32)
        hood = lax.dynamic_slice(padded, (pos_a.astype(jnp.int32), pos_b.astype(jnp.int32), pos_c.astype(jnp.int32), zero_i, zero_i), (3, 3, 3, 4, grains_all))
        return contact_stress(hood.reshape(27, 4, grains_all), flat_pairs[index])
    contact = lax.map(brick_contact, jnp.arange(bricks, dtype=jnp.int32), batch_size=8)
    loads = jax.vmap(grain_loads)(local, contact)
    centres_x = (jnp.arange(extent_downslope + 2 * border_extent, dtype=jnp.float32) - border_extent + 0.5) * cell_pitch
    centres_y = (jnp.arange(extent_spanwise + 2 * border_extent, dtype=jnp.float32) - border_extent + 0.5) * cell_pitch
    centres_z = (jnp.arange(extent_normal + 2 * border_extent, dtype=jnp.float32) - border_extent + 0.5) * cell_pitch
    grid = jnp.zeros((10, total_z + 2 * border_extent, total_x + 2 * border_extent, total_y + 2 * border_extent), jnp.float32)

    def add_brick(index, grid_now):
        pos_a, pos_b, pos_c = brick_place(index)
        wide = deposit(local[index, :3], loads[index], centres_x, centres_y, centres_z)
        wide = wide.reshape(10, extent_normal + 2 * border_extent, extent_downslope + 2 * border_extent, extent_spanwise + 2 * border_extent)
        corner = (jnp.zeros((), jnp.int32), (pos_c * extent_normal).astype(jnp.int32), (pos_a * extent_downslope).astype(jnp.int32), (pos_b * extent_spanwise).astype(jnp.int32))
        return lax.dynamic_update_slice(grid_now, lax.dynamic_slice(grid_now, corner, wide.shape) + wide, corner)
    grid = lax.fori_loop(0, bricks, add_brick, grid)
    inner = grid[:, border_extent:border_extent + total_z, border_extent:border_extent + total_x, border_extent:border_extent + total_y]
    fields = inner.reshape(10, N_GZ, extent_normal, N_GX, extent_downslope, N_GY, extent_spanwise).transpose(3, 5, 1, 0, 2, 4, 6)
    fields = fields.reshape(N_GX, N_GY, N_GZ, 10, extent_normal, extent_downslope * extent_spanwise)
    density = inner[0]
    velocity = inner[1] / (density + FLOOR_LEVEL)
    shear = inner[8]
    press = (inner[4] + inner[5] + inner[6]) / 3.0
    profile = jnp.stack([density, velocity, shear, press])
    profile = profile.reshape(4, total_z, N_GX, extent_downslope, N_GY, extent_spanwise).transpose(0, 2, 4, 1, 3, 5)
    profile = profile.reshape(4, N_GX, N_GY, total_z, extent_downslope * extent_spanwise)
    fitted, inertial = column_fit(profile)
    return (fields, fitted.transpose(1, 2, 0, 3), inertial)
```

```python
import math

import jax
import jax.numpy as jnp
from jax import lax
from jax.experimental import pallas as pl
from jax.experimental.pallas import tpu as pltpu
from jax.sharding import PartitionSpec as P

TILE = 128
BOXES_DOWNSLOPE = 8
BOXES_SPANWISE = 2
BOXES_NORMAL = 2
CELLS_PER_EDGE = 4

TILE_BOX_EDGE = 5.0
SPRING = 2.0
SOFTEN = 0.05
FLOOR_LEVEL = 0.1
RIDGE_SHARE = 0.1
CUT_LEVEL = math.exp(-12.5)
NORM_ONE = 1.0 / math.sqrt(2.0 * math.pi)

PITCH = TILE_BOX_EDGE / CELLS_PER_EDGE
REACH = 1.21
ABSENT = -10.0

NB = BOXES_DOWNSLOPE * BOXES_SPANWISE * BOXES_NORMAL
COLS = CELLS_PER_EDGE * BOXES_DOWNSLOPE * CELLS_PER_EDGE * BOXES_SPANWISE
CAPS = (16, 12, 16, 12, 14)

F32 = jnp.float32
BF16 = jnp.bfloat16


def iota(shape, dim):
    return lax.broadcasted_iota(jnp.int32, shape, dim)


def split3(value):
    high = value.astype(BF16)
    rest = value - high.astype(F32)
    mid = rest.astype(BF16)
    low = (rest - mid.astype(F32)).astype(BF16)
    return high, mid, low


def pick(value, onehot):
    high, mid, low = split3(value)
    dot = lambda part: jnp.dot(part, onehot, preferred_element_type=F32)
    return (dot(low) + dot(mid)) + dot(high)


def sort_kernel(place_ref, grains_ref, pairs_ref, out_ref):
    pairs = pairs_ref[...]
    live = pairs >= 0
    hood = jnp.where(live, pairs, 0) >> 5
    third = (hood * 11) >> 5
    part_c = hood - 3 * third
    part_b = third - 3 * ((third * 11) >> 5)

    def has(part, value):
        hit = jnp.where(live & (part == value), 1.0, 0.0)
        return jnp.max(hit, axis=1, keepdims=True) > 0.5

    last_b = place_ref[0] == 1
    last_c = place_ref[1] == 1
    box_y = has(part_b, 2) | (last_b & jnp.logical_not(has(part_b, 0)))
    box_z = has(part_c, 2) | (last_c & jnp.logical_not(has(part_c, 0)))
    rows = [grains_ref[r] for r in range(7)]
    centre = 0.5 * (jnp.min(rows[0], axis=1, keepdims=True) + jnp.max(rows[0], axis=1, keepdims=True))
    key = centre + jnp.where(box_y, 64.0, 0.0) + jnp.where(box_z, 128.0, 0.0)
    sub = iota((NB, TILE), 0)
    lane = iota((NB, TILE), 1)
    wide = jnp.broadcast_to(key, (NB, TILE))
    key_row = jnp.sum(jnp.where(sub == lane, wide, 0.0), axis=0, keepdims=True)
    before = (wide < key_row) | ((wide == key_row) & (sub < lane))
    rank = jnp.sum(jnp.where(before, 1.0, 0.0), axis=0, keepdims=True)
    onehot = jnp.where((rank == sub.astype(F32)) & (lane < NB), 1.0, 0.0).astype(BF16)[:, :NB]
    for r in range(7):
        high, mid, low = split3(rows[r])
        dot = lambda part: jnp.dot(onehot, part, preferred_element_type=F32)
        out_ref[r] = (dot(low) + dot(mid)) + dot(high)


def box_sort(grains, pairs, place):
    return pl.pallas_call(
        sort_kernel,
        out_shape=jax.ShapeDtypeStruct((7, NB, TILE), F32),
        in_specs=[
            pl.BlockSpec(memory_space=pltpu.SMEM),
            pl.BlockSpec(memory_space=pltpu.VMEM),
            pl.BlockSpec(memory_space=pltpu.VMEM),
        ],
        out_specs=pl.BlockSpec(memory_space=pltpu.VMEM),
        name="box_sort",
    )(place, grains, pairs)


def pack(lists, tri):
    rows = lists[0][1][0].shape[0]
    lane = iota((rows, TILE), 1)
    lane_f = lane.astype(F32)
    offset = jnp.zeros((rows, TILE), F32)
    outs = [jnp.zeros((rows, TILE), F32)] * 3 + [jnp.full((rows, TILE), ABSENT, F32)]
    for mask, arrays in lists:
        both = jnp.dot(jnp.where(mask, 1.0, 0.0).astype(BF16), tri, preferred_element_type=F32)
        ranks, total = both[:, :TILE], both[:, TILE:]
        wanted = lane_f - offset
        place = jnp.zeros((rows, TILE), jnp.int32)
        for bit in (64, 32, 16, 8, 4, 2, 1):
            probe = jnp.take_along_axis(ranks, place + (bit - 1), axis=1)
            place = jnp.where(probe <= wanted, place + bit, place)
        ours = (wanted >= 0.0) & (wanted < total)
        outs = [jnp.where(ours, jnp.take_along_axis(a, place, axis=1), o) for a, o in zip(arrays, outs)]
        offset = offset + total
    return outs, offset


def pair_terms(own, cand, sums):
    own_x, own_y, own_z, own_r = own
    cand_x, cand_y, cand_z, cand_r = cand
    dx, dy, dz = own_x - cand_x, own_y - cand_y, own_z - cand_z
    square = dx * dx + dy * dy + dz * dz
    distance = square * lax.rsqrt(jnp.maximum(square, 1e-30))
    overlap = jnp.maximum(own_r + cand_r - distance, 0.0)
    below = distance + SOFTEN
    guess = pl.reciprocal(below, approx=True)
    force = (0.5 * SPRING) * overlap * (guess * (2.0 - below * guess))
    fx, fy, fz = force * dx, force * dy, force * dz
    terms = (fx * dx, fy * dy, fz * dz, fx * dy, fx * dz, fy * dz)
    return tuple(s + t for s, t in zip(sums, terms))


def stress_kernel(grid_ref, side_ref, grains_ref, out_ref, cand_ref, all_ref, contact_ref, plane_ref, height_ref):
    tri_row = iota((TILE, 2 * TILE), 0)
    tri_col = iota((TILE, 2 * TILE), 1)
    tri = jnp.where((tri_row <= tri_col) | (tri_col >= TILE), 1.0, 0.0).astype(BF16)

    row = iota((16 * 8, TILE), 0)
    row_x = row & 7
    row_y = (row >> 3) & 3
    row_z = row >> 5
    span_y = BOXES_SPANWISE * TILE_BOX_EDGE
    span_z = BOXES_NORMAL * TILE_BOX_EDGE
    span_x = BOXES_DOWNSLOPE * TILE_BOX_EDGE
    shift_y = jnp.where(row_y == 0, -span_y, jnp.where(row_y == 3, span_y, 0.0))
    shift_z = jnp.where(row_z == 0, -span_z, jnp.where(row_z == 3, span_z, 0.0))
    radius = grid_ref[3]
    radius = jnp.where(radius == 0.0, ABSENT, radius)
    here = [grid_ref[0], grid_ref[1] + shift_y, grid_ref[2] + shift_z, radius]

    side = iota((16, TILE), 0)
    side_y = side & 3
    side_z = side >> 2
    side_shift_y = jnp.where(side_y == 0, -span_y, jnp.where(side_y == 3, span_y, 0.0))
    side_shift_z = jnp.where(side_z == 0, -span_z, jnp.where(side_z == 3, span_z, 0.0))
    sides = []
    for k, shift_x in ((0, -span_x), (1, span_x)):
        r = side_ref[k, 3]
        sides.append(
            [
                side_ref[k, 0] + shift_x,
                side_ref[k, 1] + side_shift_y,
                side_ref[k, 2] + side_shift_z,
                jnp.where(r == 0.0, ABSENT, r),
            ]
        )

    in_box_x = iota((16, 8, TILE), 1)

    def neighbours(centre, edge, step):
        cube = centre.reshape(16, 8, TILE)
        moved = pltpu.roll(cube, 1 if step < 0 else 7, 1)
        at_edge = in_box_x == (0 if step < 0 else 7)
        return jnp.where(at_edge, edge[:, None, :], moved).reshape(16 * 8, TILE)

    before = [neighbours(c, e, -1) for c, e in zip(here, sides[0])]
    after = [neighbours(c, e, 1) for c, e in zip(here, sides[1])]
    low_x = TILE_BOX_EDGE * row_x.astype(F32)
    beside_x, count_x = pack(
        [
            ((before[0] >= low_x - REACH) & (before[3] > 0.0), before),
            ((after[0] <= low_x + (TILE_BOX_EDGE + REACH)) & (after[3] > 0.0), after),
        ],
        tri,
    )
    worst = [jnp.max(count_x) - 8.0 * CAPS[1]]

    def cut_y(arrays, start):
        return [a.reshape(4, 4, 8, TILE)[:, start : start + 2].reshape(4 * 2 * 8, TILE) for a in arrays]

    low_y = TILE_BOX_EDGE * ((iota((64, TILE), 0) >> 3) & 1).astype(F32)

    def near_y(arrays, start):
        cut = cut_y(arrays, start)
        near = (cut[1] >= low_y - REACH) if start == 0 else (cut[1] <= low_y + (TILE_BOX_EDGE + REACH))
        return near & (cut[3] > 0.0), cut

    beside_y, count_y = pack(
        [near_y(here, 0), near_y(beside_x, 0), near_y(here, 2), near_y(beside_x, 2)], tri
    )
    worst.append(jnp.max(count_y) - 8.0 * CAPS[2])

    def cut_z(arrays, start):
        return [a[16 * start : 16 * start + 32] for a in arrays]

    low_z = TILE_BOX_EDGE * (iota((32, TILE), 0) >> 4).astype(F32)

    def near_z(arrays, start):
        cut = cut_z(arrays, start)
        near = (cut[2] >= low_z - REACH) if start == 0 else (cut[2] <= low_z + (TILE_BOX_EDGE + REACH))
        return near & (cut[3] > 0.0), cut

    mid_here, mid_x = cut_y(here, 1), cut_y(beside_x, 1)
    above, count_z = pack([near_z(mid_here, 0), near_z(mid_here, 2)], tri)
    worst.append(jnp.max(count_z) - 8.0 * CAPS[3])
    above_rest, count_w = pack(
        [near_z(mid_x, 0), near_z(beside_y, 0), near_z(mid_x, 2), near_z(beside_y, 2)], tri
    )
    worst.append(jnp.max(count_w) - 8.0 * CAPS[4])
    chunks = [cut_z(mid_here, 1), cut_z(mid_x, 1), cut_z(beside_y, 1), above, above_rest]
    for k, chunk in enumerate(chunks):
        for c in range(4):
            cand_ref[(4 * k + c) * NB : (4 * k + c + 1) * NB, :] = chunk[c]
    overflow = worst[0]
    for w in worst[1:]:
        overflow = jnp.maximum(overflow, w)

    def own_rows(t):
        return tuple(
            jnp.broadcast_to(cand_ref[pl.ds(c * NB + t, 1), :], (8, TILE)) for c in range(4)
        )

    def group(columns, first, g):
        return tuple(
            jnp.broadcast_to(columns[8 * g : 8 * g + 8, first + c : first + c + 1], (8, TILE)) for c in range(4)
        )

    def put(t, sums):
        for k in range(6):
            contact_ref[pl.ds(k * NB + t, 1), :] = jnp.sum(sums[k], axis=0, keepdims=True)

    zeros = tuple(jnp.zeros((8, TILE), F32) for _ in range(6))

    @pl.when(overflow <= 0.0)
    def _():
        def one_tile(t, carry):
            own = own_rows(t)
            columns = cand_ref[pl.ds(t, 24, stride=NB), :].T
            sums = zeros
            for k in range(5):
                for g in range(CAPS[k]):
                    sums = pair_terms(own, group(columns, 4 * k, g), sums)
            put(t, sums)
            return carry

        lax.fori_loop(0, NB, one_tile, 0)

    @pl.when(overflow > 0.0)
    def _():
        stride = 16 * 8 + 32
        for c in range(4):
            all_ref[c * stride : c * stride + 128, :] = here[c]
            all_ref[c * stride + 128 : c * stride + 144, :] = sides[0][c]
            all_ref[c * stride + 144 : c * stride + 160, :] = sides[1][c]
            all_ref[(c + 4) * stride : (c + 5) * stride, :] = jnp.zeros((stride, TILE), F32)

        def one_tile(t, carry):
            own = own_rows(t)
            tile_x, tile_y, tile_z = t & 7, (t >> 3) & 1, t >> 4

            def one_near(n, sums):
                n_x = n // 9
                n_y = (n - 9 * n_x) // 3
                n_z = n - 9 * n_x - 3 * n_y
                at_x = tile_x + n_x - 1
                plane = 4 * (tile_z + n_z) + tile_y + n_y
                place = jnp.where(
                    at_x < 0, 128 + plane, jnp.where(at_x > 7, 144 + plane, 8 * plane + at_x)
                )
                columns = all_ref[pl.ds(place, 8, stride=stride), :].T
                for g in range(16):
                    sums = pair_terms(own, group(columns, 0, g), sums)
                return sums

            put(t, lax.fori_loop(0, 27, one_near, zeros))
            return carry

        lax.fori_loop(0, NB, one_tile, 0)

    nx = CELLS_PER_EDGE * (BOXES_DOWNSLOPE + 2)
    ny = CELLS_PER_EDGE * (BOXES_SPANWISE + 2)
    nz = CELLS_PER_EDGE * (BOXES_NORMAL + 2)

    def weights(coords, centres):
        diff = coords - centres
        return jnp.maximum(jnp.exp(-0.5 * diff * diff) - CUT_LEVEL, 0.0) * NORM_ONE

    def centres(count):
        return (iota((count, TILE), 0).astype(F32) - CELLS_PER_EDGE + 0.5) * PITCH

    at_z = iota((8, TILE), 0)
    rim_z = jnp.where(at_z < 4, at_z, at_z + 8)
    centres_rim = (rim_z.astype(F32) - CELLS_PER_EDGE + 0.5) * PITCH

    def one_deposit(t, carry):
        rows = [grains_ref[pl.ds(r * NB + t, 1), :] for r in range(7)]
        wx = weights(rows[0], centres(nx))
        wy = weights(rows[1], centres(ny))
        wz = weights(rows[2], centres(nz))
        wz_rim = jnp.concatenate([wz[0:4], wz[12:16]], axis=0)
        wz_inner = wz[4:12]
        masses = 4.0 * math.pi / 3.0 * rows[3] * rows[3] * rows[3]
        vel = rows[4:7]
        cont = [contact_ref[pl.ds(k * NB + t, 1), :] for k in range(6)]
        loads = [masses, masses * vel[0], masses * vel[1], masses * vel[2]]
        for k, (i, j) in enumerate(((0, 0), (1, 1), (2, 2), (0, 1), (0, 2), (1, 2))):
            loads.append(cont[k] + masses * (vel[i] * vel[j]))
        height = [load * wz_inner for load in loads] + [load * wz_rim for load in loads]
        lanes = pl.ds(pl.multiple_of(t * TILE, TILE), TILE)
        height_ref[:, lanes] = jnp.concatenate(height, axis=0).astype(BF16)
        parts = [wx[x : x + 1] * wy for x in list(range(4)) + list(range(nx - 4, nx))]
        inner_x = wx[4 : nx - 4]
        parts += [inner_x * wy[y : y + 1] for y in list(range(4)) + list(range(ny - 4, ny))]
        inner_y = wy[4 : ny - 4]
        parts += [wx[x : x + 1] * inner_y for x in range(4, nx - 4)]
        plane_ref[:, lanes] = jnp.concatenate(parts, axis=0).astype(BF16)
        return carry

    lax.fori_loop(0, NB, one_deposit, 0)
    out_ref[...] = lax.dot_general(
        height_ref[...], plane_ref[...], (((1,), (1,)), ((), ())), preferred_element_type=F32
    )


def stress_and_deposit(grid, side, grains):
    vmem = pl.BlockSpec(memory_space=pltpu.VMEM)
    return pl.pallas_call(
        stress_kernel,
        out_shape=jax.ShapeDtypeStruct((160, 128 + 2 * 128 + COLS), F32),
        in_specs=[vmem, vmem, vmem],
        out_specs=vmem,
        scratch_shapes=[
            pltpu.VMEM((24 * NB, TILE), F32),
            pltpu.VMEM((8 * 160, TILE), F32),
            pltpu.VMEM((6 * NB, TILE), F32),
            pltpu.VMEM((128 + 2 * 128 + COLS, NB * TILE), BF16),
            pltpu.VMEM((160, NB * TILE), BF16),
        ],
        name="stress_deposit",
    )(grid, side, grains)


def rim_x_kernel(wide_ref, left_ref, right_ref, low_ref, high_ref, inner_ref):
    lane = iota((160, TILE), 1)
    got = jnp.where(lane < 64, right_ref[...], left_ref[...])
    src = iota((TILE, 1), 0)
    x = (src >> 4) & 3
    x = jnp.where(src >= 64, x, x + (CELLS_PER_EDGE * BOXES_DOWNSLOPE - 4))
    y = src & 15
    target = jnp.where(y < 4, y * 32 + x, jnp.where(y >= 12, 128 + (y - 12) * 32 + x, 256 + x * 8 + y - 4))
    onehot = jnp.where(iota((TILE, 512), 1) == target, 1.0, 0.0).astype(BF16)
    total = wide_ref[:, 128:] + pick(got, onehot)
    low_ref[...] = total[:, :128]
    high_ref[...] = total[:, 128:256]
    inner_ref[...] = total[:, 256:]


def rim_y_kernel(inner_ref, left_ref, right_ref, out_ref):
    got = jnp.concatenate([left_ref[...], right_ref[...]], axis=1)
    src = iota((256, 1), 0)
    target = (src & 31) * 8 + 4 * (src >> 7) + ((src >> 5) & 3)
    onehot = jnp.where(iota((256, 256), 1) == target, 1.0, 0.0).astype(BF16)
    out_ref[...] = inner_ref[...] + pick(got, onehot)


def plain_call(kernel, shapes, name, *args):
    vmem = pl.BlockSpec(memory_space=pltpu.VMEM)
    return pl.pallas_call(
        kernel,
        out_shape=shapes,
        in_specs=[vmem] * len(args),
        out_specs=jax.tree.map(lambda _: vmem, shapes),
        name=name,
    )(*args)


def column_fit(density, velocity, shear, press):
    upper = jnp.concatenate([velocity[1:, :], velocity[-1:, :]], axis=0)
    lower = jnp.concatenate([velocity[:1, :], velocity[:-1, :]], axis=0)
    rate = (upper - lower) / (2.0 * PITCH)
    inertial = rate * 1.0 / jnp.sqrt((press + FLOOR_LEVEL) / (density + FLOOR_LEVEL))
    friction = shear / (press + FLOOR_LEVEL)
    weight = density + FLOOR_LEVEL
    add = lambda v: jnp.sum(v, axis=0, keepdims=True)
    sum_zero = add(weight)
    sum_one = add(weight * inertial)
    sum_two = add(weight * inertial * inertial) + RIDGE_SHARE * sum_zero
    mix_zero = add(weight * friction)
    mix_one = add(weight * friction * inertial)
    determ = sum_zero * sum_two - sum_one * sum_one
    fitted = jnp.concatenate(
        [
            (mix_zero * sum_two - sum_one * mix_one) / determ,
            (sum_zero * mix_one - sum_one * mix_zero) / determ,
        ],
        axis=0,
    )
    return fitted, inertial


def exchange(low, high, axis):
    count = lax.axis_size(axis)
    if count == 1:
        return jnp.zeros_like(high), jnp.zeros_like(low)
    even = lax.axis_index(axis) % 2 == 0

    def swap(value, first):
        links = []
        for i in range(first, count - 1, 2):
            links += [(i, i + 1), (i + 1, i)]
        return lax.ppermute(value, axis, links)

    one = swap(jnp.where(even, high, low), 0)
    two = swap(jnp.where(even, low, high), 1) if count > 2 else jnp.zeros_like(low)
    return jnp.where(even, two, one), jnp.where(even, one, two)


def local(grains, pairs):
    place = jnp.stack(
        [lax.axis_index(a) == lax.axis_size(a) - 1 for a in ("gy", "gz")]
    ).astype(jnp.int32)
    own = box_sort(grains.reshape(7, NB, TILE), pairs.reshape(NB, 27), place)
    cube = own[:4].reshape(4, 2, 2, 8, TILE)
    below, above = exchange(cube[:, 0], cube[:, 1], "gz")
    cube = jnp.concatenate([below[:, None], cube, above[:, None]], axis=1)
    below, above = exchange(cube[:, :, 0], cube[:, :, 1], "gy")
    cube = jnp.concatenate([below[:, :, None], cube, above[:, :, None]], axis=2)
    below, above = exchange(cube[:, :, :, 0], cube[:, :, :, 7], "gx")
    side = jnp.stack([below, above]).reshape(2, 4, 16, TILE)
    wide = stress_and_deposit(cube.reshape(4, 128, TILE), side, own.reshape(7 * NB, TILE))
    left, right = exchange(wide[:, :128], wide[:, :128], "gx")
    block = jax.ShapeDtypeStruct((160, 128), F32)
    low, high, inner = plain_call(
        rim_x_kernel, [block, block, jax.ShapeDtypeStruct((160, COLS), F32)], "rim_x", wide, left, right
    )
    left, right = exchange(low, high, "gy")
    total = plain_call(
        rim_y_kernel, jax.ShapeDtypeStruct((160, COLS), F32), "rim_y", inner, left, right
    )
    fields = total[:80].reshape(10, 8, COLS)
    rim = total[80:].reshape(10, 8, COLS)
    from_below, from_above = exchange(rim[:, :4], rim[:, 4:], "gz")
    fields = fields + jnp.concatenate([from_below, from_above], axis=1)
    share = COLS // lax.axis_size("gz")
    start = lax.axis_index("gz") * share
    density = fields[0]
    velocity = fields[1] / (density + FLOOR_LEVEL)
    shear = fields[8]
    press = (fields[4] + fields[5] + fields[6]) / 3.0
    profile = jnp.stack([density, velocity, shear, press])
    whole = lax.all_gather(profile, "gz", axis=1, tiled=True)
    whole = lax.dynamic_slice_in_dim(whole, start, share, 2)
    fitted, inertial = column_fit(*whole)
    return (fields[None, None, None], fitted[None, None], inertial[None, None])


def solution(mesh):
    in_specs = (P("gx", "gy", "gz", None, None), P("gx", "gy", "gz", None, None))
    out_specs = (
        P("gx", "gy", "gz", None, None, None),
        P("gx", "gy", None, "gz"),
        P("gx", "gy", None, "gz"),
    )
    return jax.shard_map(local, mesh=mesh, in_specs=in_specs, out_specs=out_specs, check_vma=False)
```

```python
import math

import jax
import jax.numpy as jnp
from jax import lax
from jax.experimental import pallas as pl
from jax.experimental.pallas import tpu as pltpu
from jax.sharding import PartitionSpec as P

TILE = 128
BOXES_DOWNSLOPE = 8
BOXES_SPANWISE = 2
BOXES_NORMAL = 2
CELLS_PER_EDGE = 4

TILE_BOX_EDGE = 5.0
SPRING = 2.0
SOFTEN = 0.05
FLOOR_LEVEL = 0.1
RIDGE_SHARE = 0.1
CUT_LEVEL = math.exp(-12.5)
NORM_ONE = 1.0 / math.sqrt(2.0 * math.pi)

PITCH = TILE_BOX_EDGE / CELLS_PER_EDGE
REACH = 1.21
ABSENT = -10.0

NB = BOXES_DOWNSLOPE * BOXES_SPANWISE * BOXES_NORMAL
PITCH_ROWS = NB + 8
UNROLL = 4
COLS = CELLS_PER_EDGE * BOXES_DOWNSLOPE * CELLS_PER_EDGE * BOXES_SPANWISE
CAPS = (16, 12, 16, 12, 14)

F32 = jnp.float32
BF16 = jnp.bfloat16


def iota(shape, dim):
    return lax.broadcasted_iota(jnp.int32, shape, dim)


def split3(value):
    high = value.astype(BF16)
    rest = value - high.astype(F32)
    mid = rest.astype(BF16)
    low = (rest - mid.astype(F32)).astype(BF16)
    return high, mid, low


def pick(value, onehot):
    high, mid, low = split3(value)
    dot = lambda part: jnp.dot(part, onehot, preferred_element_type=F32)
    return (dot(low) + dot(mid)) + dot(high)


def is_last(axis):
    return lax.axis_index(axis) == lax.axis_size(axis) - 1


def is_even(axis):
    return lax.axis_index(axis) % 2 == 0


def sort_kernel(grains_ref, pairs_ref, own_ref, near_ref):
    pairs = pairs_ref[0, 0, 0]
    live = pairs >= 0
    hood = jnp.where(live, pairs, 0) >> 5
    third = (hood * 11) >> 5
    part_c = hood - 3 * third
    part_b = third - 3 * ((third * 11) >> 5)

    def has(part, value):
        hit = jnp.where(live & (part == value), 1.0, 0.0)
        return jnp.max(hit, axis=1, keepdims=True) > 0.5

    box_y = has(part_b, 2) | (is_last("gy") & jnp.logical_not(has(part_b, 0)))
    box_z = has(part_c, 2) | (is_last("gz") & jnp.logical_not(has(part_c, 0)))
    grains = grains_ref[0, 0, 0].reshape(7, NB, TILE)
    rows = [grains[r] for r in range(7)]
    centre = 0.5 * (jnp.min(rows[0], axis=1, keepdims=True) + jnp.max(rows[0], axis=1, keepdims=True))
    key = centre + jnp.where(box_y, 64.0, 0.0) + jnp.where(box_z, 128.0, 0.0)
    sub = iota((NB, TILE), 0)
    lane = iota((NB, TILE), 1)
    wide = jnp.broadcast_to(key, (NB, TILE))
    key_row = jnp.sum(jnp.where(sub == lane, wide, 0.0), axis=0, keepdims=True)
    before = (wide < key_row) | ((wide == key_row) & (sub < lane))
    rank = jnp.sum(jnp.where(before, 1.0, 0.0), axis=0, keepdims=True)
    onehot = jnp.where((rank == sub.astype(F32)) & (lane < NB), 1.0, 0.0).astype(BF16)[:, :NB]
    for r in range(7):
        high, mid, low = split3(rows[r])
        dot = lambda part: jnp.dot(onehot, part, preferred_element_type=F32)
        value = (dot(low) + dot(mid)) + dot(high)
        own_ref[r] = value
        if r < 4:
            near_ref[r] = value


def box_sort(grains, pairs):
    shape = lambda rows: jax.ShapeDtypeStruct((rows, NB, TILE), F32)
    return plain_call(sort_kernel, [shape(7), shape(4)], "box_sort", grains, pairs)


def lane_take(value, index):
    dims = lax.GatherDimensionNumbers(
        offset_dims=(),
        collapsed_slice_dims=(1,),
        start_index_map=(1,),
        operand_batching_dims=(0,),
        start_indices_batching_dims=(0,),
    )
    return lax.gather(
        value, index[..., None], dims, (1, 1), mode=lax.GatherScatterMode.PROMISE_IN_BOUNDS
    )


def pack(groups, tri):
    masks = [jnp.where(mask, 1.0, 0.0).astype(BF16) for lists in groups for mask, _ in lists]
    both = jnp.dot(jnp.concatenate(masks, axis=0), tri, preferred_element_type=F32)
    rows = masks[0].shape[0]
    lane_f = iota((rows, TILE), 1).astype(F32)
    packed, at = [], 0
    for lists in groups:
        offset = jnp.zeros((rows, TILE), F32)
        outs = [jnp.zeros((rows, TILE), F32)] * 3 + [jnp.full((rows, TILE), ABSENT, F32)]
        for _, arrays in lists:
            ranks, total = both[at : at + rows, :TILE], both[at : at + rows, TILE:]
            at += rows
            wanted = lane_f - offset
            place = jnp.zeros((rows, TILE), jnp.int32)
            for bit in (64, 32, 16, 8, 4, 2, 1):
                probe = lane_take(ranks, place + (bit - 1))
                place = jnp.where(probe <= wanted, place + bit, place)
            ours = (wanted >= 0.0) & (wanted < total)
            outs = [jnp.where(ours, lane_take(a, place), o) for a, o in zip(arrays, outs)]
            offset = offset + total
        packed.append((outs, offset))
    return packed


def pair_terms(own, cand, sums):
    own_x, own_y, own_z, own_r = own
    cand_x, cand_y, cand_z, cand_r = cand
    dx, dy, dz = own_x - cand_x, own_y - cand_y, own_z - cand_z
    square = dx * dx + dy * dy + dz * dz
    distance = square * lax.rsqrt(jnp.maximum(square, 1e-30))
    overlap = jnp.maximum(own_r + cand_r - distance, 0.0)
    below = distance + SOFTEN
    guess = pl.reciprocal(below, approx=True)
    force = (0.5 * SPRING) * overlap * (guess * (2.0 - below * guess))
    fx, fy, fz = force * dx, force * dy, force * dz
    terms = (fx * dx, fy * dy, fz * dz, fx * dy, fx * dz, fy * dz)
    return tuple(s + t for s, t in zip(sums, terms))


def stress_kernel(grid_ref, side_ref, grains_ref, rim0_ref, rim1_ref, out_ref, cand_ref, all_ref, contact_ref, plane_ref, height_ref,
    feature_ref, moment_ref, own_ref, sum_ref,
):
    tri_row = iota((TILE, 2 * TILE), 0)
    tri_col = iota((TILE, 2 * TILE), 1)
    tri = jnp.where((tri_row <= tri_col) | (tri_col >= TILE), 1.0, 0.0).astype(BF16)

    span_x = BOXES_DOWNSLOPE * TILE_BOX_EDGE
    span_y = BOXES_SPANWISE * TILE_BOX_EDGE
    span_z = BOXES_NORMAL * TILE_BOX_EDGE

    def shifts(place, span):
        return jnp.where(place == 0, -span, jnp.where(place == 3, span, 0.0))

    def alive(radius):
        return jnp.where(radius == 0.0, ABSENT, radius)

    row = iota((128, TILE), 0)
    low_x = TILE_BOX_EDGE * (row & 7).astype(F32)
    low_y = TILE_BOX_EDGE * ((iota((64, TILE), 0) >> 3) & 1).astype(F32)
    low_z = TILE_BOX_EDGE * (iota((32, TILE), 0) >> 4).astype(F32)
    here = [
        grid_ref[0],
        grid_ref[1] + shifts((row >> 3) & 3, span_y),
        grid_ref[2] + shifts(row >> 5, span_z),
        alive(grid_ref[3]),
    ]
    side_row = iota((16, TILE), 0)
    sides = []
    for k, shift_x in ((0, -span_x), (1, span_x)):
        sides.append(
            [
                side_ref[k, 0] + shift_x,
                side_ref[k, 1] + shifts(side_row & 3, span_y),
                side_ref[k, 2] + shifts(side_row >> 2, span_z),
                alive(side_ref[k, 3]),
            ]
        )
    in_box_x = iota((16, 8, TILE), 1)

    def neighbours(centre, edge, step):
        cube = centre.reshape(16, 8, TILE)
        moved = pltpu.roll(cube, 1 if step < 0 else 7, 1)
        at_edge = in_box_x == (0 if step < 0 else 7)
        return jnp.where(at_edge, edge[:, None, :], moved).reshape(128, TILE)

    def near(arrays, axis, low, step):
        limit = arrays[axis] >= low - REACH if step < 0 else arrays[axis] <= low + (TILE_BOX_EDGE + REACH)
        return limit & (arrays[3] > 0.0), arrays

    def cut_y(arrays, start):
        return [a.reshape(4, 4, 8, TILE)[:, start : start + 2].reshape(64, TILE) for a in arrays]

    def cut_z(arrays, start):
        return [a[16 * start : 16 * start + 32] for a in arrays]

    before = [neighbours(c, e, -1) for c, e in zip(here, sides[0])]
    after = [neighbours(c, e, 1) for c, e in zip(here, sides[1])]
    ((beside_x, count_x),) = pack([[near(before, 0, low_x, -1), near(after, 0, low_x, 1)]], tri)
    ((beside_y, count_y),) = pack(
        [
            [
                near(cut_y(here, 0), 1, low_y, -1),
                near(cut_y(beside_x, 0), 1, low_y, -1),
                near(cut_y(here, 2), 1, low_y, 1),
                near(cut_y(beside_x, 2), 1, low_y, 1),
            ]
        ],
        tri,
    )
    mid, mid_x = cut_y(here, 1), cut_y(beside_x, 1)
    (above, count_z), (above_rest, count_w) = pack(
        [
            [near(cut_z(mid, 0), 2, low_z, -1), near(cut_z(mid, 2), 2, low_z, 1)],
            [
                near(cut_z(mid_x, 0), 2, low_z, -1),
                near(cut_z(beside_y, 0), 2, low_z, -1),
                near(cut_z(mid_x, 2), 2, low_z, 1),
                near(cut_z(beside_y, 2), 2, low_z, 1),
            ],
        ],
        tri,
    )
    worst = [
        jnp.max(count, axis=0, keepdims=True) - 8.0 * cap
        for count, cap in zip((count_x, count_y, count_z, count_w), CAPS[1:])
    ]

    def keep(ref, first, values):
        for f, value in enumerate(values):
            at = (first + f) * PITCH_ROWS
            ref[at : at + NB, :] = value

    half_box = 0.5 * TILE_BOX_EDGE
    ones = jnp.ones((NB, TILE), F32)
    none = jnp.zeros((NB, TILE), F32)

    def parts(value):
        return [p.astype(F32) for p in split3(value)]

    middle = [
        TILE_BOX_EDGE * (iota((NB, TILE), 0) & 7).astype(F32) + half_box,
        TILE_BOX_EDGE * ((iota((NB, TILE), 0) >> 3) & 1).astype(F32) + half_box,
        low_z + half_box,
    ]
    for k, chunk in enumerate((cut_z(mid, 1), cut_z(mid_x, 1), cut_z(beside_y, 1), above, above_rest)):
        x, y, z = (chunk[c] - middle[c] for c in range(3))
        squares = [x * x, y * y, z * z]
        norm = squares[0] + squares[1] + squares[2]
        xs, ys, zs, ns, rs = (parts(v) for v in (x, y, z, norm, chunk[3]))
        keep(
            feature_ref, 16 * k,
            [xs[0], ys[0], zs[0], xs[1], ys[1], zs[1], ones, ns[0]]
            + [xs[2], ys[2], zs[2], ns[1], ns[2]] + rs,
        )
        products = squares + [x * y, x * z, y * z]
        highs = [v.astype(BF16).astype(F32) for v in products]
        lows = [v - h for v, h in zip(products, highs)]
        keep(moment_ref, 16 * k, highs + [none] * 2 + lows + [none] * 2)
        if k == 0:
            for c in range(4):
                cand_ref[c * NB : c * NB + NB, :] = chunk[c]
            xi, yi, zi = ([-2.0 * p for p in v] for v in (xs, ys, zs))
            keep(
                own_ref, 0,
                [xi[0], yi[0], zi[0], xi[0], yi[0], zi[0], ns[0], ones]
                + [xi[0], yi[0], zi[0], ones, ones] + [none] * 3
                + [xi[1], yi[1], zi[1], xi[1], yi[1], zi[1], ns[1], none]
                + [xi[2], yi[2], zi[2], none, none, none, ns[2], none]
                + rs + [x, y, z],
            )
    overflow = worst[0]
    for w in worst[1:]:
        overflow = jnp.maximum(overflow, w)
    overflow = jnp.max(overflow)

    nx = CELLS_PER_EDGE * (BOXES_DOWNSLOPE + 2)
    ny = CELLS_PER_EDGE * (BOXES_SPANWISE + 2)

    def weights(coords, centres):
        diff = coords - centres
        return jnp.maximum(jnp.exp(-0.5 * diff * diff) - CUT_LEVEL, 0.0) * NORM_ONE

    def centres(places):
        return (places.astype(F32) - CELLS_PER_EDGE + 0.5) * PITCH

    at_z = iota((8, TILE), 0)
    centres_inner = centres(at_z + 4)
    centres_rim = centres(jnp.where(at_z < 4, at_z, at_z + 8))

    def put_plane(t):
        wx = weights(grains_ref[pl.ds(t, 1), :], centres(iota((nx, TILE), 0)))
        wy = weights(grains_ref[pl.ds(NB + t, 1), :], centres(iota((ny, TILE), 0)))
        parts = [wx[x : x + 1] * wy for x in list(range(4)) + list(range(nx - 4, nx))]
        inner_x = wx[4 : nx - 4]
        parts += [inner_x * wy[y : y + 1] for y in list(range(4)) + list(range(ny - 4, ny))]
        inner_y = wy[4 : ny - 4]
        parts += [wx[x : x + 1] * inner_y for x in range(4, nx - 4)]
        lanes = pl.ds(pl.multiple_of(t * TILE, TILE), TILE)
        plane_ref[:, lanes] = jnp.concatenate(parts, axis=0).astype(BF16)

    def put_height(t):
        rows = [grains_ref[pl.ds(r * NB + t, 1), :] for r in range(2, 7)]
        wz_inner = weights(rows[0], centres_inner)
        wz_rim = weights(rows[0], centres_rim)
        masses = 4.0 * math.pi / 3.0 * rows[1] * rows[1] * rows[1]
        vel = rows[2:]
        cont = [contact_ref[pl.ds(k * NB + t, 1), :] for k in range(6)]
        loads = [masses, masses * vel[0], masses * vel[1], masses * vel[2]]
        for k, (i, j) in enumerate(((0, 0), (1, 1), (2, 2), (0, 1), (0, 2), (1, 2))):
            loads.append(cont[k] + masses * (vel[i] * vel[j]))
        height = [load * wz_inner for load in loads] + [load * wz_rim for load in loads]
        lanes = pl.ds(pl.multiple_of(t * TILE, TILE), TILE)
        height_ref[:, lanes] = jnp.concatenate(height, axis=0).astype(BF16)

    def own_rows(t):
        return tuple(
            jnp.broadcast_to(cand_ref[pl.ds(c * NB + t, 1), :], (8, TILE)) for c in range(4)
        )

    def group(columns, first, g):
        return tuple(
            jnp.broadcast_to(columns[8 * g : 8 * g + 8, first + c : first + c + 1], (8, TILE)) for c in range(4)
        )

    def put(t, sums):
        for k in range(6):
            contact_ref[pl.ds(k * NB + t, 1), :] = jnp.sum(sums[k], axis=0, keepdims=True)

    zeros = tuple(jnp.zeros((8, TILE), F32) for _ in range(6))

    @pl.when(overflow <= 0.0)
    def _():
        sub = iota((8, TILE), 0)

        def one_tile(t, carry):
            put_plane(t)
            radii = [own_ref[pl.ds((32 + p) * PITCH_ROWS + t, 1), :] for p in range(3)]
            radii = [jnp.where(sub == 6, jnp.broadcast_to(r, (8, TILE)), 0.0) for r in radii]
            reach = [radii[0], jnp.where(sub >= 5, 1.0, 0.0), radii[1], radii[2]]
            rhs = jnp.concatenate(
                [own_ref[pl.ds(t, 32, stride=PITCH_ROWS), :], jnp.concatenate(reach, axis=0)], axis=1
            ).astype(BF16)
            highs, lows, moments = [], [], []
            for k in range(5):
                rows = feature_ref[pl.ds(16 * k * PITCH_ROWS + t, 16, stride=PITCH_ROWS), :]
                first = rows[:8]
                lhs = jnp.concatenate([rows, first, first], axis=0).T.astype(BF16)
                both = jnp.dot(lhs[: 8 * CAPS[k]], rhs, preferred_element_type=F32)
                square = jnp.maximum(both[:, :TILE], 1e-12)
                distance = square * lax.rsqrt(square)
                overlap = jnp.maximum(both[:, TILE:] - distance, 0.0)
                below = distance + SOFTEN
                guess = pl.reciprocal(below, approx=True)
                force = overlap * (guess * (2.0 - below * guess))
                if k == 0:
                    at = iota((TILE, TILE), 0) == iota((TILE, TILE), 1)
                    force = jnp.where(at, 0.0, force)
                high = force.astype(BF16)
                low = (force - high.astype(F32)).astype(BF16)
                rest = TILE - 8 * CAPS[k]
                highs.append(high)
                lows.append(low)
                if rest:
                    highs.append(jnp.zeros((rest, TILE), BF16))
                    lows.append(jnp.zeros((rest, TILE), BF16))
                more = moment_ref[pl.ds(16 * k * PITCH_ROWS + t, 16, stride=PITCH_ROWS), :]
                moments.append(jnp.concatenate([first, more, first], axis=0))
            lhs = jnp.concatenate(moments, axis=1).astype(BF16)
            one = jnp.dot(lhs, jnp.concatenate(highs, axis=0), preferred_element_type=F32)
            two = jnp.dot(lhs[:16], jnp.concatenate(lows, axis=0), preferred_element_type=F32)
            sum_ref[pl.ds(t, 8, stride=PITCH_ROWS), :] = one[:8] + two[:8]
            sum_ref[pl.ds(8 * PITCH_ROWS + t, 8, stride=PITCH_ROWS), :] = one[8:16] + (one[16:24] + two[8:])
            return carry

        def some_tiles(q, carry):
            for i in range(UNROLL):
                one_tile(UNROLL * q + i, carry)
            return carry

        lax.fori_loop(0, NB // UNROLL, some_tiles, 0)
        total = [sum_ref[m * PITCH_ROWS : m * PITCH_ROWS + NB, :] for m in range(14)]
        first = [total[c] + total[3 + c] for c in range(3)]
        own_mid = [own_ref[(35 + c) * PITCH_ROWS : (35 + c) * PITCH_ROWS + NB, :] for c in range(3)]
        for k, (i, j) in enumerate(((0, 0), (1, 1), (2, 2), (0, 1), (0, 2), (1, 2))):
            a, b = own_mid[i], own_mid[j]
            contact_ref[k * NB : (k + 1) * NB, :] = (0.5 * SPRING) * (
                total[8 + k] - (a * first[j] + b * first[i]) + a * b * total[6]
            )

    @pl.when(overflow > 0.0)
    def _():
        stride = 16 * 8 + 32
        for c in range(4):
            all_ref[c * stride : c * stride + 128, :] = here[c]
            all_ref[c * stride + 128 : c * stride + 144, :] = sides[0][c]
            all_ref[c * stride + 144 : c * stride + 160, :] = sides[1][c]
        all_ref[4 * stride : 8 * stride, :] = jnp.zeros((4 * stride, TILE), F32)

        def one_tile(t, carry):
            own = own_rows(t)
            tile_x, tile_y, tile_z = t & 7, (t >> 3) & 1, t >> 4

            def one_near(n, sums):
                n_x = n // 9
                n_y = (n - 9 * n_x) // 3
                n_z = n - 9 * n_x - 3 * n_y
                at_x = tile_x + n_x - 1
                plane = 4 * (tile_z + n_z) + tile_y + n_y
                place = jnp.where(
                    at_x < 0, 128 + plane, jnp.where(at_x > 7, 144 + plane, 8 * plane + at_x)
                )
                columns = all_ref[pl.ds(place, 8, stride=stride), :].T
                for g in range(16):
                    sums = pair_terms(own, group(columns, 0, g), sums)
                return sums

            put(t, lax.fori_loop(0, 27, one_near, zeros))
            put_plane(t)
            return carry

        lax.fori_loop(0, NB, one_tile, 0)

    def four_heights(q, carry):
        for i in range(4):
            put_height(4 * q + i)
        return carry

    lax.fori_loop(0, NB // 4, four_heights, 0)
    wide = lax.dot_general(
        height_ref[...], plane_ref[...], (((1,), (1,)), ((), ())), preferred_element_type=F32
    )
    out_ref[...] = wide[:, TILE:]
    rim = wide[:, :TILE]
    rim = jnp.where(is_even("gx"), pltpu.roll(rim, 64, 1), rim)
    upper, lower = rim[:80], rim[80:]
    left_half = iota((80, TILE), 1) < 64
    rim0_ref[...] = jnp.where(left_half, upper, pltpu.roll(lower, 64, 1))
    rim1_ref[...] = jnp.where(left_half, pltpu.roll(upper, 64, 1), lower)


def stress_and_deposit(grid, side, grains):
    vmem = pl.BlockSpec(memory_space=pltpu.VMEM)
    return pl.pallas_call(
        stress_kernel,
        out_shape=[
            jax.ShapeDtypeStruct((80, TILE), F32),
            jax.ShapeDtypeStruct((80, TILE), F32),
            jax.ShapeDtypeStruct((160, 2 * TILE + COLS), F32),
        ],
        in_specs=[vmem, vmem, vmem],
        out_specs=[vmem, vmem, vmem],
        scratch_shapes=[
            pltpu.VMEM((4 * NB, TILE), F32),
            pltpu.VMEM((8 * 160, TILE), F32),
            pltpu.VMEM((6 * NB, TILE), F32),
            pltpu.VMEM((128 + 2 * 128 + COLS, NB * TILE), BF16),
            pltpu.VMEM((160, NB * TILE), BF16),
            pltpu.VMEM((5 * 16 * PITCH_ROWS, TILE), F32),
            pltpu.VMEM((5 * 16 * PITCH_ROWS, TILE), F32),
            pltpu.VMEM((38 * PITCH_ROWS, TILE), F32),
            pltpu.VMEM((16 * PITCH_ROWS, TILE), F32),
        ],
        name="stress_deposit",
    )(grid, side, grains)


def rim_x_kernel(wide_ref, first_ref, second_ref, rim0_ref, rim1_ref, inner_ref):
    even = is_even("gx")
    right = jnp.where(even, first_ref[...], second_ref[...])
    left = jnp.where(even, second_ref[...], first_ref[...])
    left_half = iota((80, TILE), 1) < 64
    got = jnp.concatenate(
        [
            jnp.where(left_half, right, pltpu.roll(left, 64, 1)),
            jnp.where(left_half, pltpu.roll(right, 64, 1), left),
        ],
        axis=0,
    )
    src = iota((TILE, 1), 0)
    x = (src >> 4) & 3
    x = jnp.where(src >= 64, x, x + (CELLS_PER_EDGE * BOXES_DOWNSLOPE - 4))
    y = src & 15
    target = jnp.where(y < 4, y * 32 + x, jnp.where(y >= 12, 128 + (y - 12) * 32 + x, 256 + x * 8 + y - 4))
    onehot = jnp.where(iota((TILE, 512), 1) == target, 1.0, 0.0).astype(BF16)
    total = wide_ref[...] + pick(got, onehot)
    low, high = total[:, :TILE], total[:, TILE : 2 * TILE]
    even = is_even("gy")
    rim0_ref[...] = jnp.where(even, high, low)
    rim1_ref[...] = jnp.where(even, low, high)
    inner_ref[...] = total[:, 2 * TILE :]


def add_rim_y(inner_ref, first_ref, second_ref):
    even = is_even("gy")
    right = jnp.where(even, first_ref[...], second_ref[...])
    left = jnp.where(even, second_ref[...], first_ref[...])
    got = jnp.concatenate([left, right], axis=1)
    src = iota((256, 1), 0)
    target = (src & 31) * 8 + 4 * (src >> 7) + ((src >> 5) & 3)
    onehot = jnp.where(iota((256, 256), 1) == target, 1.0, 0.0).astype(BF16)
    return inner_ref[...] + pick(got, onehot)


def rim_y_kernel(inner_ref, first_ref, second_ref, out_ref):
    out_ref[...] = add_rim_y(inner_ref, first_ref, second_ref)


PROFILED = (0, 1, 4, 5, 6, 8)


def rim_y_two_kernel(inner_ref, first_ref, second_ref, out_ref, send_ref):
    total = add_rim_y(inner_ref, first_ref, second_ref)
    out_ref[...] = total
    lower = lax.axis_index("gz") == 0
    top = iota((8, COLS), 0) < 4
    for p in range(5):
        one = total[80 + 16 * p : 88 + 16 * p]
        two = total[88 + 16 * p : 96 + 16 * p]
        to_upper = jnp.where(top, pltpu.roll(one, 4, 0), two)
        to_lower = jnp.where(top, one, pltpu.roll(two, 4, 0))
        both = jnp.where(lower, to_upper, to_lower)
        send_ref[8 * p : 8 * p + 8, :] = both[:, :TILE]
        send_ref[40 + 8 * p : 48 + 8 * p, :] = both[:, TILE:]
    for i, c in enumerate(PROFILED):
        rows = total[8 * c : 8 * c + 8]
        send_ref[80 + 8 * i : 88 + 8 * i, :] = jnp.where(lower, rows[:, TILE:], rows[:, :TILE])


def finish_two_kernel(total_ref, got_ref, fields_ref, fits_ref, inertial_ref):
    lower = lax.axis_index("gz") == 0
    row = iota((8, COLS), 0)
    from_rim = jnp.where(lower, 7 - row, row)
    ours = from_rim < 4
    theirs = from_rim[:, :TILE] >= 4
    fields = []
    for p in range(5):
        got = jnp.concatenate(
            [got_ref[8 * p : 8 * p + 8, :], got_ref[40 + 8 * p : 48 + 8 * p, :]], axis=1
        )
        turned = pltpu.roll(got, 4, 0)
        for i, add in enumerate(
            (jnp.where(lower, turned, got), jnp.where(lower, got, turned))
        ):
            c = 2 * p + i
            fields.append(total_ref[8 * c : 8 * c + 8, :] + jnp.where(ours, add, 0.0))
            fields_ref[0, 0, 0, c] = fields[c]
    column = {}
    for i, c in enumerate(PROFILED):
        mine = jnp.where(lower, fields[c][:, :TILE], fields[c][:, TILE:])
        rim = total_ref[80 + 8 * c : 88 + 8 * c, :]
        rim = pltpu.roll(jnp.where(lower, rim[:, :TILE], rim[:, TILE:]), 4, 0)
        other = got_ref[80 + 8 * i : 88 + 8 * i, :] + jnp.where(theirs, rim, 0.0)
        column[c] = jnp.concatenate(
            [jnp.where(lower, mine, other), jnp.where(lower, other, mine)], axis=0
        )
    density = column[0]
    velocity = column[1] / (density + FLOOR_LEVEL)
    press = (column[4] + column[5] + column[6]) / 3.0
    fitted, inertial = column_fit(density, velocity, column[8], press)
    fits_ref[0, 0] = fitted
    inertial_ref[0, 0] = inertial


def plain_call(kernel, shapes, name, *args):
    vmem = pl.BlockSpec(memory_space=pltpu.VMEM)
    return pl.pallas_call(
        kernel,
        out_shape=shapes,
        in_specs=[vmem] * len(args),
        out_specs=jax.tree.map(lambda _: vmem, shapes),
        name=name,
    )(*args)


def column_fit(density, velocity, shear, press):
    upper = jnp.concatenate([velocity[1:, :], velocity[-1:, :]], axis=0)
    lower = jnp.concatenate([velocity[:1, :], velocity[:-1, :]], axis=0)
    rate = (upper - lower) / (2.0 * PITCH)
    inertial = rate * 1.0 / jnp.sqrt((press + FLOOR_LEVEL) / (density + FLOOR_LEVEL))
    friction = shear / (press + FLOOR_LEVEL)
    weight = density + FLOOR_LEVEL
    add = lambda v: jnp.sum(v, axis=0, keepdims=True)
    sum_zero = add(weight)
    sum_one = add(weight * inertial)
    sum_two = add(weight * inertial * inertial) + RIDGE_SHARE * sum_zero
    mix_zero = add(weight * friction)
    mix_one = add(weight * friction * inertial)
    determ = sum_zero * sum_two - sum_one * sum_one
    fitted = jnp.concatenate(
        [
            (mix_zero * sum_two - sum_one * mix_one) / determ,
            (sum_zero * mix_one - sum_one * mix_zero) / determ,
        ],
        axis=0,
    )
    return fitted, inertial


def swaps(first, second, axis):
    count = lax.axis_size(axis)
    got = []
    for start, value in ((0, first), (1, second)):
        links = []
        for i in range(start, count - 1, 2):
            links += [(i, i + 1), (i + 1, i)]
        got.append(lax.ppermute(value, axis, links) if links else jnp.zeros_like(value))
    return got


def exchange(low, high, axis):
    even = is_even(axis)
    one, two = swaps(jnp.where(even, high, low), jnp.where(even, low, high), axis)
    return jnp.where(even, two, one), jnp.where(even, one, two)


def local(grains, pairs):
    own, near = box_sort(grains, pairs)
    cube = near.reshape(4, 2, 2, 8, TILE)
    below, above = exchange(cube[:, 0], cube[:, 1], "gz")
    cube = jnp.concatenate([below[:, None], cube, above[:, None]], axis=1)
    below, above = exchange(cube[:, :, 0], cube[:, :, 1], "gy")
    cube = jnp.concatenate([below[:, :, None], cube, above[:, :, None]], axis=2)
    below, above = exchange(cube[:, :, :, 0], cube[:, :, :, 7], "gx")
    side = jnp.stack([below, above]).reshape(2, 4, 16, TILE)
    rim0, rim1, wide = stress_and_deposit(cube.reshape(4, 128, TILE), side, own.reshape(7 * NB, TILE))
    first, second = swaps(rim0, rim1, "gx")
    block = jax.ShapeDtypeStruct((160, TILE), F32)
    square = jax.ShapeDtypeStruct((160, COLS), F32)
    rim0, rim1, inner = plain_call(rim_x_kernel, [block, block, square], "rim_x", wide, first, second)
    first, second = swaps(rim0, rim1, "gy")
    if lax.axis_size("gz") == 2:
        sends = jax.ShapeDtypeStruct((128, TILE), F32)
        total, send = plain_call(rim_y_two_kernel, [square, sends], "rim_y", inner, first, second)
        got, _ = swaps(send, send, "gz")
        outs = [(1, 1, 1, 10, 8, COLS), (1, 1, 2, TILE), (1, 1, 16, TILE)]
        outs = [jax.ShapeDtypeStruct(shape, F32) for shape in outs]
        return tuple(plain_call(finish_two_kernel, outs, "finish", total, got))
    total = plain_call(rim_y_kernel, square, "rim_y", inner, first, second)
    fields = total[:80].reshape(10, 8, COLS)
    rim = total[80:].reshape(10, 8, COLS)
    from_below, from_above = exchange(rim[:, :4], rim[:, 4:], "gz")
    fields = fields + jnp.concatenate([from_below, from_above], axis=1)
    share = COLS // lax.axis_size("gz")
    start = lax.axis_index("gz") * share
    density = fields[0]
    velocity = fields[1] / (density + FLOOR_LEVEL)
    shear = fields[8]
    press = (fields[4] + fields[5] + fields[6]) / 3.0
    profile = jnp.stack([density, velocity, shear, press])
    whole = lax.all_gather(profile, "gz", axis=1, tiled=True)
    whole = lax.dynamic_slice_in_dim(whole, start, share, 2)
    fitted, inertial = column_fit(*whole)
    return (fields[None, None, None], fitted[None, None], inertial[None, None])


def solution(mesh):
    in_specs = (P("gx", "gy", "gz", None, None), P("gx", "gy", "gz", None, None))
    out_specs = (
        P("gx", "gy", "gz", None, None, None),
        P("gx", "gy", None, "gz"),
        P("gx", "gy", None, "gz"),
    )
    return jax.shard_map(local, mesh=mesh, in_specs=in_specs, out_specs=out_specs, check_vma=False)
```

```python
import math

import jax
import jax.numpy as jnp
from jax import lax
from jax.experimental import pallas as pl
from jax.experimental.pallas import tpu as pltpu
from jax.sharding import PartitionSpec as P

TILE = 128
BOXES_DOWNSLOPE = 8
BOXES_SPANWISE = 2
BOXES_NORMAL = 2
CELLS_PER_EDGE = 4

TILE_BOX_EDGE = 5.0
SPRING = 2.0
SOFTEN = 0.05
FLOOR_LEVEL = 0.1
RIDGE_SHARE = 0.1
CUT_LEVEL = math.exp(-12.5)
NORM_ONE = 1.0 / math.sqrt(2.0 * math.pi)

PITCH = TILE_BOX_EDGE / CELLS_PER_EDGE
REACH = 1.21
ABSENT = -10.0

NB = BOXES_DOWNSLOPE * BOXES_SPANWISE * BOXES_NORMAL
PITCH_ROWS = NB + 8
UNROLL = 4
COLS = CELLS_PER_EDGE * BOXES_DOWNSLOPE * CELLS_PER_EDGE * BOXES_SPANWISE
CAPS = (16, 12, 16, 12, 14)

F32 = jnp.float32
BF16 = jnp.bfloat16


def iota(shape, dim):
    return lax.broadcasted_iota(jnp.int32, shape, dim)


def split3(value):
    high = value.astype(BF16)
    rest = value - high.astype(F32)
    mid = rest.astype(BF16)
    low = (rest - mid.astype(F32)).astype(BF16)
    return high, mid, low


def pick(value, onehot):
    high, mid, low = split3(value)
    dot = lambda part: jnp.dot(part, onehot, preferred_element_type=F32)
    return (dot(low) + dot(mid)) + dot(high)


def is_last(axis):
    return lax.axis_index(axis) == lax.axis_size(axis) - 1


def is_even(axis):
    return lax.axis_index(axis) % 2 == 0


def sort_kernel(grains_ref, pairs_ref, own_ref, near_ref):
    flags = {(part, value): jnp.zeros((1, NB), F32) for part in "yz" for value in (0, 2)}
    for n in range(pairs_ref.shape[0]):
        pair = pairs_ref[n]
        hood = jnp.where(pair >= 0, pair, 13 * NB) >> 5
        third = (hood * 11) >> 5
        parts = {"y": third - 3 * ((third * 11) >> 5), "z": hood - 3 * third}
        flags = {k: jnp.where(parts[k[0]] == k[1], 1.0, f) for k, f in flags.items()}

    def upper(part, axis):
        alone = jnp.where(is_last(axis), 1.0 - flags[part, 0], 0.0)
        return jnp.maximum(flags[part, 2], alone)

    group = 64.0 * upper("y", "gy") + 128.0 * upper("z", "gz")
    rows = [grains_ref[r] for r in range(7)]
    centre = 0.5 * (jnp.min(rows[0], axis=1, keepdims=True) + jnp.max(rows[0], axis=1, keepdims=True))
    sub = iota((NB, TILE), 0)
    lane = iota((NB, TILE), 1)
    same = sub == lane
    group = jnp.concatenate([group, jnp.zeros((1, TILE - NB), F32)], axis=1)
    key = centre + jnp.sum(jnp.where(same, group, 0.0), axis=1, keepdims=True)
    wide = jnp.broadcast_to(key, (NB, TILE))
    key_row = jnp.sum(jnp.where(same, wide, 0.0), axis=0, keepdims=True)
    before = (wide < key_row) | ((wide == key_row) & (sub < lane))
    rank = jnp.sum(jnp.where(before, 1.0, 0.0), axis=0, keepdims=True)
    onehot = jnp.where((rank == sub.astype(F32)) & (lane < NB), 1.0, 0.0).astype(BF16)[:, :NB]
    for r in range(7):
        high, mid, low = split3(rows[r])
        dot = lambda part: jnp.dot(onehot, part, preferred_element_type=F32)
        value = (dot(low) + dot(mid)) + dot(high)
        own_ref[r] = value
        if r < 4:
            near_ref[r] = value


def box_sort(grains, pairs):
    shapes = [on_chip((7, NB, TILE)), on_chip((4, NB, TILE))]
    listed = pairs.transpose(0, 1, 2, 4, 3).reshape(pairs.shape[4], 1, NB)
    return plain_call(sort_kernel, shapes, "box_sort", grains.reshape(7, NB, TILE), listed)


def lane_take(value, index):
    dims = lax.GatherDimensionNumbers(
        offset_dims=(),
        collapsed_slice_dims=(1,),
        start_index_map=(1,),
        operand_batching_dims=(0,),
        start_indices_batching_dims=(0,),
    )
    return lax.gather(
        value, index[..., None], dims, (1, 1), mode=lax.GatherScatterMode.PROMISE_IN_BOUNDS
    )


def pack(groups, tri):
    masks = [jnp.where(mask, 1.0, 0.0).astype(BF16) for lists in groups for mask, _ in lists]
    both = jnp.dot(jnp.concatenate(masks, axis=0), tri, preferred_element_type=F32)
    rows = masks[0].shape[0]
    lane_f = iota((rows, TILE), 1).astype(F32)
    packed, at = [], 0
    for lists in groups:
        offset = jnp.zeros((rows, TILE), F32)
        outs = [jnp.zeros((rows, TILE), F32)] * 3 + [jnp.full((rows, TILE), ABSENT, F32)]
        for _, arrays in lists:
            ranks, total = both[at : at + rows, :TILE], both[at : at + rows, TILE:]
            at += rows
            wanted = lane_f - offset
            place = jnp.zeros((rows, TILE), jnp.int32)
            for bit in (64, 32, 16, 8, 4, 2, 1):
                probe = lane_take(ranks, place + (bit - 1))
                place = jnp.where(probe <= wanted, place + bit, place)
            ours = (wanted >= 0.0) & (wanted < total)
            outs = [jnp.where(ours, lane_take(a, place), o) for a, o in zip(arrays, outs)]
            offset = offset + total
        packed.append((outs, offset))
    return packed


def pair_terms(own, cand, sums):
    own_x, own_y, own_z, own_r = own
    cand_x, cand_y, cand_z, cand_r = cand
    dx, dy, dz = own_x - cand_x, own_y - cand_y, own_z - cand_z
    square = dx * dx + dy * dy + dz * dz
    distance = square * lax.rsqrt(jnp.maximum(square, 1e-30))
    overlap = jnp.maximum(own_r + cand_r - distance, 0.0)
    below = distance + SOFTEN
    guess = pl.reciprocal(below, approx=True)
    force = (0.5 * SPRING) * overlap * (guess * (2.0 - below * guess))
    fx, fy, fz = force * dx, force * dy, force * dz
    terms = (fx * dx, fy * dy, fz * dz, fx * dy, fx * dz, fy * dz)
    return tuple(s + t for s, t in zip(sums, terms))


def stress_kernel(grid_ref, side_ref, grains_ref, rim0_ref, rim1_ref, out_ref, cand_ref, all_ref, contact_ref, plane_ref, height_ref,
    feature_ref, moment_ref, own_ref, sum_ref,
):
    tri_row = iota((TILE, 2 * TILE), 0)
    tri_col = iota((TILE, 2 * TILE), 1)
    tri = jnp.where((tri_row <= tri_col) | (tri_col >= TILE), 1.0, 0.0).astype(BF16)

    span_x = BOXES_DOWNSLOPE * TILE_BOX_EDGE
    span_y = BOXES_SPANWISE * TILE_BOX_EDGE
    span_z = BOXES_NORMAL * TILE_BOX_EDGE

    def shifts(place, span):
        return jnp.where(place == 0, -span, jnp.where(place == 3, span, 0.0))

    def alive(radius):
        return jnp.where(radius == 0.0, ABSENT, radius)

    row = iota((128, TILE), 0)
    low_x = TILE_BOX_EDGE * (row & 7).astype(F32)
    low_y = TILE_BOX_EDGE * ((iota((64, TILE), 0) >> 3) & 1).astype(F32)
    low_z = TILE_BOX_EDGE * (iota((32, TILE), 0) >> 4).astype(F32)
    here = [
        grid_ref[0],
        grid_ref[1] + shifts((row >> 3) & 3, span_y),
        grid_ref[2] + shifts(row >> 5, span_z),
        alive(grid_ref[3]),
    ]
    side_row = iota((16, TILE), 0)
    sides = []
    for k, shift_x in ((0, -span_x), (1, span_x)):
        sides.append(
            [
                side_ref[k, 0] + shift_x,
                side_ref[k, 1] + shifts(side_row & 3, span_y),
                side_ref[k, 2] + shifts(side_row >> 2, span_z),
                alive(side_ref[k, 3]),
            ]
        )
    in_box_x = iota((16, 8, TILE), 1)

    def neighbours(centre, edge, step):
        cube = centre.reshape(16, 8, TILE)
        moved = pltpu.roll(cube, 1 if step < 0 else 7, 1)
        at_edge = in_box_x == (0 if step < 0 else 7)
        return jnp.where(at_edge, edge[:, None, :], moved).reshape(128, TILE)

    def near(arrays, axis, low, step):
        limit = arrays[axis] >= low - REACH if step < 0 else arrays[axis] <= low + (TILE_BOX_EDGE + REACH)
        return limit & (arrays[3] > 0.0), arrays

    def cut_y(arrays, start):
        return [a.reshape(4, 4, 8, TILE)[:, start : start + 2].reshape(64, TILE) for a in arrays]

    def cut_z(arrays, start):
        return [a[16 * start : 16 * start + 32] for a in arrays]

    before = [neighbours(c, e, -1) for c, e in zip(here, sides[0])]
    after = [neighbours(c, e, 1) for c, e in zip(here, sides[1])]
    ((beside_x, count_x),) = pack([[near(before, 0, low_x, -1), near(after, 0, low_x, 1)]], tri)
    ((beside_y, count_y),) = pack(
        [
            [
                near(cut_y(here, 0), 1, low_y, -1),
                near(cut_y(beside_x, 0), 1, low_y, -1),
                near(cut_y(here, 2), 1, low_y, 1),
                near(cut_y(beside_x, 2), 1, low_y, 1),
            ]
        ],
        tri,
    )
    mid, mid_x = cut_y(here, 1), cut_y(beside_x, 1)
    (above, count_z), (above_rest, count_w) = pack(
        [
            [near(cut_z(mid, 0), 2, low_z, -1), near(cut_z(mid, 2), 2, low_z, 1)],
            [
                near(cut_z(mid_x, 0), 2, low_z, -1),
                near(cut_z(beside_y, 0), 2, low_z, -1),
                near(cut_z(mid_x, 2), 2, low_z, 1),
                near(cut_z(beside_y, 2), 2, low_z, 1),
            ],
        ],
        tri,
    )
    worst = [
        jnp.max(count, axis=0, keepdims=True) - 8.0 * cap
        for count, cap in zip((count_x, count_y, count_z, count_w), CAPS[1:])
    ]

    def keep(ref, first, values):
        for f, value in enumerate(values):
            at = (first + f) * PITCH_ROWS
            ref[at : at + NB, :] = value

    half_box = 0.5 * TILE_BOX_EDGE
    ones = jnp.ones((NB, TILE), F32)
    none = jnp.zeros((NB, TILE), F32)

    def parts(value):
        return [p.astype(F32) for p in split3(value)]

    middle = [
        TILE_BOX_EDGE * (iota((NB, TILE), 0) & 7).astype(F32) + half_box,
        TILE_BOX_EDGE * ((iota((NB, TILE), 0) >> 3) & 1).astype(F32) + half_box,
        low_z + half_box,
    ]
    for k, chunk in enumerate((cut_z(mid, 1), cut_z(mid_x, 1), cut_z(beside_y, 1), above, above_rest)):
        x, y, z = (chunk[c] - middle[c] for c in range(3))
        squares = [x * x, y * y, z * z]
        norm = squares[0] + squares[1] + squares[2]
        xs, ys, zs, ns, rs = (parts(v) for v in (x, y, z, norm, chunk[3]))
        keep(
            feature_ref, 16 * k,
            [xs[0], ys[0], zs[0], xs[1], ys[1], zs[1], ones, ns[0]]
            + [xs[2], ys[2], zs[2], ns[1], ns[2]] + rs,
        )
        products = squares + [x * y, x * z, y * z]
        highs = [v.astype(BF16).astype(F32) for v in products]
        lows = [v - h for v, h in zip(products, highs)]
        keep(moment_ref, 16 * k, highs + [none] * 2 + lows + [none] * 2)
        if k == 0:
            for c in range(4):
                cand_ref[c * NB : c * NB + NB, :] = chunk[c]
            xi, yi, zi = ([-2.0 * p for p in v] for v in (xs, ys, zs))
            keep(
                own_ref, 0,
                [xi[0], yi[0], zi[0], xi[0], yi[0], zi[0], ns[0], ones]
                + [xi[0], yi[0], zi[0], ones, ones] + [none] * 3
                + [xi[1], yi[1], zi[1], xi[1], yi[1], zi[1], ns[1], none]
                + [xi[2], yi[2], zi[2], none, none, none, ns[2], none]
                + rs + [x, y, z],
            )
    overflow = worst[0]
    for w in worst[1:]:
        overflow = jnp.maximum(overflow, w)
    overflow = jnp.max(overflow)

    nx = CELLS_PER_EDGE * (BOXES_DOWNSLOPE + 2)
    ny = CELLS_PER_EDGE * (BOXES_SPANWISE + 2)

    def weights(coords, centres):
        diff = coords - centres
        return jnp.maximum(jnp.exp(-0.5 * diff * diff) - CUT_LEVEL, 0.0) * NORM_ONE

    def centres(places):
        return (places.astype(F32) - CELLS_PER_EDGE + 0.5) * PITCH

    at_z = iota((8, TILE), 0)
    centres_inner = centres(at_z + 4)
    centres_rim = centres(jnp.where(at_z < 4, at_z, at_z + 8))

    def put_plane(t):
        wx = weights(grains_ref[pl.ds(t, 1), :], centres(iota((nx, TILE), 0)))
        wy = weights(grains_ref[pl.ds(NB + t, 1), :], centres(iota((ny, TILE), 0)))
        parts = [wx[x : x + 1] * wy for x in list(range(4)) + list(range(nx - 4, nx))]
        inner_x = wx[4 : nx - 4]
        parts += [inner_x * wy[y : y + 1] for y in list(range(4)) + list(range(ny - 4, ny))]
        inner_y = wy[4 : ny - 4]
        parts += [wx[x : x + 1] * inner_y for x in range(4, nx - 4)]
        lanes = pl.ds(pl.multiple_of(t * TILE, TILE), TILE)
        plane_ref[:, lanes] = jnp.concatenate(parts, axis=0).astype(BF16)

    def put_height(t):
        rows = [grains_ref[pl.ds(r * NB + t, 1), :] for r in range(2, 7)]
        wz_inner = weights(rows[0], centres_inner)
        wz_rim = weights(rows[0], centres_rim)
        masses = 4.0 * math.pi / 3.0 * rows[1] * rows[1] * rows[1]
        vel = rows[2:]
        cont = [contact_ref[pl.ds(k * NB + t, 1), :] for k in range(6)]
        loads = [masses, masses * vel[0], masses * vel[1], masses * vel[2]]
        for k, (i, j) in enumerate(((0, 0), (1, 1), (2, 2), (0, 1), (0, 2), (1, 2))):
            loads.append(cont[k] + masses * (vel[i] * vel[j]))
        height = [load * wz_inner for load in loads] + [load * wz_rim for load in loads]
        lanes = pl.ds(pl.multiple_of(t * TILE, TILE), TILE)
        height_ref[:, lanes] = jnp.concatenate(height, axis=0).astype(BF16)

    def own_rows(t):
        return tuple(
            jnp.broadcast_to(cand_ref[pl.ds(c * NB + t, 1), :], (8, TILE)) for c in range(4)
        )

    def group(columns, first, g):
        return tuple(
            jnp.broadcast_to(columns[8 * g : 8 * g + 8, first + c : first + c + 1], (8, TILE)) for c in range(4)
        )

    def put(t, sums):
        for k in range(6):
            contact_ref[pl.ds(k * NB + t, 1), :] = jnp.sum(sums[k], axis=0, keepdims=True)

    zeros = tuple(jnp.zeros((8, TILE), F32) for _ in range(6))

    @pl.when(overflow <= 0.0)
    def _():
        sub = iota((8, TILE), 0)

        def one_tile(t, carry):
            put_plane(t)
            radii = [own_ref[pl.ds((32 + p) * PITCH_ROWS + t, 1), :] for p in range(3)]
            radii = [jnp.where(sub == 6, jnp.broadcast_to(r, (8, TILE)), 0.0) for r in radii]
            reach = [radii[0], jnp.where(sub >= 5, 1.0, 0.0), radii[1], radii[2]]
            rhs = jnp.concatenate(
                [own_ref[pl.ds(t, 32, stride=PITCH_ROWS), :], jnp.concatenate(reach, axis=0)], axis=1
            ).astype(BF16)
            highs, lows, moments = [], [], []
            for k in range(5):
                rows = feature_ref[pl.ds(16 * k * PITCH_ROWS + t, 16, stride=PITCH_ROWS), :]
                first = rows[:8]
                lhs = jnp.concatenate([rows, first, first], axis=0).T.astype(BF16)
                both = jnp.dot(lhs[: 8 * CAPS[k]], rhs, preferred_element_type=F32)
                square = jnp.maximum(both[:, :TILE], 1e-12)
                distance = square * lax.rsqrt(square)
                overlap = jnp.maximum(both[:, TILE:] - distance, 0.0)
                below = distance + SOFTEN
                guess = pl.reciprocal(below, approx=True)
                force = overlap * (guess * (2.0 - below * guess))
                if k == 0:
                    at = iota((TILE, TILE), 0) == iota((TILE, TILE), 1)
                    force = jnp.where(at, 0.0, force)
                high = force.astype(BF16)
                low = (force - high.astype(F32)).astype(BF16)
                rest = TILE - 8 * CAPS[k]
                highs.append(high)
                lows.append(low)
                if rest:
                    highs.append(jnp.zeros((rest, TILE), BF16))
                    lows.append(jnp.zeros((rest, TILE), BF16))
                more = moment_ref[pl.ds(16 * k * PITCH_ROWS + t, 16, stride=PITCH_ROWS), :]
                moments.append(jnp.concatenate([first, more, first], axis=0))
            lhs = jnp.concatenate(moments, axis=1).astype(BF16)
            one = jnp.dot(lhs, jnp.concatenate(highs, axis=0), preferred_element_type=F32)
            two = jnp.dot(lhs[:16], jnp.concatenate(lows, axis=0), preferred_element_type=F32)
            sum_ref[pl.ds(t, 8, stride=PITCH_ROWS), :] = one[:8] + two[:8]
            sum_ref[pl.ds(8 * PITCH_ROWS + t, 8, stride=PITCH_ROWS), :] = one[8:16] + (one[16:24] + two[8:])
            return carry

        def some_tiles(q, carry):
            for i in range(UNROLL):
                one_tile(UNROLL * q + i, carry)
            return carry

        lax.fori_loop(0, NB // UNROLL, some_tiles, 0)
        total = [sum_ref[m * PITCH_ROWS : m * PITCH_ROWS + NB, :] for m in range(14)]
        first = [total[c] + total[3 + c] for c in range(3)]
        own_mid = [own_ref[(35 + c) * PITCH_ROWS : (35 + c) * PITCH_ROWS + NB, :] for c in range(3)]
        for k, (i, j) in enumerate(((0, 0), (1, 1), (2, 2), (0, 1), (0, 2), (1, 2))):
            a, b = own_mid[i], own_mid[j]
            contact_ref[k * NB : (k + 1) * NB, :] = (0.5 * SPRING) * (
                total[8 + k] - (a * first[j] + b * first[i]) + a * b * total[6]
            )

    @pl.when(overflow > 0.0)
    def _():
        stride = 16 * 8 + 32
        for c in range(4):
            all_ref[c * stride : c * stride + 128, :] = here[c]
            all_ref[c * stride + 128 : c * stride + 144, :] = sides[0][c]
            all_ref[c * stride + 144 : c * stride + 160, :] = sides[1][c]
        all_ref[4 * stride : 8 * stride, :] = jnp.zeros((4 * stride, TILE), F32)

        def one_tile(t, carry):
            own = own_rows(t)
            tile_x, tile_y, tile_z = t & 7, (t >> 3) & 1, t >> 4

            def one_near(n, sums):
                n_x = n // 9
                n_y = (n - 9 * n_x) // 3
                n_z = n - 9 * n_x - 3 * n_y
                at_x = tile_x + n_x - 1
                plane = 4 * (tile_z + n_z) + tile_y + n_y
                place = jnp.where(
                    at_x < 0, 128 + plane, jnp.where(at_x > 7, 144 + plane, 8 * plane + at_x)
                )
                columns = all_ref[pl.ds(place, 8, stride=stride), :].T
                for g in range(16):
                    sums = pair_terms(own, group(columns, 0, g), sums)
                return sums

            put(t, lax.fori_loop(0, 27, one_near, zeros))
            put_plane(t)
            return carry

        lax.fori_loop(0, NB, one_tile, 0)

    def four_heights(q, carry):
        for i in range(4):
            put_height(4 * q + i)
        return carry

    lax.fori_loop(0, NB // 4, four_heights, 0)
    wide = lax.dot_general(
        height_ref[...], plane_ref[...], (((1,), (1,)), ((), ())), preferred_element_type=F32
    )
    out_ref[...] = wide[:, TILE:]
    rim = wide[:, :TILE]
    rim = jnp.where(is_even("gx"), pltpu.roll(rim, 64, 1), rim)
    upper, lower = rim[:80], rim[80:]
    left_half = iota((80, TILE), 1) < 64
    rim0_ref[...] = jnp.where(left_half, upper, pltpu.roll(lower, 64, 1))
    rim1_ref[...] = jnp.where(left_half, pltpu.roll(upper, 64, 1), lower)


def stress_and_deposit(grid, side, grains):
    columns = 3 * TILE + COLS
    return plain_call(
        stress_kernel,
        [on_chip((80, TILE)), on_chip((80, TILE)), on_chip((160, 2 * TILE + COLS))],
        "stress_deposit",
        held(grid),
        held(side),
        held(grains),
        scratch=[
            pltpu.VMEM((4 * NB, TILE), F32),
            pltpu.VMEM((8 * 160, TILE), F32),
            pltpu.VMEM((6 * NB, TILE), F32),
            pltpu.VMEM((columns, NB * TILE), BF16),
            pltpu.VMEM((160, NB * TILE), BF16),
            pltpu.VMEM((5 * 16 * PITCH_ROWS, TILE), F32),
            pltpu.VMEM((5 * 16 * PITCH_ROWS, TILE), F32),
            pltpu.VMEM((38 * PITCH_ROWS, TILE), F32),
            pltpu.VMEM((16 * PITCH_ROWS, TILE), F32),
        ],
    )


def rim_x_kernel(wide_ref, first_ref, second_ref, rim0_ref, rim1_ref, inner_ref):
    even = is_even("gx")
    right = jnp.where(even, first_ref[...], second_ref[...])
    left = jnp.where(even, second_ref[...], first_ref[...])
    left_half = iota((80, TILE), 1) < 64
    got = jnp.concatenate(
        [
            jnp.where(left_half, right, pltpu.roll(left, 64, 1)),
            jnp.where(left_half, pltpu.roll(right, 64, 1), left),
        ],
        axis=0,
    )
    src = iota((TILE, 1), 0)
    x = (src >> 4) & 3
    x = jnp.where(src >= 64, x, x + (CELLS_PER_EDGE * BOXES_DOWNSLOPE - 4))
    y = src & 15
    target = jnp.where(y < 4, y * 32 + x, jnp.where(y >= 12, 128 + (y - 12) * 32 + x, 256 + x * 8 + y - 4))
    onehot = jnp.where(iota((TILE, 512), 1) == target, 1.0, 0.0).astype(BF16)
    total = wide_ref[...] + pick(got, onehot)
    low, high = total[:, :TILE], total[:, TILE : 2 * TILE]
    even = is_even("gy")
    rim0_ref[...] = jnp.where(even, high, low)
    rim1_ref[...] = jnp.where(even, low, high)
    inner_ref[...] = total[:, 2 * TILE :]


def add_rim_y(inner_ref, first_ref, second_ref):
    even = is_even("gy")
    right = jnp.where(even, first_ref[...], second_ref[...])
    left = jnp.where(even, second_ref[...], first_ref[...])
    got = jnp.concatenate([left, right], axis=1)
    src = iota((256, 1), 0)
    target = (src & 31) * 8 + 4 * (src >> 7) + ((src >> 5) & 3)
    onehot = jnp.where(iota((256, 256), 1) == target, 1.0, 0.0).astype(BF16)
    return inner_ref[...] + pick(got, onehot)


def rim_y_kernel(inner_ref, first_ref, second_ref, out_ref):
    out_ref[...] = add_rim_y(inner_ref, first_ref, second_ref)


PROFILED = (0, 1, 4, 5, 6, 8)


def rim_y_two_kernel(inner_ref, first_ref, second_ref, out_ref, send_ref):
    total = add_rim_y(inner_ref, first_ref, second_ref)
    out_ref[...] = total
    lower = lax.axis_index("gz") == 0
    top = iota((8, COLS), 0) < 4
    for p in range(5):
        one = total[80 + 16 * p : 88 + 16 * p]
        two = total[88 + 16 * p : 96 + 16 * p]
        to_upper = jnp.where(top, pltpu.roll(one, 4, 0), two)
        to_lower = jnp.where(top, one, pltpu.roll(two, 4, 0))
        both = jnp.where(lower, to_upper, to_lower)
        send_ref[8 * p : 8 * p + 8, :] = both[:, :TILE]
        send_ref[40 + 8 * p : 48 + 8 * p, :] = both[:, TILE:]
    for i, c in enumerate(PROFILED):
        rows = total[8 * c : 8 * c + 8]
        send_ref[80 + 8 * i : 88 + 8 * i, :] = jnp.where(lower, rows[:, TILE:], rows[:, :TILE])


def finish_two_kernel(total_ref, got_ref, fields_ref, fits_ref, inertial_ref):
    lower = lax.axis_index("gz") == 0
    row = iota((8, COLS), 0)
    from_rim = jnp.where(lower, 7 - row, row)
    ours = from_rim < 4
    theirs = from_rim[:, :TILE] >= 4
    fields = []
    for p in range(5):
        got = jnp.concatenate(
            [got_ref[8 * p : 8 * p + 8, :], got_ref[40 + 8 * p : 48 + 8 * p, :]], axis=1
        )
        turned = pltpu.roll(got, 4, 0)
        for i, add in enumerate(
            (jnp.where(lower, turned, got), jnp.where(lower, got, turned))
        ):
            c = 2 * p + i
            fields.append(total_ref[8 * c : 8 * c + 8, :] + jnp.where(ours, add, 0.0))
            fields_ref[0, 0, 0, c] = fields[c]
    column = {}
    for i, c in enumerate(PROFILED):
        mine = jnp.where(lower, fields[c][:, :TILE], fields[c][:, TILE:])
        rim = total_ref[80 + 8 * c : 88 + 8 * c, :]
        rim = pltpu.roll(jnp.where(lower, rim[:, :TILE], rim[:, TILE:]), 4, 0)
        other = got_ref[80 + 8 * i : 88 + 8 * i, :] + jnp.where(theirs, rim, 0.0)
        column[c] = jnp.concatenate(
            [jnp.where(lower, mine, other), jnp.where(lower, other, mine)], axis=0
        )
    density = column[0]
    velocity = column[1] / (density + FLOOR_LEVEL)
    press = (column[4] + column[5] + column[6]) / 3.0
    fitted, inertial = column_fit(density, velocity, column[8], press)
    fits_ref[0, 0] = fitted
    inertial_ref[0, 0] = inertial


def held(array):
    return pltpu.with_memory_space_constraint(array, pltpu.VMEM)


def on_chip(shape):
    return pltpu.VMEM(shape, F32)


def plain_call(kernel, shapes, name, *args, scratch=()):
    vmem = pl.BlockSpec(memory_space=pltpu.VMEM)
    return pl.pallas_call(
        kernel,
        out_shape=shapes,
        in_specs=[vmem] * len(args),
        out_specs=jax.tree.map(lambda _: vmem, shapes),
        scratch_shapes=scratch,
        name=name,
    )(*args)


def column_fit(density, velocity, shear, press):
    upper = jnp.concatenate([velocity[1:, :], velocity[-1:, :]], axis=0)
    lower = jnp.concatenate([velocity[:1, :], velocity[:-1, :]], axis=0)
    rate = (upper - lower) / (2.0 * PITCH)
    inertial = rate * 1.0 / jnp.sqrt((press + FLOOR_LEVEL) / (density + FLOOR_LEVEL))
    friction = shear / (press + FLOOR_LEVEL)
    weight = density + FLOOR_LEVEL
    add = lambda v: jnp.sum(v, axis=0, keepdims=True)
    sum_zero = add(weight)
    sum_one = add(weight * inertial)
    sum_two = add(weight * inertial * inertial) + RIDGE_SHARE * sum_zero
    mix_zero = add(weight * friction)
    mix_one = add(weight * friction * inertial)
    determ = sum_zero * sum_two - sum_one * sum_one
    fitted = jnp.concatenate(
        [
            (mix_zero * sum_two - sum_one * mix_one) / determ,
            (sum_zero * mix_one - sum_one * mix_zero) / determ,
        ],
        axis=0,
    )
    return fitted, inertial


def swaps(first, second, axis):
    count = lax.axis_size(axis)
    got = []
    for start, value in ((0, first), (1, second)):
        links = []
        for i in range(start, count - 1, 2):
            links += [(i, i + 1), (i + 1, i)]
        got.append(lax.ppermute(value, axis, links) if links else jnp.zeros_like(value))
    return got


def exchange(low, high, axis):
    even = is_even(axis)
    one, two = swaps(jnp.where(even, high, low), jnp.where(even, low, high), axis)
    return jnp.where(even, two, one), jnp.where(even, one, two)


def local(grains, pairs):
    own, near = box_sort(grains, pairs)
    cube = near.reshape(4, 2, 2, 8, TILE)
    below, above = exchange(cube[:, 0], cube[:, 1], "gz")
    cube = jnp.concatenate([below[:, None], cube, above[:, None]], axis=1)
    below, above = exchange(cube[:, :, 0], cube[:, :, 1], "gy")
    cube = jnp.concatenate([below[:, :, None], cube, above[:, :, None]], axis=2)
    below, above = exchange(cube[:, :, :, 0], cube[:, :, :, 7], "gx")
    side = jnp.stack([below, above]).reshape(2, 4, 16, TILE)
    rim0, rim1, wide = stress_and_deposit(cube.reshape(4, 128, TILE), side, own.reshape(7 * NB, TILE))
    first, second = swaps(rim0, rim1, "gx")
    block, square = on_chip((160, TILE)), on_chip((160, COLS))
    rim0, rim1, inner = plain_call(
        rim_x_kernel, [block, block, square], "rim_x", held(wide), held(first), held(second)
    )
    first, second = swaps(rim0, rim1, "gy")
    if lax.axis_size("gz") == 2:
        sends = on_chip((128, TILE))
        total, send = plain_call(
            rim_y_two_kernel, [square, sends], "rim_y", held(inner), held(first), held(second)
        )
        got, _ = swaps(send, send, "gz")
        outs = [(1, 1, 1, 10, 8, COLS), (1, 1, 2, TILE), (1, 1, 16, TILE)]
        outs = [jax.ShapeDtypeStruct(shape, F32) for shape in outs]
        return tuple(plain_call(finish_two_kernel, outs, "finish", held(total), held(got)))
    total = plain_call(rim_y_kernel, square, "rim_y", held(inner), held(first), held(second))
    fields = total[:80].reshape(10, 8, COLS)
    rim = total[80:].reshape(10, 8, COLS)
    from_below, from_above = exchange(rim[:, :4], rim[:, 4:], "gz")
    fields = fields + jnp.concatenate([from_below, from_above], axis=1)
    share = COLS // lax.axis_size("gz")
    start = lax.axis_index("gz") * share
    density = fields[0]
    velocity = fields[1] / (density + FLOOR_LEVEL)
    shear = fields[8]
    press = (fields[4] + fields[5] + fields[6]) / 3.0
    profile = jnp.stack([density, velocity, shear, press])
    whole = lax.all_gather(profile, "gz", axis=1, tiled=True)
    whole = lax.dynamic_slice_in_dim(whole, start, share, 2)
    fitted, inertial = column_fit(*whole)
    return (fields[None, None, None], fitted[None, None], inertial[None, None])


def solution(mesh):
    in_specs = (P("gx", "gy", "gz", None, None), P("gx", "gy", "gz", None, None))
    out_specs = (
        P("gx", "gy", "gz", None, None, None),
        P("gx", "gy", None, "gz"),
        P("gx", "gy", None, "gz"),
    )
    return jax.shard_map(local, mesh=mesh, in_specs=in_specs, out_specs=out_specs, check_vma=False)
```

```python
import math

import jax
import jax.numpy as jnp
from jax import lax
from jax.experimental import pallas as pl
from jax.experimental.pallas import tpu as pltpu
from jax.sharding import PartitionSpec as P

TILE = 128
BOXES_DOWNSLOPE = 8
BOXES_SPANWISE = 2
BOXES_NORMAL = 2
CELLS_PER_EDGE = 4

TILE_BOX_EDGE = 5.0
SPRING = 2.0
SOFTEN = 0.05
FLOOR_LEVEL = 0.1
RIDGE_SHARE = 0.1
CUT_LEVEL = math.exp(-12.5)
NORM_ONE = 1.0 / math.sqrt(2.0 * math.pi)

PITCH = TILE_BOX_EDGE / CELLS_PER_EDGE
REACH = 1.21
ABSENT = -10.0

NB = BOXES_DOWNSLOPE * BOXES_SPANWISE * BOXES_NORMAL
PITCH_ROWS = NB + 8
COLS = CELLS_PER_EDGE * BOXES_DOWNSLOPE * CELLS_PER_EDGE * BOXES_SPANWISE
CAPS = (16, 12, 16, 12, 14)

KERNEL_VMEM = 32 * 1024 * 1024

F32 = jnp.float32
BF16 = jnp.bfloat16


def iota(shape, dim):
    return lax.broadcasted_iota(jnp.int32, shape, dim)


def split3(value):
    high = value.astype(BF16)
    rest = value - high.astype(F32)
    mid = rest.astype(BF16)
    low = (rest - mid.astype(F32)).astype(BF16)
    return high, mid, low


def pick(value, onehot):
    high, mid, low = split3(value)
    dot = lambda part: jnp.dot(part, onehot, preferred_element_type=F32)
    return (dot(low) + dot(mid)) + dot(high)


def is_last(axis):
    return lax.axis_index(axis) == lax.axis_size(axis) - 1


def is_even(axis):
    return lax.axis_index(axis) % 2 == 0


def sort_kernel(grains_ref, pairs_ref, own_ref, near_ref):
    flags = {(part, value): jnp.zeros((1, NB), F32) for part in "yz" for value in (0, 2)}
    for n in range(pairs_ref.shape[0]):
        pair = pairs_ref[n]
        hood = jnp.where(pair >= 0, pair, 13 * NB) >> 5
        third = (hood * 11) >> 5
        parts = {"y": third - 3 * ((third * 11) >> 5), "z": hood - 3 * third}
        flags = {k: jnp.where(parts[k[0]] == k[1], 1.0, f) for k, f in flags.items()}

    def upper(part, axis):
        alone = jnp.where(is_last(axis), 1.0 - flags[part, 0], 0.0)
        return jnp.maximum(flags[part, 2], alone)

    group = 64.0 * upper("y", "gy") + 128.0 * upper("z", "gz")
    rows = [grains_ref[r] for r in range(7)]
    centre = 0.5 * (jnp.min(rows[0], axis=1, keepdims=True) + jnp.max(rows[0], axis=1, keepdims=True))
    sub = iota((NB, TILE), 0)
    lane = iota((NB, TILE), 1)
    same = sub == lane
    group = jnp.concatenate([group, jnp.zeros((1, TILE - NB), F32)], axis=1)
    key = centre + jnp.sum(jnp.where(same, group, 0.0), axis=1, keepdims=True)
    wide = jnp.broadcast_to(key, (NB, TILE))
    key_row = jnp.sum(jnp.where(same, wide, 0.0), axis=0, keepdims=True)
    before = (wide < key_row) | ((wide == key_row) & (sub < lane))
    rank = jnp.sum(jnp.where(before, 1.0, 0.0), axis=0, keepdims=True)
    onehot = jnp.where((rank == sub.astype(F32)) & (lane < NB), 1.0, 0.0).astype(BF16)[:, :NB]
    for r in range(7):
        high, mid, low = split3(rows[r])
        dot = lambda part: jnp.dot(onehot, part, preferred_element_type=F32)
        value = (dot(low) + dot(mid)) + dot(high)
        own_ref[r] = value
        if r < 4:
            near_ref[r] = value


def box_sort(grains, pairs):
    shapes = [on_chip((7, NB, TILE)), on_chip((4, NB, TILE))]
    listed = pairs.transpose(0, 1, 2, 4, 3).reshape(pairs.shape[4], 1, NB)
    arrays = (pltpu.with_memory_space_constraint(a, pltpu.HBM) for a in (grains.reshape(7, NB, TILE), listed))
    return plain_call(sort_kernel, shapes, "box_sort", *arrays)


def lane_take(value, index):
    dims = lax.GatherDimensionNumbers(
        offset_dims=(),
        collapsed_slice_dims=(1,),
        start_index_map=(1,),
        operand_batching_dims=(0,),
        start_indices_batching_dims=(0,),
    )
    return lax.gather(
        value, index[..., None], dims, (1, 1), mode=lax.GatherScatterMode.PROMISE_IN_BOUNDS
    )


def pack(groups, tri):
    masks = [jnp.where(mask, 1.0, 0.0).astype(BF16) for lists in groups for mask, _ in lists]
    both = jnp.dot(jnp.concatenate(masks, axis=0), tri, preferred_element_type=F32)
    rows = masks[0].shape[0]
    lane_f = iota((rows, TILE), 1).astype(F32)
    packed, at = [], 0
    for lists in groups:
        offset = jnp.zeros((rows, TILE), F32)
        outs = [jnp.zeros((rows, TILE), F32)] * 3 + [jnp.full((rows, TILE), ABSENT, F32)]
        for _, arrays in lists:
            ranks, total = both[at : at + rows, :TILE], both[at : at + rows, TILE:]
            at += rows
            wanted = lane_f - offset
            place = jnp.zeros((rows, TILE), jnp.int32)
            for bit in (64, 32, 16, 8, 4, 2, 1):
                probe = lane_take(ranks, place + (bit - 1))
                place = jnp.where(probe <= wanted, place + bit, place)
            ours = (wanted >= 0.0) & (wanted < total)
            outs = [jnp.where(ours, lane_take(a, place), o) for a, o in zip(arrays, outs)]
            offset = offset + total
        packed.append((outs, offset))
    return packed


def pair_terms(own, cand, sums):
    own_x, own_y, own_z, own_r = own
    cand_x, cand_y, cand_z, cand_r = cand
    dx, dy, dz = own_x - cand_x, own_y - cand_y, own_z - cand_z
    square = dx * dx + dy * dy + dz * dz
    distance = square * lax.rsqrt(jnp.maximum(square, 1e-30))
    overlap = jnp.maximum(own_r + cand_r - distance, 0.0)
    below = distance + SOFTEN
    guess = pl.reciprocal(below, approx=True)
    force = (0.5 * SPRING) * overlap * (guess * (2.0 - below * guess))
    fx, fy, fz = force * dx, force * dy, force * dz
    terms = (fx * dx, fy * dy, fz * dz, fx * dy, fx * dz, fy * dz)
    return tuple(s + t for s, t in zip(sums, terms))


def weights(coords, centres):
    diff = coords - centres
    return jnp.maximum(jnp.exp(-0.5 * diff * diff) - CUT_LEVEL, 0.0) * NORM_ONE


def centres(places):
    return (places.astype(F32) - CELLS_PER_EDGE + 0.5) * PITCH


def plane_kernel(own_ref, plane_ref):
    nx = CELLS_PER_EDGE * (BOXES_DOWNSLOPE + 2)
    ny = CELLS_PER_EDGE * (BOXES_SPANWISE + 2)

    def put_plane(t):
        wx = weights(own_ref[0, pl.ds(t, 1), :], centres(iota((nx, TILE), 0)))
        wy = weights(own_ref[1, pl.ds(t, 1), :], centres(iota((ny, TILE), 0)))
        parts = [wx[x : x + 1] * wy for x in list(range(4)) + list(range(nx - 4, nx))]
        inner_x = wx[4 : nx - 4]
        parts += [inner_x * wy[y : y + 1] for y in list(range(4)) + list(range(ny - 4, ny))]
        inner_y = wy[4 : ny - 4]
        parts += [wx[x : x + 1] * inner_y for x in range(4, nx - 4)]
        lanes = pl.ds(pl.multiple_of(t * TILE, TILE), TILE)
        plane_ref[:, lanes] = jnp.concatenate(parts, axis=0).astype(BF16)

    def four_planes(q, carry):
        for i in range(4):
            put_plane(4 * q + i)
        return carry

    lax.fori_loop(0, NB // 4, four_planes, 0)


def stress_kernel(
    grid_ref, side_ref, grains_ref, plane_ref, rim0_ref, rim1_ref, out_ref,
    cand_ref, all_ref, contact_ref, height_ref, feature_ref, moment_ref, own_ref, sum_ref, even_ref, odd_ref,
):
    tri_row = iota((TILE, 2 * TILE), 0)
    tri_col = iota((TILE, 2 * TILE), 1)
    tri = jnp.where((tri_row <= tri_col) | (tri_col >= TILE), 1.0, 0.0).astype(BF16)

    span_x = BOXES_DOWNSLOPE * TILE_BOX_EDGE
    span_y = BOXES_SPANWISE * TILE_BOX_EDGE
    span_z = BOXES_NORMAL * TILE_BOX_EDGE

    def shifts(place, span):
        return jnp.where(place == 0, -span, jnp.where(place == 3, span, 0.0))

    def alive(radius):
        return jnp.where(radius == 0.0, ABSENT, radius)

    row = iota((128, TILE), 0)
    low_x = TILE_BOX_EDGE * (row & 7).astype(F32)
    low_y = TILE_BOX_EDGE * ((iota((64, TILE), 0) >> 3) & 1).astype(F32)
    low_z = TILE_BOX_EDGE * (iota((32, TILE), 0) >> 4).astype(F32)
    here = [
        grid_ref[0],
        grid_ref[1] + shifts((row >> 3) & 3, span_y),
        grid_ref[2] + shifts(row >> 5, span_z),
        alive(grid_ref[3]),
    ]
    side_row = iota((16, TILE), 0)
    sides = []
    for k, shift_x in ((0, -span_x), (1, span_x)):
        sides.append(
            [
                side_ref[k, 0] + shift_x,
                side_ref[k, 1] + shifts(side_row & 3, span_y),
                side_ref[k, 2] + shifts(side_row >> 2, span_z),
                alive(side_ref[k, 3]),
            ]
        )
    in_box_x = iota((16, 8, TILE), 1)

    def neighbours(centre, edge, step):
        cube = centre.reshape(16, 8, TILE)
        moved = pltpu.roll(cube, 1 if step < 0 else 7, 1)
        at_edge = in_box_x == (0 if step < 0 else 7)
        return jnp.where(at_edge, edge[:, None, :], moved).reshape(128, TILE)

    def near(arrays, axis, low, step):
        limit = arrays[axis] >= low - REACH if step < 0 else arrays[axis] <= low + (TILE_BOX_EDGE + REACH)
        return limit & (arrays[3] > 0.0), arrays

    def cut_y(arrays, start):
        return [a.reshape(4, 4, 8, TILE)[:, start : start + 2].reshape(64, TILE) for a in arrays]

    def cut_z(arrays, start):
        return [a[16 * start : 16 * start + 32] for a in arrays]

    before = [neighbours(c, e, -1) for c, e in zip(here, sides[0])]
    after = [neighbours(c, e, 1) for c, e in zip(here, sides[1])]
    ((beside_x, count_x),) = pack([[near(before, 0, low_x, -1), near(after, 0, low_x, 1)]], tri)
    ((beside_y, count_y),) = pack(
        [
            [
                near(cut_y(here, 0), 1, low_y, -1),
                near(cut_y(beside_x, 0), 1, low_y, -1),
                near(cut_y(here, 2), 1, low_y, 1),
                near(cut_y(beside_x, 2), 1, low_y, 1),
            ]
        ],
        tri,
    )
    mid, mid_x = cut_y(here, 1), cut_y(beside_x, 1)
    (above, count_z), (above_rest, count_w) = pack(
        [
            [near(cut_z(mid, 0), 2, low_z, -1), near(cut_z(mid, 2), 2, low_z, 1)],
            [
                near(cut_z(mid_x, 0), 2, low_z, -1),
                near(cut_z(beside_y, 0), 2, low_z, -1),
                near(cut_z(mid_x, 2), 2, low_z, 1),
                near(cut_z(beside_y, 2), 2, low_z, 1),
            ],
        ],
        tri,
    )
    worst = [
        jnp.max(count, axis=0, keepdims=True) - 8.0 * cap
        for count, cap in zip((count_x, count_y, count_z, count_w), CAPS[1:])
    ]

    def keep(ref, first, values):
        for f, value in enumerate(values):
            at = (first + f) * PITCH_ROWS
            ref[at : at + NB, :] = value

    half_box = 0.5 * TILE_BOX_EDGE
    ones = jnp.ones((NB, TILE), F32)
    none = jnp.zeros((NB, TILE), F32)

    def parts(value):
        return [p.astype(F32) for p in split3(value)]

    middle = [
        TILE_BOX_EDGE * (iota((NB, TILE), 0) & 7).astype(F32) + half_box,
        TILE_BOX_EDGE * ((iota((NB, TILE), 0) >> 3) & 1).astype(F32) + half_box,
        low_z + half_box,
    ]
    for k, chunk in enumerate((cut_z(mid, 1), cut_z(mid_x, 1), cut_z(beside_y, 1), above, above_rest)):
        x, y, z = (chunk[c] - middle[c] for c in range(3))
        squares = [x * x, y * y, z * z]
        norm = squares[0] + squares[1] + squares[2]
        xs, ys, zs, ns, rs = (parts(v) for v in (x, y, z, norm, chunk[3]))
        keep(
            feature_ref, 16 * k,
            [xs[0], ys[0], zs[0], xs[1], ys[1], zs[1], ones, ns[0]]
            + [xs[2], ys[2], zs[2], ns[1], ns[2]] + rs,
        )
        products = squares + [x * y, x * z, y * z]
        highs = [v.astype(BF16).astype(F32) for v in products]
        lows = [v - h for v, h in zip(products, highs)]
        keep(moment_ref, 16 * k, highs + [none] * 2 + lows + [none] * 2)
        if k == 0:
            for c in range(4):
                cand_ref[c * NB : c * NB + NB, :] = chunk[c]
            xi, yi, zi = ([-2.0 * p for p in v] for v in (xs, ys, zs))
            keep(
                own_ref, 0,
                [xi[0], yi[0], zi[0], xi[0], yi[0], zi[0], ns[0], ones]
                + [xi[0], yi[0], zi[0], ones, ones] + [none] * 3
                + [xi[1], yi[1], zi[1], xi[1], yi[1], zi[1], ns[1], none]
                + [xi[2], yi[2], zi[2], none, none, none, ns[2], none]
                + rs + [x, y, z],
            )
    overflow = worst[0]
    for w in worst[1:]:
        overflow = jnp.maximum(overflow, w)
    overflow = jnp.max(overflow)

    at_z = iota((8, TILE), 0)
    centres_inner = centres(at_z + 4)
    centres_rim = centres(jnp.where(at_z < 4, at_z, at_z + 8))

    def put_height(t):
        rows = [grains_ref[pl.ds(r * NB + t, 1), :] for r in range(2, 7)]
        wz_inner = weights(rows[0], centres_inner)
        wz_rim = weights(rows[0], centres_rim)
        masses = 4.0 * math.pi / 3.0 * rows[1] * rows[1] * rows[1]
        vel = rows[2:]
        cont = [contact_ref[pl.ds(k * NB + t, 1), :] for k in range(6)]
        loads = [masses, masses * vel[0], masses * vel[1], masses * vel[2]]
        for k, (i, j) in enumerate(((0, 0), (1, 1), (2, 2), (0, 1), (0, 2), (1, 2))):
            loads.append(cont[k] + masses * (vel[i] * vel[j]))
        height = [load * wz_inner for load in loads] + [load * wz_rim for load in loads]
        lanes = pl.ds(pl.multiple_of(t * TILE, TILE), TILE)
        height_ref[:, lanes] = jnp.concatenate(height, axis=0).astype(BF16)

    def own_rows(t):
        return tuple(
            jnp.broadcast_to(cand_ref[pl.ds(c * NB + t, 1), :], (8, TILE)) for c in range(4)
        )

    def group(columns, first, g):
        return tuple(
            jnp.broadcast_to(columns[8 * g : 8 * g + 8, first + c : first + c + 1], (8, TILE)) for c in range(4)
        )

    def put(t, sums):
        for k in range(6):
            contact_ref[pl.ds(k * NB + t, 1), :] = jnp.sum(sums[k], axis=0, keepdims=True)

    zeros = tuple(jnp.zeros((8, TILE), F32) for _ in range(6))

    @pl.when(overflow <= 0.0)
    def _():
        sub = iota((8, TILE), 0)
        starts = [8 * sum(CAPS[:k]) for k in range(5)]

        def own_side(t):
            radii = [own_ref[pl.ds((32 + p) * PITCH_ROWS + t, 1), :] for p in range(3)]
            radii = [jnp.where(sub == 6, jnp.broadcast_to(r, (8, TILE)), 0.0) for r in radii]
            reach = [radii[0], jnp.where(sub >= 5, 1.0, 0.0), radii[1], radii[2]]
            return jnp.concatenate(
                [own_ref[pl.ds(t, 32, stride=PITCH_ROWS), :], jnp.concatenate(reach, axis=0)], axis=1
            ).astype(BF16)

        def measure_pairs(t, k, rhs, ref):
            rows = feature_ref[pl.ds(16 * k * PITCH_ROWS + t, 16, stride=PITCH_ROWS), :]
            first = rows[:8]
            lhs = jnp.concatenate([rows, first, first], axis=0).T.astype(BF16)
            size = 8 * CAPS[k]
            ref[starts[k] : starts[k] + size, :] = jnp.dot(lhs[:size], rhs, preferred_element_type=F32)

        def forces(k, ref):
            size = 8 * CAPS[k]
            square = jnp.maximum(ref[starts[k] : starts[k] + size, :TILE], 1e-12)
            distance = square * lax.rsqrt(square)
            overlap = jnp.maximum(ref[starts[k] : starts[k] + size, TILE:] - distance, 0.0)
            below = distance + SOFTEN
            guess = pl.reciprocal(below, approx=True)
            force = overlap * (guess * (2.0 - below * guess))
            if k == 0:
                at = iota((TILE, TILE), 0) == iota((TILE, TILE), 1)
                force = jnp.where(at, 0.0, force)
            high = force.astype(BF16)
            low = (force - high.astype(F32)).astype(BF16)
            rest = TILE - size
            if rest:
                none = jnp.zeros((rest, TILE), BF16)
                high, low = (jnp.concatenate([v, none], axis=0) for v in (high, low))
            return high, low

        def add_up(t, parts):
            moments = []
            for k in range(5):
                first = feature_ref[pl.ds(16 * k * PITCH_ROWS + t, 8, stride=PITCH_ROWS), :]
                more = moment_ref[pl.ds(16 * k * PITCH_ROWS + t, 16, stride=PITCH_ROWS), :]
                moments.append(jnp.concatenate([first, more, first], axis=0))
            lhs = jnp.concatenate(moments, axis=1).astype(BF16)
            highs = jnp.concatenate([p[0] for p in parts], axis=0)
            lows = jnp.concatenate([p[1] for p in parts], axis=0)
            one = jnp.dot(lhs, highs, preferred_element_type=F32)
            two = jnp.dot(lhs[:16], lows, preferred_element_type=F32)
            sum_ref[pl.ds(t, 8, stride=PITCH_ROWS), :] = one[:8] + two[:8]
            sum_ref[pl.ds(8 * PITCH_ROWS + t, 8, stride=PITCH_ROWS), :] = one[8:16] + (one[16:24] + two[8:])

        def step(t, here_ref, next_t, next_ref):
            rhs = own_side(next_t)
            parts = []
            for k in range(5):
                measure_pairs(next_t, k, rhs, next_ref)
                parts.append(forces(k, here_ref))
            add_up(t, parts)

        first_rhs = own_side(0)
        for k in range(5):
            measure_pairs(0, k, first_rhs, even_ref)

        def four_tiles(q, carry):
            step(4 * q, even_ref, 4 * q + 1, odd_ref)
            step(4 * q + 1, odd_ref, 4 * q + 2, even_ref)
            step(4 * q + 2, even_ref, 4 * q + 3, odd_ref)
            step(4 * q + 3, odd_ref, jnp.minimum(4 * q + 4, NB - 1), even_ref)
            return carry

        lax.fori_loop(0, NB // 4, four_tiles, 0)
        total = [sum_ref[m * PITCH_ROWS : m * PITCH_ROWS + NB, :] for m in range(14)]
        first = [total[c] + total[3 + c] for c in range(3)]
        own_mid = [own_ref[(35 + c) * PITCH_ROWS : (35 + c) * PITCH_ROWS + NB, :] for c in range(3)]
        for k, (i, j) in enumerate(((0, 0), (1, 1), (2, 2), (0, 1), (0, 2), (1, 2))):
            a, b = own_mid[i], own_mid[j]
            contact_ref[k * NB : (k + 1) * NB, :] = (0.5 * SPRING) * (
                total[8 + k] - (a * first[j] + b * first[i]) + a * b * total[6]
            )

    @pl.when(overflow > 0.0)
    def _():
        stride = 16 * 8 + 32
        for c in range(4):
            all_ref[c * stride : c * stride + 128, :] = here[c]
            all_ref[c * stride + 128 : c * stride + 144, :] = sides[0][c]
            all_ref[c * stride + 144 : c * stride + 160, :] = sides[1][c]
        all_ref[4 * stride : 8 * stride, :] = jnp.zeros((4 * stride, TILE), F32)

        def one_tile(t, carry):
            own = own_rows(t)
            tile_x, tile_y, tile_z = t & 7, (t >> 3) & 1, t >> 4

            def one_near(n, sums):
                n_x = n // 9
                n_y = (n - 9 * n_x) // 3
                n_z = n - 9 * n_x - 3 * n_y
                at_x = tile_x + n_x - 1
                plane = 4 * (tile_z + n_z) + tile_y + n_y
                place = jnp.where(
                    at_x < 0, 128 + plane, jnp.where(at_x > 7, 144 + plane, 8 * plane + at_x)
                )
                columns = all_ref[pl.ds(place, 8, stride=stride), :].T
                for g in range(16):
                    sums = pair_terms(own, group(columns, 0, g), sums)
                return sums

            put(t, lax.fori_loop(0, 27, one_near, zeros))
            return carry

        lax.fori_loop(0, NB, one_tile, 0)

    def four_heights(q, carry):
        for i in range(4):
            put_height(4 * q + i)
        return carry

    lax.fori_loop(0, NB // 4, four_heights, 0)
    wide = lax.dot_general(
        height_ref[...], plane_ref[...], (((1,), (1,)), ((), ())), preferred_element_type=F32
    )
    out_ref[...] = wide[:, TILE:]
    rim = wide[:, :TILE]
    rim = jnp.where(is_even("gx"), pltpu.roll(rim, 64, 1), rim)
    upper, lower = rim[:80], rim[80:]
    left_half = iota((80, TILE), 1) < 64
    rim0_ref[...] = jnp.where(left_half, upper, pltpu.roll(lower, 64, 1))
    rim1_ref[...] = jnp.where(left_half, pltpu.roll(upper, 64, 1), lower)


def stress_and_deposit(grid, side, grains, plane):
    return plain_call(
        stress_kernel,
        [on_chip((80, TILE)), on_chip((80, TILE)), on_chip((160, 2 * TILE + COLS))],
        "stress_deposit",
        held(grid),
        held(side),
        held(grains),
        held(plane),
        scratch=[
            pltpu.VMEM((4 * NB, TILE), F32),
            pltpu.VMEM((8 * 160, TILE), F32),
            pltpu.VMEM((6 * NB, TILE), F32),
            pltpu.VMEM((160, NB * TILE), BF16),
            pltpu.VMEM((5 * 16 * PITCH_ROWS, TILE), F32),
            pltpu.VMEM((5 * 16 * PITCH_ROWS, TILE), F32),
            pltpu.VMEM((38 * PITCH_ROWS, TILE), F32),
            pltpu.VMEM((16 * PITCH_ROWS, TILE), F32),
            pltpu.VMEM((8 * sum(CAPS), 2 * TILE), F32),
            pltpu.VMEM((8 * sum(CAPS), 2 * TILE), F32),
        ],
    )


def rim_x_kernel(wide_ref, first_ref, second_ref, rim0_ref, rim1_ref, inner_ref):
    even = is_even("gx")
    right = jnp.where(even, first_ref[...], second_ref[...])
    left = jnp.where(even, second_ref[...], first_ref[...])
    left_half = iota((80, TILE), 1) < 64
    got = jnp.concatenate(
        [
            jnp.where(left_half, right, pltpu.roll(left, 64, 1)),
            jnp.where(left_half, pltpu.roll(right, 64, 1), left),
        ],
        axis=0,
    )
    src = iota((TILE, 1), 0)
    x = (src >> 4) & 3
    x = jnp.where(src >= 64, x, x + (CELLS_PER_EDGE * BOXES_DOWNSLOPE - 4))
    y = src & 15
    target = jnp.where(y < 4, y * 32 + x, jnp.where(y >= 12, 128 + (y - 12) * 32 + x, 256 + x * 8 + y - 4))
    onehot = jnp.where(iota((TILE, 512), 1) == target, 1.0, 0.0).astype(BF16)
    total = wide_ref[...] + pick(got, onehot)
    low, high = total[:, :TILE], total[:, TILE : 2 * TILE]
    even = is_even("gy")
    rim0_ref[...] = jnp.where(even, high, low)
    rim1_ref[...] = jnp.where(even, low, high)
    inner_ref[...] = total[:, 2 * TILE :]


def add_rim_y(inner_ref, first_ref, second_ref):
    even = is_even("gy")
    right = jnp.where(even, first_ref[...], second_ref[...])
    left = jnp.where(even, second_ref[...], first_ref[...])
    got = jnp.concatenate([left, right], axis=1)
    src = iota((256, 1), 0)
    target = (src & 31) * 8 + 4 * (src >> 7) + ((src >> 5) & 3)
    onehot = jnp.where(iota((256, 256), 1) == target, 1.0, 0.0).astype(BF16)
    return inner_ref[...] + pick(got, onehot)


def rim_y_kernel(inner_ref, first_ref, second_ref, out_ref):
    out_ref[...] = add_rim_y(inner_ref, first_ref, second_ref)


PROFILED = (0, 1, 4, 5, 6, 8)


def rim_y_two_kernel(inner_ref, first_ref, second_ref, out_ref, send_ref):
    total = add_rim_y(inner_ref, first_ref, second_ref)
    out_ref[...] = total
    lower = lax.axis_index("gz") == 0
    top = iota((8, COLS), 0) < 4
    for p in range(5):
        one = total[80 + 16 * p : 88 + 16 * p]
        two = total[88 + 16 * p : 96 + 16 * p]
        to_upper = jnp.where(top, pltpu.roll(one, 4, 0), two)
        to_lower = jnp.where(top, one, pltpu.roll(two, 4, 0))
        both = jnp.where(lower, to_upper, to_lower)
        send_ref[8 * p : 8 * p + 8, :] = both[:, :TILE]
        send_ref[40 + 8 * p : 48 + 8 * p, :] = both[:, TILE:]
    for i, c in enumerate(PROFILED):
        rows = total[8 * c : 8 * c + 8]
        send_ref[80 + 8 * i : 88 + 8 * i, :] = jnp.where(lower, rows[:, TILE:], rows[:, :TILE])


def finish_two_kernel(total_ref, got_ref, fields_ref, fits_ref, inertial_ref):
    lower = lax.axis_index("gz") == 0
    row = iota((8, COLS), 0)
    from_rim = jnp.where(lower, 7 - row, row)
    ours = from_rim < 4
    theirs = from_rim[:, :TILE] >= 4
    fields = []
    for p in range(5):
        got = jnp.concatenate(
            [got_ref[8 * p : 8 * p + 8, :], got_ref[40 + 8 * p : 48 + 8 * p, :]], axis=1
        )
        turned = pltpu.roll(got, 4, 0)
        for i, add in enumerate(
            (jnp.where(lower, turned, got), jnp.where(lower, got, turned))
        ):
            c = 2 * p + i
            fields.append(total_ref[8 * c : 8 * c + 8, :] + jnp.where(ours, add, 0.0))
            fields_ref[0, 0, 0, c] = fields[c]
    column = {}
    for i, c in enumerate(PROFILED):
        mine = jnp.where(lower, fields[c][:, :TILE], fields[c][:, TILE:])
        rim = total_ref[80 + 8 * c : 88 + 8 * c, :]
        rim = pltpu.roll(jnp.where(lower, rim[:, :TILE], rim[:, TILE:]), 4, 0)
        other = got_ref[80 + 8 * i : 88 + 8 * i, :] + jnp.where(theirs, rim, 0.0)
        column[c] = jnp.concatenate(
            [jnp.where(lower, mine, other), jnp.where(lower, other, mine)], axis=0
        )
    density = column[0]
    velocity = column[1] / (density + FLOOR_LEVEL)
    press = (column[4] + column[5] + column[6]) / 3.0
    fitted, inertial = column_fit(density, velocity, column[8], press)
    fits_ref[0, 0] = fitted
    inertial_ref[0, 0] = inertial


def held(array):
    return pltpu.with_memory_space_constraint(array, pltpu.VMEM)


def on_chip(shape, dtype=F32):
    return pltpu.VMEM(shape, dtype)


def plain_call(kernel, shapes, name, *args, scratch=()):
    vmem = pl.BlockSpec(memory_space=pltpu.VMEM)
    return pl.pallas_call(
        kernel,
        out_shape=shapes,
        in_specs=[vmem] * len(args),
        out_specs=jax.tree.map(lambda _: vmem, shapes),
        scratch_shapes=scratch,
        compiler_params=pltpu.CompilerParams(vmem_limit_bytes=KERNEL_VMEM),
        name=name,
    )(*args)


def column_fit(density, velocity, shear, press):
    upper = jnp.concatenate([velocity[1:, :], velocity[-1:, :]], axis=0)
    lower = jnp.concatenate([velocity[:1, :], velocity[:-1, :]], axis=0)
    rate = (upper - lower) / (2.0 * PITCH)
    inertial = rate * 1.0 / jnp.sqrt((press + FLOOR_LEVEL) / (density + FLOOR_LEVEL))
    friction = shear / (press + FLOOR_LEVEL)
    weight = density + FLOOR_LEVEL
    add = lambda v: jnp.sum(v, axis=0, keepdims=True)
    sum_zero = add(weight)
    sum_one = add(weight * inertial)
    sum_two = add(weight * inertial * inertial) + RIDGE_SHARE * sum_zero
    mix_zero = add(weight * friction)
    mix_one = add(weight * friction * inertial)
    determ = sum_zero * sum_two - sum_one * sum_one
    fitted = jnp.concatenate(
        [
            (mix_zero * sum_two - sum_one * mix_one) / determ,
            (sum_zero * mix_one - sum_one * mix_zero) / determ,
        ],
        axis=0,
    )
    return fitted, inertial


def swaps(first, second, axis):
    count = lax.axis_size(axis)
    got = []
    for start, value in ((0, first), (1, second)):
        links = []
        for i in range(start, count - 1, 2):
            links += [(i, i + 1), (i + 1, i)]
        got.append(lax.ppermute(value, axis, links) if links else jnp.zeros_like(value))
    return got


def exchange(low, high, axis):
    even = is_even(axis)
    one, two = swaps(jnp.where(even, high, low), jnp.where(even, low, high), axis)
    return jnp.where(even, two, one), jnp.where(even, one, two)


def local(grains, pairs):
    own, near = box_sort(grains, pairs)
    cube = near.reshape(4, 2, 2, 8, TILE)
    below, above = exchange(cube[:, 0], cube[:, 1], "gz")
    cube = jnp.concatenate([below[:, None], cube, above[:, None]], axis=1)
    sends = (cube[:, :, 0], cube[:, :, 1])
    sends, placed = lax.optimization_barrier((sends, own))
    plane = plain_call(
        plane_kernel, on_chip((3 * TILE + COLS, NB * TILE), BF16), "plane", held(placed)
    )
    below, above = exchange(*sends, "gy")
    cube = jnp.concatenate([below[:, :, None], cube, above[:, :, None]], axis=2)
    cube, plane = lax.optimization_barrier((cube, plane))
    below, above = exchange(cube[:, :, :, 0], cube[:, :, :, 7], "gx")
    side = jnp.stack([below, above]).reshape(2, 4, 16, TILE)
    rim0, rim1, wide = stress_and_deposit(cube.reshape(4, 128, TILE), side, own.reshape(7 * NB, TILE), plane)
    first, second = swaps(rim0, rim1, "gx")
    block, square = on_chip((160, TILE)), on_chip((160, COLS))
    rim0, rim1, inner = plain_call(
        rim_x_kernel, [block, block, square], "rim_x", held(wide), held(first), held(second)
    )
    first, second = swaps(rim0, rim1, "gy")
    if lax.axis_size("gz") == 2:
        sends = on_chip((128, TILE))
        total, send = plain_call(
            rim_y_two_kernel, [square, sends], "rim_y", held(inner), held(first), held(second)
        )
        got, _ = swaps(send, send, "gz")
        outs = [(1, 1, 1, 10, 8, COLS), (1, 1, 2, TILE), (1, 1, 16, TILE)]
        outs = [jax.ShapeDtypeStruct(shape, F32) for shape in outs]
        return tuple(plain_call(finish_two_kernel, outs, "finish", held(total), held(got)))
    total = plain_call(rim_y_kernel, square, "rim_y", held(inner), held(first), held(second))
    fields = total[:80].reshape(10, 8, COLS)
    rim = total[80:].reshape(10, 8, COLS)
    from_below, from_above = exchange(rim[:, :4], rim[:, 4:], "gz")
    fields = fields + jnp.concatenate([from_below, from_above], axis=1)
    share = COLS // lax.axis_size("gz")
    start = lax.axis_index("gz") * share
    density = fields[0]
    velocity = fields[1] / (density + FLOOR_LEVEL)
    shear = fields[8]
    press = (fields[4] + fields[5] + fields[6]) / 3.0
    profile = jnp.stack([density, velocity, shear, press])
    whole = lax.all_gather(profile, "gz", axis=1, tiled=True)
    whole = lax.dynamic_slice_in_dim(whole, start, share, 2)
    fitted, inertial = column_fit(*whole)
    return (fields[None, None, None], fitted[None, None], inertial[None, None])


def solution(mesh):
    in_specs = (P("gx", "gy", "gz", None, None), P("gx", "gy", "gz", None, None))
    out_specs = (
        P("gx", "gy", "gz", None, None, None),
        P("gx", "gy", None, "gz"),
        P("gx", "gy", None, "gz"),
    )
    return jax.shard_map(local, mesh=mesh, in_specs=in_specs, out_specs=out_specs, check_vma=False)
```

```python
import math

import jax
import jax.numpy as jnp
from jax import lax
from jax.experimental import pallas as pl
from jax.experimental.pallas import tpu as pltpu
from jax.sharding import PartitionSpec as P

TILE = 128
BOXES_DOWNSLOPE = 8
BOXES_SPANWISE = 2
BOXES_NORMAL = 2
CELLS_PER_EDGE = 4

TILE_BOX_EDGE = 5.0
SPRING = 2.0
SOFTEN = 0.05
FLOOR_LEVEL = 0.1
RIDGE_SHARE = 0.1
CUT_LEVEL = math.exp(-12.5)
NORM_ONE = 1.0 / math.sqrt(2.0 * math.pi)

PITCH = TILE_BOX_EDGE / CELLS_PER_EDGE
REACH = 1.21
ABSENT = -10.0

NB = BOXES_DOWNSLOPE * BOXES_SPANWISE * BOXES_NORMAL
PITCH_ROWS = NB + 8
COLS = CELLS_PER_EDGE * BOXES_DOWNSLOPE * CELLS_PER_EDGE * BOXES_SPANWISE
CAPS = (16, 12, 16, 12, 14)

KERNEL_VMEM = 32 * 1024 * 1024

F32 = jnp.float32
BF16 = jnp.bfloat16


def iota(shape, dim):
    return lax.broadcasted_iota(jnp.int32, shape, dim)


def split3(value):
    high = value.astype(BF16)
    rest = value - high.astype(F32)
    mid = rest.astype(BF16)
    low = (rest - mid.astype(F32)).astype(BF16)
    return high, mid, low


def pick(value, onehot):
    high, mid, low = split3(value)
    dot = lambda part: jnp.dot(part, onehot, preferred_element_type=F32)
    return (dot(low) + dot(mid)) + dot(high)


def is_last(axis):
    return lax.axis_index(axis) == lax.axis_size(axis) - 1


def is_even(axis):
    return lax.axis_index(axis) % 2 == 0


def sort_kernel(grains_ref, pairs_ref, own_ref, near_ref):
    flags = {(part, value): jnp.zeros((1, NB), F32) for part in "yz" for value in (0, 2)}
    for n in range(pairs_ref.shape[0]):
        pair = pairs_ref[n]
        hood = jnp.where(pair >= 0, pair, 13 * NB) >> 5
        third = (hood * 11) >> 5
        parts = {"y": third - 3 * ((third * 11) >> 5), "z": hood - 3 * third}
        flags = {k: jnp.where(parts[k[0]] == k[1], 1.0, f) for k, f in flags.items()}

    def upper(part, axis):
        alone = jnp.where(is_last(axis), 1.0 - flags[part, 0], 0.0)
        return jnp.maximum(flags[part, 2], alone)

    group = 64.0 * upper("y", "gy") + 128.0 * upper("z", "gz")
    rows = [grains_ref[r] for r in range(7)]
    centre = 0.5 * (jnp.min(rows[0], axis=1, keepdims=True) + jnp.max(rows[0], axis=1, keepdims=True))
    sub = iota((NB, TILE), 0)
    lane = iota((NB, TILE), 1)
    same = sub == lane
    group = jnp.concatenate([group, jnp.zeros((1, TILE - NB), F32)], axis=1)
    key = centre + jnp.sum(jnp.where(same, group, 0.0), axis=1, keepdims=True)
    wide = jnp.broadcast_to(key, (NB, TILE))
    key_row = jnp.sum(jnp.where(same, wide, 0.0), axis=0, keepdims=True)
    before = (wide < key_row) | ((wide == key_row) & (sub < lane))
    rank = jnp.sum(jnp.where(before, 1.0, 0.0), axis=0, keepdims=True)
    onehot = jnp.where((rank == sub.astype(F32)) & (lane < NB), 1.0, 0.0).astype(BF16)[:, :NB]
    for r in range(7):
        high, mid, low = split3(rows[r])
        dot = lambda part: jnp.dot(onehot, part, preferred_element_type=F32)
        value = (dot(low) + dot(mid)) + dot(high)
        own_ref[r] = value
        if r < 4:
            near_ref[r] = value


def box_sort(grains, pairs):
    shapes = [on_chip((7, NB, TILE)), on_chip((4, NB, TILE))]
    listed = pairs.transpose(0, 1, 2, 4, 3).reshape(pairs.shape[4], 1, NB)
    arrays = (pltpu.with_memory_space_constraint(a, pltpu.HBM) for a in (grains.reshape(7, NB, TILE), listed))
    return plain_call(sort_kernel, shapes, "box_sort", *arrays)


def lane_take(value, index):
    dims = lax.GatherDimensionNumbers(
        offset_dims=(),
        collapsed_slice_dims=(1,),
        start_index_map=(1,),
        operand_batching_dims=(0,),
        start_indices_batching_dims=(0,),
    )
    return lax.gather(
        value, index[..., None], dims, (1, 1), mode=lax.GatherScatterMode.PROMISE_IN_BOUNDS
    )


def pack(groups, tri):
    masks = [jnp.where(mask, 1.0, 0.0).astype(BF16) for lists in groups for mask, _ in lists]
    both = jnp.dot(jnp.concatenate(masks, axis=0), tri, preferred_element_type=F32)
    rows = masks[0].shape[0]
    ranks = both[:, :TILE]
    totals = [both[n * rows : (n + 1) * rows, TILE:] for n in range(len(masks))]
    offsets, ends, at = [], [], 0
    for lists in groups:
        offset = jnp.zeros((rows, TILE), F32)
        for _ in lists:
            offsets.append(offset)
            offset = offset + totals[at]
            at += 1
        ends.append(offset)
    lane_f = iota((rows, TILE), 1).astype(F32)
    wanted = jnp.concatenate([lane_f - offset for offset in offsets], axis=0)
    place = jnp.zeros(wanted.shape, jnp.int32)
    for bit in (64, 32, 16, 8, 4, 2, 1):
        place = jnp.where(lane_take(ranks, place + (bit - 1)) <= wanted, place + bit, place)
    packed, at = [], 0
    for lists, end in zip(groups, ends):
        outs = [jnp.zeros((rows, TILE), F32)] * 3 + [jnp.full((rows, TILE), ABSENT, F32)]
        for _, arrays in lists:
            here = slice(at * rows, (at + 1) * rows)
            ours = (wanted[here] >= 0.0) & (wanted[here] < totals[at])
            outs = [jnp.where(ours, lane_take(v, place[here]), o) for v, o in zip(arrays, outs)]
            at += 1
        packed.append((outs, end))
    return packed


def pair_terms(own, cand, sums):
    own_x, own_y, own_z, own_r = own
    cand_x, cand_y, cand_z, cand_r = cand
    dx, dy, dz = own_x - cand_x, own_y - cand_y, own_z - cand_z
    square = dx * dx + dy * dy + dz * dz
    distance = square * lax.rsqrt(jnp.maximum(square, 1e-30))
    overlap = jnp.maximum(own_r + cand_r - distance, 0.0)
    below = distance + SOFTEN
    guess = pl.reciprocal(below, approx=True)
    force = (0.5 * SPRING) * overlap * (guess * (2.0 - below * guess))
    fx, fy, fz = force * dx, force * dy, force * dz
    terms = (fx * dx, fy * dy, fz * dz, fx * dy, fx * dz, fy * dz)
    return tuple(s + t for s, t in zip(sums, terms))


def weights(coords, centres):
    diff = coords - centres
    return jnp.maximum(jnp.exp(-0.5 * diff * diff) - CUT_LEVEL, 0.0) * NORM_ONE


def centres(places):
    return (places.astype(F32) - CELLS_PER_EDGE + 0.5) * PITCH


def plane_kernel(own_ref, plane_ref):
    nx = CELLS_PER_EDGE * (BOXES_DOWNSLOPE + 2)
    ny = CELLS_PER_EDGE * (BOXES_SPANWISE + 2)

    def put_plane(t):
        wx = weights(own_ref[0, pl.ds(t, 1), :], centres(iota((nx, TILE), 0)))
        wy = weights(own_ref[1, pl.ds(t, 1), :], centres(iota((ny, TILE), 0)))
        parts = [wx[x : x + 1] * wy for x in list(range(4)) + list(range(nx - 4, nx))]
        inner_x = wx[4 : nx - 4]
        parts += [inner_x * wy[y : y + 1] for y in list(range(4)) + list(range(ny - 4, ny))]
        inner_y = wy[4 : ny - 4]
        parts += [wx[x : x + 1] * inner_y for x in range(4, nx - 4)]
        lanes = pl.ds(pl.multiple_of(t * TILE, TILE), TILE)
        plane_ref[:, lanes] = jnp.concatenate(parts, axis=0).astype(BF16)

    def four_planes(q, carry):
        for i in range(4):
            put_plane(4 * q + i)
        return carry

    lax.fori_loop(0, NB // 4, four_planes, 0)


SPAN_X = BOXES_DOWNSLOPE * TILE_BOX_EDGE
SPAN_Y = BOXES_SPANWISE * TILE_BOX_EDGE
SPAN_Z = BOXES_NORMAL * TILE_BOX_EDGE


def running_sums():
    row, col = iota((TILE, 2 * TILE), 0), iota((TILE, 2 * TILE), 1)
    return jnp.where((row <= col) | (col >= TILE), 1.0, 0.0).astype(BF16)


def shifts(place, span):
    return jnp.where(place == 0, -span, jnp.where(place == 3, span, 0.0))


def alive(radius):
    return jnp.where(radius == 0.0, ABSENT, radius)


def near(arrays, axis, low, step):
    limit = arrays[axis] >= low - REACH if step < 0 else arrays[axis] <= low + (TILE_BOX_EDGE + REACH)
    return limit & (arrays[3] > 0.0), arrays


def in_this_frame(grid_ref):
    row = iota((128, TILE), 0)
    return [
        grid_ref[0],
        grid_ref[1] + shifts((row >> 3) & 3, SPAN_Y),
        grid_ref[2] + shifts(row >> 5, SPAN_Z),
        alive(grid_ref[3]),
    ]


def beside_in_this_frame(side_ref):
    row = iota((16, TILE), 0)
    return [
        [
            side_ref[k, 0] + shift_x,
            side_ref[k, 1] + shifts(row & 3, SPAN_Y),
            side_ref[k, 2] + shifts(row >> 2, SPAN_Z),
            alive(side_ref[k, 3]),
        ]
        for k, shift_x in ((0, -SPAN_X), (1, SPAN_X))
    ]


def parts(value):
    return [p.astype(F32) for p in split3(value)]


def keep(ref, first, values):
    for f, value in enumerate(values):
        at = (first + f) * PITCH_ROWS
        ref[at : at + NB, :] = value


def keep_chunks(chunks, feature_ref, moment_ref, own_ref=None):
    half_box = 0.5 * TILE_BOX_EDGE
    ones = jnp.ones((NB, TILE), F32)
    none = jnp.zeros((NB, TILE), F32)
    tile = iota((NB, TILE), 0)
    middle = [
        TILE_BOX_EDGE * (tile & 7).astype(F32) + half_box,
        TILE_BOX_EDGE * ((tile >> 3) & 1).astype(F32) + half_box,
        TILE_BOX_EDGE * (tile >> 4).astype(F32) + half_box,
    ]
    for k, chunk in enumerate(chunks):
        x, y, z = (chunk[c] - middle[c] for c in range(3))
        squares = [x * x, y * y, z * z]
        norm = squares[0] + squares[1] + squares[2]
        xs, ys, zs, ns, rs = (parts(v) for v in (x, y, z, norm, chunk[3]))
        keep(
            feature_ref, 16 * k,
            [xs[0], ys[0], zs[0], xs[1], ys[1], zs[1], ones, ns[0]]
            + [xs[2], ys[2], zs[2], ns[1], ns[2]] + rs,
        )
        products = squares + [x * y, x * z, y * z]
        highs = [v.astype(BF16).astype(F32) for v in products]
        lows = [v - h for v, h in zip(products, highs)]
        keep(moment_ref, 16 * k, highs + [none] * 2 + lows + [none] * 2)
        if own_ref is not None and k == 0:
            xi, yi, zi = ([-2.0 * p for p in v] for v in (xs, ys, zs))
            keep(
                own_ref, 0,
                [xi[0], yi[0], zi[0], xi[0], yi[0], zi[0], ns[0], ones]
                + [xi[0], yi[0], zi[0], ones, ones] + [none] * 3
                + [xi[1], yi[1], zi[1], xi[1], yi[1], zi[1], ns[1], none]
                + [xi[2], yi[2], zi[2], none, none, none, ns[2], none]
                + rs + [x, y, z],
            )


def excess(counts, caps):
    worst = [jnp.max(n, axis=0, keepdims=True) - 8.0 * cap for n, cap in zip(counts, caps)]
    while len(worst) > 1:
        worst = [jnp.maximum(worst[0], worst[1])] + worst[2:]
    return worst[0]


def pick_rows(arrays, starts, size):
    return [jnp.concatenate([v[at : at + size] for at in starts], axis=0) for v in arrays]


def near_kernel(grid_ref, lists_ref, excess_ref, feature_ref, moment_ref, own_ref):
    tri = running_sums()
    here = in_this_frame(grid_ref)
    low_z = TILE_BOX_EDGE * (iota((64, TILE), 0) >> 5).astype(F32)
    low_y = TILE_BOX_EDGE * ((iota((32, TILE), 0) >> 3) & 1).astype(F32)
    cut_z = lambda start: [v[32 * start : 32 * start + 64] for v in here]
    cut_y = lambda arrays, start: pick_rows(arrays, (8 * start, 32 + 8 * start), 16)
    level = cut_z(1)
    ((beside_z, count_z),) = pack([[near(cut_z(0), 2, low_z, -1), near(cut_z(2), 2, low_z, 1)]], tri)
    ((beside_y, count_y),) = pack(
        [
            [
                near(cut_y(level, 0), 1, low_y, -1),
                near(cut_y(beside_z, 0), 1, low_y, -1),
                near(cut_y(level, 2), 1, low_y, 1),
                near(cut_y(beside_z, 2), 1, low_y, 1),
            ]
        ],
        tri,
    )
    excess_ref[...] = excess((count_z, count_y), CAPS[1:3])
    chunks = [cut_y(level, 1), cut_y(beside_z, 1), beside_y]
    for k in range(2):
        for c in range(4):
            lists_ref[4 * k + c] = chunks[1 + k][c]
    keep_chunks(chunks, feature_ref, moment_ref, own_ref)


def find_near(grid):
    table = lambda rows: on_chip((rows * PITCH_ROWS, TILE))
    shapes = [on_chip((8, NB, TILE)), on_chip((1, TILE)), table(3 * 16), table(3 * 16), table(38)]
    return plain_call(near_kernel, shapes, "near", held(grid))


def stress_kernel(
    grid_ref, side_ref, grains_ref, plane_ref, lists_ref, excess_ref, feature_near_ref, moment_near_ref, own_ref,
    rim0_ref, rim1_ref, out_ref,
    all_ref, contact_ref, height_ref, feature_far_ref, moment_far_ref, sum_ref, even_ref, odd_ref,
):
    tri = running_sums()
    sides = beside_in_this_frame(side_ref)

    edge = [jnp.concatenate([low, high], axis=0) for low, high in zip(*sides)]
    low_z = TILE_BOX_EDGE * ((iota((16, TILE), 0) >> 2) & 1).astype(F32)
    low_y = TILE_BOX_EDGE * (iota((8, TILE), 0) & 1).astype(F32)
    cut_z = lambda start: pick_rows(edge, (4 * start, 16 + 4 * start), 8)
    cut_y = lambda arrays, start: pick_rows(arrays, [4 * i + start for i in range(4)], 2)
    level = cut_z(1)
    ((edge_z, count_ez),) = pack([[near(cut_z(0), 2, low_z, -1), near(cut_z(2), 2, low_z, 1)]], tri)
    ((edge_y, count_ey),) = pack(
        [
            [
                near(cut_y(level, 0), 1, low_y, -1),
                near(cut_y(edge_z, 0), 1, low_y, -1),
                near(cut_y(level, 2), 1, low_y, 1),
                near(cut_y(edge_z, 2), 1, low_y, 1),
            ]
        ],
        tri,
    )
    edge_own, edge_z = cut_y(level, 1), cut_y(edge_z, 1)

    low_x = TILE_BOX_EDGE * (iota((NB, TILE), 0) & 7).astype(F32)
    in_box_x = iota((4, 8, TILE), 1)

    def along_x(arrays, edges, step):
        found = []
        for value, rim in zip(arrays, edges):
            moved = pltpu.roll(value.reshape(4, 8, TILE), 1 if step < 0 else 7, 1)
            rim = rim[:4] if step < 0 else rim[4:]
            at_edge = in_box_x == (0 if step < 0 else 7)
            found.append(jnp.where(at_edge, rim[:, None, :], moved).reshape(NB, TILE))
        return near(found, 0, low_x, step)

    own = [grains_ref[c * NB : (c + 1) * NB, :] for c in range(4)]
    list_z = [lists_ref[c] for c in range(4)]
    list_y = [lists_ref[4 + c] for c in range(4)]
    (beside, count_x), (beside_rest, count_w) = pack(
        [
            [along_x(own, edge_own, -1), along_x(own, edge_own, 1)],
            [
                along_x(list_z, edge_z, -1),
                along_x(list_y, edge_y, -1),
                along_x(list_z, edge_z, 1),
                along_x(list_y, edge_y, 1),
            ],
        ],
        tri,
    )
    keep_chunks([beside, beside_rest], feature_far_ref, moment_far_ref)
    overflow = jnp.maximum(
        excess_ref[...], excess((count_ez, count_ey, count_x, count_w), CAPS[1:])
    )
    overflow = jnp.max(overflow)

    def table(near_ref, far_ref, k):
        return (near_ref, k) if k < 3 else (far_ref, k - 3)

    at_z = iota((8, TILE), 0)
    centres_inner = centres(at_z + 4)
    centres_rim = centres(jnp.where(at_z < 4, at_z, at_z + 8))

    def put_height(t):
        rows = [grains_ref[pl.ds(r * NB + t, 1), :] for r in range(2, 7)]
        wz_inner = weights(rows[0], centres_inner)
        wz_rim = weights(rows[0], centres_rim)
        masses = 4.0 * math.pi / 3.0 * rows[1] * rows[1] * rows[1]
        vel = rows[2:]
        cont = [contact_ref[pl.ds(k * NB + t, 1), :] for k in range(6)]
        loads = [masses, masses * vel[0], masses * vel[1], masses * vel[2]]
        for k, (i, j) in enumerate(((0, 0), (1, 1), (2, 2), (0, 1), (0, 2), (1, 2))):
            loads.append(cont[k] + masses * (vel[i] * vel[j]))
        height = [load * wz_inner for load in loads] + [load * wz_rim for load in loads]
        lanes = pl.ds(pl.multiple_of(t * TILE, TILE), TILE)
        height_ref[:, lanes] = jnp.concatenate(height, axis=0).astype(BF16)

    def own_rows(t):
        return tuple(
            jnp.broadcast_to(grains_ref[pl.ds(c * NB + t, 1), :], (8, TILE)) for c in range(4)
        )

    def group(columns, first, g):
        return tuple(
            jnp.broadcast_to(columns[8 * g : 8 * g + 8, first + c : first + c + 1], (8, TILE)) for c in range(4)
        )

    def put(t, sums):
        for k in range(6):
            contact_ref[pl.ds(k * NB + t, 1), :] = jnp.sum(sums[k], axis=0, keepdims=True)

    zeros = tuple(jnp.zeros((8, TILE), F32) for _ in range(6))

    @pl.when(overflow <= 0.0)
    def _():
        sub = iota((8, TILE), 0)
        starts = [8 * sum(CAPS[:k]) for k in range(5)]

        def own_side(t):
            radii = [own_ref[pl.ds((32 + p) * PITCH_ROWS + t, 1), :] for p in range(3)]
            radii = [jnp.where(sub == 6, jnp.broadcast_to(r, (8, TILE)), 0.0) for r in radii]
            reach = [radii[0], jnp.where(sub >= 5, 1.0, 0.0), radii[1], radii[2]]
            return jnp.concatenate(
                [own_ref[pl.ds(t, 32, stride=PITCH_ROWS), :], jnp.concatenate(reach, axis=0)], axis=1
            ).astype(BF16)

        def measure_pairs(t, k, rhs, ref):
            source, n = table(feature_near_ref, feature_far_ref, k)
            rows = source[pl.ds(16 * n * PITCH_ROWS + t, 16, stride=PITCH_ROWS), :]
            first = rows[:8]
            lhs = jnp.concatenate([rows, first, first], axis=0).T.astype(BF16)
            size = 8 * CAPS[k]
            ref[starts[k] : starts[k] + size, :] = jnp.dot(lhs[:size], rhs, preferred_element_type=F32)

        def forces(k, ref):
            size = 8 * CAPS[k]
            square = jnp.maximum(ref[starts[k] : starts[k] + size, :TILE], 1e-12)
            distance = square * lax.rsqrt(square)
            overlap = jnp.maximum(ref[starts[k] : starts[k] + size, TILE:] - distance, 0.0)
            below = distance + SOFTEN
            guess = pl.reciprocal(below, approx=True)
            force = overlap * (guess * (2.0 - below * guess))
            if k == 0:
                at = iota((TILE, TILE), 0) == iota((TILE, TILE), 1)
                force = jnp.where(at, 0.0, force)
            high = force.astype(BF16)
            low = (force - high.astype(F32)).astype(BF16)
            rest = TILE - size
            if rest:
                none = jnp.zeros((rest, TILE), BF16)
                high, low = (jnp.concatenate([v, none], axis=0) for v in (high, low))
            return high, low

        def add_up(t, parts):
            moments = []
            for k in range(5):
                source, n = table(feature_near_ref, feature_far_ref, k)
                first = source[pl.ds(16 * n * PITCH_ROWS + t, 8, stride=PITCH_ROWS), :]
                source, n = table(moment_near_ref, moment_far_ref, k)
                more = source[pl.ds(16 * n * PITCH_ROWS + t, 16, stride=PITCH_ROWS), :]
                moments.append(jnp.concatenate([first, more, first], axis=0))
            lhs = jnp.concatenate(moments, axis=1).astype(BF16)
            highs = jnp.concatenate([p[0] for p in parts], axis=0)
            lows = jnp.concatenate([p[1] for p in parts], axis=0)
            one = jnp.dot(lhs, highs, preferred_element_type=F32)
            two = jnp.dot(lhs[:16], lows, preferred_element_type=F32)
            sum_ref[pl.ds(t, 8, stride=PITCH_ROWS), :] = one[:8] + two[:8]
            sum_ref[pl.ds(8 * PITCH_ROWS + t, 8, stride=PITCH_ROWS), :] = one[8:16] + (one[16:24] + two[8:])

        def step(t, here_ref, next_t, next_ref):
            rhs = own_side(next_t)
            parts = []
            for k in range(5):
                measure_pairs(next_t, k, rhs, next_ref)
                parts.append(forces(k, here_ref))
            add_up(t, parts)

        first_rhs = own_side(0)
        for k in range(5):
            measure_pairs(0, k, first_rhs, even_ref)

        def four_tiles(q, carry):
            step(4 * q, even_ref, 4 * q + 1, odd_ref)
            step(4 * q + 1, odd_ref, 4 * q + 2, even_ref)
            step(4 * q + 2, even_ref, 4 * q + 3, odd_ref)
            step(4 * q + 3, odd_ref, jnp.minimum(4 * q + 4, NB - 1), even_ref)
            return carry

        lax.fori_loop(0, NB // 4, four_tiles, 0)
        total = [sum_ref[m * PITCH_ROWS : m * PITCH_ROWS + NB, :] for m in range(14)]
        first = [total[c] + total[3 + c] for c in range(3)]
        own_mid = [own_ref[(35 + c) * PITCH_ROWS : (35 + c) * PITCH_ROWS + NB, :] for c in range(3)]
        for k, (i, j) in enumerate(((0, 0), (1, 1), (2, 2), (0, 1), (0, 2), (1, 2))):
            a, b = own_mid[i], own_mid[j]
            contact_ref[k * NB : (k + 1) * NB, :] = (0.5 * SPRING) * (
                total[8 + k] - (a * first[j] + b * first[i]) + a * b * total[6]
            )

    @pl.when(overflow > 0.0)
    def _():
        stride = 16 * 8 + 32
        here = in_this_frame(grid_ref)
        for c in range(4):
            all_ref[c * stride : c * stride + 128, :] = here[c]
            all_ref[c * stride + 128 : c * stride + 144, :] = sides[0][c]
            all_ref[c * stride + 144 : c * stride + 160, :] = sides[1][c]
        all_ref[4 * stride : 8 * stride, :] = jnp.zeros((4 * stride, TILE), F32)

        def one_tile(t, carry):
            own = own_rows(t)
            tile_x, tile_y, tile_z = t & 7, (t >> 3) & 1, t >> 4

            def one_near(n, sums):
                n_x = n // 9
                n_y = (n - 9 * n_x) // 3
                n_z = n - 9 * n_x - 3 * n_y
                at_x = tile_x + n_x - 1
                plane = 4 * (tile_z + n_z) + tile_y + n_y
                place = jnp.where(
                    at_x < 0, 128 + plane, jnp.where(at_x > 7, 144 + plane, 8 * plane + at_x)
                )
                columns = all_ref[pl.ds(place, 8, stride=stride), :].T
                for g in range(16):
                    sums = pair_terms(own, group(columns, 0, g), sums)
                return sums

            put(t, lax.fori_loop(0, 27, one_near, zeros))
            return carry

        lax.fori_loop(0, NB, one_tile, 0)

    def four_heights(q, carry):
        for i in range(4):
            put_height(4 * q + i)
        return carry

    lax.fori_loop(0, NB // 4, four_heights, 0)
    wide = lax.dot_general(
        height_ref[...], plane_ref[...], (((1,), (1,)), ((), ())), preferred_element_type=F32
    )
    out_ref[...] = wide[:, TILE:]
    rim = wide[:, :TILE]
    rim = jnp.where(is_even("gx"), pltpu.roll(rim, 64, 1), rim)
    upper, lower = rim[:80], rim[80:]
    left_half = iota((80, TILE), 1) < 64
    rim0_ref[...] = jnp.where(left_half, upper, pltpu.roll(lower, 64, 1))
    rim1_ref[...] = jnp.where(left_half, pltpu.roll(upper, 64, 1), lower)


def stress_and_deposit(grid, side, grains, plane, *tables):
    return plain_call(
        stress_kernel,
        [on_chip((80, TILE)), on_chip((80, TILE)), on_chip((160, 2 * TILE + COLS))],
        "stress_deposit",
        held(grid),
        held(side),
        held(grains),
        held(plane),
        *(held(v) for v in tables),
        scratch=[
            pltpu.VMEM((8 * 160, TILE), F32),
            pltpu.VMEM((6 * NB, TILE), F32),
            pltpu.VMEM((160, NB * TILE), BF16),
            pltpu.VMEM((2 * 16 * PITCH_ROWS, TILE), F32),
            pltpu.VMEM((2 * 16 * PITCH_ROWS, TILE), F32),
            pltpu.VMEM((16 * PITCH_ROWS, TILE), F32),
            pltpu.VMEM((8 * sum(CAPS), 2 * TILE), F32),
            pltpu.VMEM((8 * sum(CAPS), 2 * TILE), F32),
        ],
    )


def rim_x_kernel(wide_ref, first_ref, second_ref, rim0_ref, rim1_ref, inner_ref):
    even = is_even("gx")
    right = jnp.where(even, first_ref[...], second_ref[...])
    left = jnp.where(even, second_ref[...], first_ref[...])
    left_half = iota((80, TILE), 1) < 64
    got = jnp.concatenate(
        [
            jnp.where(left_half, right, pltpu.roll(left, 64, 1)),
            jnp.where(left_half, pltpu.roll(right, 64, 1), left),
        ],
        axis=0,
    )
    src = iota((TILE, 1), 0)
    x = (src >> 4) & 3
    x = jnp.where(src >= 64, x, x + (CELLS_PER_EDGE * BOXES_DOWNSLOPE - 4))
    y = src & 15
    target = jnp.where(y < 4, y * 32 + x, jnp.where(y >= 12, 128 + (y - 12) * 32 + x, 256 + x * 8 + y - 4))
    onehot = jnp.where(iota((TILE, 512), 1) == target, 1.0, 0.0).astype(BF16)
    total = wide_ref[...] + pick(got, onehot)
    low, high = total[:, :TILE], total[:, TILE : 2 * TILE]
    even = is_even("gy")
    rim0_ref[...] = jnp.where(even, high, low)
    rim1_ref[...] = jnp.where(even, low, high)
    inner_ref[...] = total[:, 2 * TILE :]


def add_rim_y(inner_ref, first_ref, second_ref):
    even = is_even("gy")
    right = jnp.where(even, first_ref[...], second_ref[...])
    left = jnp.where(even, second_ref[...], first_ref[...])
    got = jnp.concatenate([left, right], axis=1)
    src = iota((256, 1), 0)
    target = (src & 31) * 8 + 4 * (src >> 7) + ((src >> 5) & 3)
    onehot = jnp.where(iota((256, 256), 1) == target, 1.0, 0.0).astype(BF16)
    return inner_ref[...] + pick(got, onehot)


def rim_y_kernel(inner_ref, first_ref, second_ref, out_ref):
    out_ref[...] = add_rim_y(inner_ref, first_ref, second_ref)


PROFILED = (0, 1, 4, 5, 6, 8)


def rim_y_two_kernel(inner_ref, first_ref, second_ref, out_ref, send_ref):
    total = add_rim_y(inner_ref, first_ref, second_ref)
    out_ref[...] = total
    lower = lax.axis_index("gz") == 0
    top = iota((8, COLS), 0) < 4
    for p in range(5):
        one = total[80 + 16 * p : 88 + 16 * p]
        two = total[88 + 16 * p : 96 + 16 * p]
        to_upper = jnp.where(top, pltpu.roll(one, 4, 0), two)
        to_lower = jnp.where(top, one, pltpu.roll(two, 4, 0))
        both = jnp.where(lower, to_upper, to_lower)
        send_ref[8 * p : 8 * p + 8, :] = both[:, :TILE]
        send_ref[40 + 8 * p : 48 + 8 * p, :] = both[:, TILE:]
    for i, c in enumerate(PROFILED):
        rows = total[8 * c : 8 * c + 8]
        send_ref[80 + 8 * i : 88 + 8 * i, :] = jnp.where(lower, rows[:, TILE:], rows[:, :TILE])


def finish_two_kernel(total_ref, got_ref, fields_ref, fits_ref, inertial_ref):
    lower = lax.axis_index("gz") == 0
    row = iota((8, COLS), 0)
    from_rim = jnp.where(lower, 7 - row, row)
    ours = from_rim < 4
    theirs = from_rim[:, :TILE] >= 4
    fields = []
    for p in range(5):
        got = jnp.concatenate(
            [got_ref[8 * p : 8 * p + 8, :], got_ref[40 + 8 * p : 48 + 8 * p, :]], axis=1
        )
        turned = pltpu.roll(got, 4, 0)
        for i, add in enumerate(
            (jnp.where(lower, turned, got), jnp.where(lower, got, turned))
        ):
            c = 2 * p + i
            fields.append(total_ref[8 * c : 8 * c + 8, :] + jnp.where(ours, add, 0.0))
            fields_ref[0, 0, 0, c] = fields[c]
    column = {}
    for i, c in enumerate(PROFILED):
        mine = jnp.where(lower, fields[c][:, :TILE], fields[c][:, TILE:])
        rim = total_ref[80 + 8 * c : 88 + 8 * c, :]
        rim = pltpu.roll(jnp.where(lower, rim[:, :TILE], rim[:, TILE:]), 4, 0)
        other = got_ref[80 + 8 * i : 88 + 8 * i, :] + jnp.where(theirs, rim, 0.0)
        column[c] = jnp.concatenate(
            [jnp.where(lower, mine, other), jnp.where(lower, other, mine)], axis=0
        )
    density = column[0]
    velocity = column[1] / (density + FLOOR_LEVEL)
    press = (column[4] + column[5] + column[6]) / 3.0
    fitted, inertial = column_fit(density, velocity, column[8], press)
    fits_ref[0, 0] = fitted
    inertial_ref[0, 0] = inertial


def held(array):
    return pltpu.with_memory_space_constraint(array, pltpu.VMEM)


def on_chip(shape, dtype=F32):
    return pltpu.VMEM(shape, dtype)


def plain_call(kernel, shapes, name, *args, scratch=()):
    vmem = pl.BlockSpec(memory_space=pltpu.VMEM)
    return pl.pallas_call(
        kernel,
        out_shape=shapes,
        in_specs=[vmem] * len(args),
        out_specs=jax.tree.map(lambda _: vmem, shapes),
        scratch_shapes=scratch,
        compiler_params=pltpu.CompilerParams(vmem_limit_bytes=KERNEL_VMEM),
        name=name,
    )(*args)


def column_fit(density, velocity, shear, press):
    upper = jnp.concatenate([velocity[1:, :], velocity[-1:, :]], axis=0)
    lower = jnp.concatenate([velocity[:1, :], velocity[:-1, :]], axis=0)
    rate = (upper - lower) / (2.0 * PITCH)
    inertial = rate * 1.0 / jnp.sqrt((press + FLOOR_LEVEL) / (density + FLOOR_LEVEL))
    friction = shear / (press + FLOOR_LEVEL)
    weight = density + FLOOR_LEVEL
    add = lambda v: jnp.sum(v, axis=0, keepdims=True)
    sum_zero = add(weight)
    sum_one = add(weight * inertial)
    sum_two = add(weight * inertial * inertial) + RIDGE_SHARE * sum_zero
    mix_zero = add(weight * friction)
    mix_one = add(weight * friction * inertial)
    determ = sum_zero * sum_two - sum_one * sum_one
    fitted = jnp.concatenate(
        [
            (mix_zero * sum_two - sum_one * mix_one) / determ,
            (sum_zero * mix_one - sum_one * mix_zero) / determ,
        ],
        axis=0,
    )
    return fitted, inertial


def swaps(first, second, axis):
    count = lax.axis_size(axis)
    got = []
    for start, value in ((0, first), (1, second)):
        links = []
        for i in range(start, count - 1, 2):
            links += [(i, i + 1), (i + 1, i)]
        got.append(lax.ppermute(value, axis, links) if links else jnp.zeros_like(value))
    return got


def exchange(low, high, axis):
    even = is_even(axis)
    one, two = swaps(jnp.where(even, high, low), jnp.where(even, low, high), axis)
    return jnp.where(even, two, one), jnp.where(even, one, two)


def local(grains, pairs):
    own, near = box_sort(grains, pairs)
    cube = near.reshape(4, 2, 2, 8, TILE)
    below, above = exchange(cube[:, 0], cube[:, 1], "gz")
    cube = jnp.concatenate([below[:, None], cube, above[:, None]], axis=1)
    sends = (cube[:, :, 0], cube[:, :, 1])
    sends, placed = lax.optimization_barrier((sends, own))
    plane = plain_call(
        plane_kernel, on_chip((3 * TILE + COLS, NB * TILE), BF16), "plane", held(placed)
    )
    below, above = exchange(*sends, "gy")
    cube = jnp.concatenate([below[:, :, None], cube, above[:, :, None]], axis=2)
    cube, plane = lax.optimization_barrier((cube, plane))
    sends = (cube[:, :, :, 0], cube[:, :, :, 7])
    sends, placed = lax.optimization_barrier((sends, cube))
    tables = find_near(placed.reshape(4, 128, TILE))
    below, above = exchange(*sends, "gx")
    side = jnp.stack([below, above]).reshape(2, 4, 16, TILE)
    rim0, rim1, wide = stress_and_deposit(cube.reshape(4, 128, TILE), side, own.reshape(7 * NB, TILE), plane, *tables)
    first, second = swaps(rim0, rim1, "gx")
    block, square = on_chip((160, TILE)), on_chip((160, COLS))
    rim0, rim1, inner = plain_call(
        rim_x_kernel, [block, block, square], "rim_x", held(wide), held(first), held(second)
    )
    first, second = swaps(rim0, rim1, "gy")
    if lax.axis_size("gz") == 2:
        sends = on_chip((128, TILE))
        total, send = plain_call(
            rim_y_two_kernel, [square, sends], "rim_y", held(inner), held(first), held(second)
        )
        got, _ = swaps(send, send, "gz")
        outs = [(1, 1, 1, 10, 8, COLS), (1, 1, 2, TILE), (1, 1, 16, TILE)]
        outs = [jax.ShapeDtypeStruct(shape, F32) for shape in outs]
        return tuple(plain_call(finish_two_kernel, outs, "finish", held(total), held(got)))
    total = plain_call(rim_y_kernel, square, "rim_y", held(inner), held(first), held(second))
    fields = total[:80].reshape(10, 8, COLS)
    rim = total[80:].reshape(10, 8, COLS)
    from_below, from_above = exchange(rim[:, :4], rim[:, 4:], "gz")
    fields = fields + jnp.concatenate([from_below, from_above], axis=1)
    share = COLS // lax.axis_size("gz")
    start = lax.axis_index("gz") * share
    density = fields[0]
    velocity = fields[1] / (density + FLOOR_LEVEL)
    shear = fields[8]
    press = (fields[4] + fields[5] + fields[6]) / 3.0
    profile = jnp.stack([density, velocity, shear, press])
    whole = lax.all_gather(profile, "gz", axis=1, tiled=True)
    whole = lax.dynamic_slice_in_dim(whole, start, share, 2)
    fitted, inertial = column_fit(*whole)
    return (fields[None, None, None], fitted[None, None], inertial[None, None])


def solution(mesh):
    in_specs = (P("gx", "gy", "gz", None, None), P("gx", "gy", "gz", None, None))
    out_specs = (
        P("gx", "gy", "gz", None, None, None),
        P("gx", "gy", None, "gz"),
        P("gx", "gy", None, "gz"),
    )
    return jax.shard_map(local, mesh=mesh, in_specs=in_specs, out_specs=out_specs, check_vma=False)
```

```python
import math

import jax
import jax.numpy as jnp
from jax import lax
from jax.experimental import pallas as pl
from jax.experimental.pallas import tpu as pltpu
from jax.sharding import PartitionSpec as P

TILE = 128
BOXES_DOWNSLOPE = 8
BOXES_SPANWISE = 2
BOXES_NORMAL = 2
CELLS_PER_EDGE = 4

TILE_BOX_EDGE = 5.0
SPRING = 2.0
SOFTEN = 0.05
FLOOR_LEVEL = 0.1
RIDGE_SHARE = 0.1
CUT_LEVEL = math.exp(-12.5)
NORM_ONE = 1.0 / math.sqrt(2.0 * math.pi)

PITCH = TILE_BOX_EDGE / CELLS_PER_EDGE
REACH = 1.21
ABSENT = -10.0

NB = BOXES_DOWNSLOPE * BOXES_SPANWISE * BOXES_NORMAL
PITCH_ROWS = NB + 8
COLS = CELLS_PER_EDGE * BOXES_DOWNSLOPE * CELLS_PER_EDGE * BOXES_SPANWISE
CAPS = (16, 12, 16, 12, 14)

KERNEL_VMEM = 32 * 1024 * 1024

F32 = jnp.float32
BF16 = jnp.bfloat16


def iota(shape, dim):
    return lax.broadcasted_iota(jnp.int32, shape, dim)


def split3(value):
    high = value.astype(BF16)
    rest = value - high.astype(F32)
    mid = rest.astype(BF16)
    low = (rest - mid.astype(F32)).astype(BF16)
    return high, mid, low


def pick(value, onehot):
    high, mid, low = split3(value)
    dot = lambda part: jnp.dot(part, onehot, preferred_element_type=F32)
    return (dot(low) + dot(mid)) + dot(high)


def is_last(axis):
    return lax.axis_index(axis) == lax.axis_size(axis) - 1


def is_even(axis):
    return lax.axis_index(axis) % 2 == 0


def sort_kernel(grains_ref, pairs_ref, own_ref, near_ref):
    flags = {(part, value): jnp.zeros((1, NB), F32) for part in "yz" for value in (0, 2)}
    for n in range(pairs_ref.shape[0]):
        pair = pairs_ref[n]
        hood = jnp.where(pair >= 0, pair, 13 * NB) >> 5
        third = (hood * 11) >> 5
        parts = {"y": third - 3 * ((third * 11) >> 5), "z": hood - 3 * third}
        flags = {k: jnp.where(parts[k[0]] == k[1], 1.0, f) for k, f in flags.items()}

    def upper(part, axis):
        alone = jnp.where(is_last(axis), 1.0 - flags[part, 0], 0.0)
        return jnp.maximum(flags[part, 2], alone)

    group = 64.0 * upper("y", "gy") + 128.0 * upper("z", "gz")
    rows = [grains_ref[r] for r in range(7)]
    centre = 0.5 * (jnp.min(rows[0], axis=1, keepdims=True) + jnp.max(rows[0], axis=1, keepdims=True))
    sub = iota((NB, TILE), 0)
    lane = iota((NB, TILE), 1)
    same = sub == lane
    group = jnp.concatenate([group, jnp.zeros((1, TILE - NB), F32)], axis=1)
    key = centre + jnp.sum(jnp.where(same, group, 0.0), axis=1, keepdims=True)
    wide = jnp.broadcast_to(key, (NB, TILE))
    key_row = jnp.sum(jnp.where(same, wide, 0.0), axis=0, keepdims=True)
    before = (wide < key_row) | ((wide == key_row) & (sub < lane))
    rank = jnp.sum(jnp.where(before, 1.0, 0.0), axis=0, keepdims=True)
    onehot = jnp.where((rank == sub.astype(F32)) & (lane < NB), 1.0, 0.0).astype(BF16)[:, :NB]
    for r in range(7):
        high, mid, low = split3(rows[r])
        dot = lambda part: jnp.dot(onehot, part, preferred_element_type=F32)
        value = (dot(low) + dot(mid)) + dot(high)
        own_ref[r] = value
        if r < 4:
            near_ref[r] = value


def box_sort(grains, pairs):
    shapes = [on_chip((7, NB, TILE)), on_chip((4, NB, TILE))]
    listed = pairs.transpose(0, 1, 2, 4, 3).reshape(pairs.shape[4], 1, NB)
    arrays = (pltpu.with_memory_space_constraint(a, pltpu.HBM) for a in (grains.reshape(7, NB, TILE), listed))
    return plain_call(sort_kernel, shapes, "box_sort", *arrays)


def lane_take(value, index):
    dims = lax.GatherDimensionNumbers(
        offset_dims=(),
        collapsed_slice_dims=(1,),
        start_index_map=(1,),
        operand_batching_dims=(0,),
        start_indices_batching_dims=(0,),
    )
    return lax.gather(
        value, index[..., None], dims, (1, 1), mode=lax.GatherScatterMode.PROMISE_IN_BOUNDS
    )


def pack(groups, tri):
    masks = [jnp.where(mask, 1.0, 0.0).astype(BF16) for lists in groups for mask, _ in lists]
    both = jnp.dot(jnp.concatenate(masks, axis=0), tri, preferred_element_type=F32)
    rows = masks[0].shape[0]
    ranks = both[:, :TILE]
    totals = [both[n * rows : (n + 1) * rows, TILE:] for n in range(len(masks))]
    offsets, ends, at = [], [], 0
    for lists in groups:
        offset = jnp.zeros((rows, TILE), F32)
        for _ in lists:
            offsets.append(offset)
            offset = offset + totals[at]
            at += 1
        ends.append(offset)
    lane_f = iota((rows, TILE), 1).astype(F32)
    wanted = jnp.concatenate([lane_f - offset for offset in offsets], axis=0)
    place = jnp.zeros(wanted.shape, jnp.int32)
    for bit in (64, 32, 16, 8, 4, 2, 1):
        place = jnp.where(lane_take(ranks, place + (bit - 1)) <= wanted, place + bit, place)
    packed, at = [], 0
    for lists, end in zip(groups, ends):
        outs = [jnp.zeros((rows, TILE), F32)] * 3 + [jnp.full((rows, TILE), ABSENT, F32)]
        for _, arrays in lists:
            here = slice(at * rows, (at + 1) * rows)
            ours = (wanted[here] >= 0.0) & (wanted[here] < totals[at])
            outs = [jnp.where(ours, lane_take(v, place[here]), o) for v, o in zip(arrays, outs)]
            at += 1
        packed.append((outs, end))
    return packed


def pair_terms(own, cand, sums):
    own_x, own_y, own_z, own_r = own
    cand_x, cand_y, cand_z, cand_r = cand
    dx, dy, dz = own_x - cand_x, own_y - cand_y, own_z - cand_z
    square = dx * dx + dy * dy + dz * dz
    distance = square * lax.rsqrt(jnp.maximum(square, 1e-30))
    overlap = jnp.maximum(own_r + cand_r - distance, 0.0)
    below = distance + SOFTEN
    guess = pl.reciprocal(below, approx=True)
    force = (0.5 * SPRING) * overlap * (guess * (2.0 - below * guess))
    fx, fy, fz = force * dx, force * dy, force * dz
    terms = (fx * dx, fy * dy, fz * dz, fx * dy, fx * dz, fy * dz)
    return tuple(s + t for s, t in zip(sums, terms))


def weights(coords, centres):
    diff = coords - centres
    return jnp.maximum(jnp.exp(-0.5 * diff * diff) - CUT_LEVEL, 0.0) * NORM_ONE


def centres(places):
    return (places.astype(F32) - CELLS_PER_EDGE + 0.5) * PITCH


def plane_kernel(own_ref, plane_ref):
    nx = CELLS_PER_EDGE * (BOXES_DOWNSLOPE + 2)
    ny = CELLS_PER_EDGE * (BOXES_SPANWISE + 2)

    def put_plane(t):
        wx = weights(own_ref[0, pl.ds(t, 1), :], centres(iota((nx, TILE), 0)))
        wy = weights(own_ref[1, pl.ds(t, 1), :], centres(iota((ny, TILE), 0)))
        parts = [wx[x : x + 1] * wy for x in list(range(4)) + list(range(nx - 4, nx))]
        inner_x = wx[4 : nx - 4]
        parts += [inner_x * wy[y : y + 1] for y in list(range(4)) + list(range(ny - 4, ny))]
        inner_y = wy[4 : ny - 4]
        parts += [wx[x : x + 1] * inner_y for x in range(4, nx - 4)]
        lanes = pl.ds(pl.multiple_of(t * TILE, TILE), TILE)
        plane_ref[:, lanes] = jnp.concatenate(parts, axis=0).astype(BF16)

    def four_planes(q, carry):
        for i in range(4):
            put_plane(4 * q + i)
        return carry

    lax.fori_loop(0, NB // 4, four_planes, 0)


SPAN_X = BOXES_DOWNSLOPE * TILE_BOX_EDGE
SPAN_Y = BOXES_SPANWISE * TILE_BOX_EDGE
SPAN_Z = BOXES_NORMAL * TILE_BOX_EDGE


def running_sums():
    row, col = iota((TILE, 2 * TILE), 0), iota((TILE, 2 * TILE), 1)
    return jnp.where((row <= col) | (col >= TILE), 1.0, 0.0).astype(BF16)


def shifts(place, span):
    return jnp.where(place == 0, -span, jnp.where(place == 3, span, 0.0))


def alive(radius):
    return jnp.where(radius == 0.0, ABSENT, radius)


def near(arrays, axis, low, step):
    limit = arrays[axis] >= low - REACH if step < 0 else arrays[axis] <= low + (TILE_BOX_EDGE + REACH)
    return limit & (arrays[3] > 0.0), arrays


def in_this_frame(grid_ref):
    row = iota((128, TILE), 0)
    return [
        grid_ref[0],
        grid_ref[1] + shifts((row >> 3) & 3, SPAN_Y),
        grid_ref[2] + shifts(row >> 5, SPAN_Z),
        alive(grid_ref[3]),
    ]


def beside_in_this_frame(side_ref):
    row = iota((16, TILE), 0)
    return [
        [
            side_ref[k, 0] + shift_x,
            side_ref[k, 1] + shifts(row & 3, SPAN_Y),
            side_ref[k, 2] + shifts(row >> 2, SPAN_Z),
            alive(side_ref[k, 3]),
        ]
        for k, shift_x in ((0, -SPAN_X), (1, SPAN_X))
    ]


def parts(value):
    return [p.astype(F32) for p in split3(value)]


def keep(ref, first, values):
    for f, value in enumerate(values):
        at = (first + f) * PITCH_ROWS
        ref[at : at + NB, :] = value


def keep_chunks(chunks, feature_ref, moment_ref, own_ref=None):
    half_box = 0.5 * TILE_BOX_EDGE
    ones = jnp.ones((NB, TILE), F32)
    none = jnp.zeros((NB, TILE), F32)
    tile = iota((NB, TILE), 0)
    middle = [
        TILE_BOX_EDGE * (tile & 7).astype(F32) + half_box,
        TILE_BOX_EDGE * ((tile >> 3) & 1).astype(F32) + half_box,
        TILE_BOX_EDGE * (tile >> 4).astype(F32) + half_box,
    ]
    for k, chunk in enumerate(chunks):
        x, y, z = (chunk[c] - middle[c] for c in range(3))
        squares = [x * x, y * y, z * z]
        norm = squares[0] + squares[1] + squares[2]
        xs, ys, zs, ns, rs = (parts(v) for v in (x, y, z, norm, chunk[3]))
        keep(
            feature_ref, 16 * k,
            [xs[0], ys[0], zs[0], xs[1], ys[1], zs[1], ones, ns[0]]
            + [xs[2], ys[2], zs[2], ns[1], ns[2]] + rs,
        )
        products = squares + [x * y, x * z, y * z]
        highs = [v.astype(BF16).astype(F32) for v in products]
        lows = [v - h for v, h in zip(products, highs)]
        keep(moment_ref, 16 * k, highs + [none] * 2 + lows + [none] * 2)
        if own_ref is not None and k == 0:
            xi, yi, zi = ([-2.0 * p for p in v] for v in (xs, ys, zs))
            keep(
                own_ref, 0,
                [xi[0], yi[0], zi[0], xi[0], yi[0], zi[0], ns[0], ones]
                + [xi[0], yi[0], zi[0], ones, ones] + [none] * 3
                + [xi[1], yi[1], zi[1], xi[1], yi[1], zi[1], ns[1], none]
                + [xi[2], yi[2], zi[2], none, none, none, ns[2], none]
                + rs + [x, y, z],
            )


def excess(counts, caps):
    worst = [jnp.max(n, axis=0, keepdims=True) - 8.0 * cap for n, cap in zip(counts, caps)]
    while len(worst) > 1:
        worst = [jnp.maximum(worst[0], worst[1])] + worst[2:]
    return worst[0]


def pick_rows(arrays, starts, size):
    return [jnp.concatenate([v[at : at + size] for at in starts], axis=0) for v in arrays]


def near_kernel(grid_ref, lists_ref, excess_ref, feature_ref, moment_ref, own_ref):
    tri = running_sums()
    here = in_this_frame(grid_ref)
    low_z = TILE_BOX_EDGE * (iota((64, TILE), 0) >> 5).astype(F32)
    low_y = TILE_BOX_EDGE * ((iota((32, TILE), 0) >> 3) & 1).astype(F32)
    cut_z = lambda start: [v[32 * start : 32 * start + 64] for v in here]
    cut_y = lambda arrays, start: pick_rows(arrays, (8 * start, 32 + 8 * start), 16)
    level = cut_z(1)
    ((beside_z, count_z),) = pack([[near(cut_z(0), 2, low_z, -1), near(cut_z(2), 2, low_z, 1)]], tri)
    ((beside_y, count_y),) = pack(
        [
            [
                near(cut_y(level, 0), 1, low_y, -1),
                near(cut_y(beside_z, 0), 1, low_y, -1),
                near(cut_y(level, 2), 1, low_y, 1),
                near(cut_y(beside_z, 2), 1, low_y, 1),
            ]
        ],
        tri,
    )
    excess_ref[...] = excess((count_z, count_y), CAPS[1:3])
    chunks = [cut_y(level, 1), cut_y(beside_z, 1), beside_y]
    for k in range(2):
        for c in range(4):
            lists_ref[4 * k + c] = chunks[1 + k][c]
    keep_chunks(chunks, feature_ref, moment_ref, own_ref)


def find_near(grid):
    table = lambda rows: on_chip((rows * PITCH_ROWS, TILE))
    shapes = [on_chip((8, NB, TILE)), on_chip((1, TILE)), table(3 * 16), table(3 * 16), table(38)]
    return plain_call(near_kernel, shapes, "near", held(grid))


def two_along_z():
    return lax.axis_size("gz") == 2


def field_rows():
    return 80 + (48 if two_along_z() else 80)


def stress_kernel(
    grid_ref, side_ref, grains_ref, plane_ref, lists_ref, excess_ref, feature_near_ref, moment_near_ref, own_ref,
    rim0_ref, rim1_ref, out_ref,
    all_ref, contact_ref, height_ref, feature_far_ref, moment_far_ref, sum_ref, even_ref, odd_ref,
):
    tri = running_sums()
    sides = beside_in_this_frame(side_ref)

    edge = [jnp.concatenate([low, high], axis=0) for low, high in zip(*sides)]
    row = iota((8, TILE), 0)
    low_z = TILE_BOX_EDGE * ((row >> 1) & 1).astype(F32)
    low_y = TILE_BOX_EDGE * (row & 1).astype(F32)

    def around(dz, dy):
        return pick_rows(edge, [16 * s + 4 * (z + 1 + dz) + 1 + dy for s in range(2) for z in range(2)], 2)

    def near_edge(dz, dy):
        arrays = around(dz, dy)
        mask = jnp.where(row < 4, arrays[0], SPAN_X - arrays[0]) >= -REACH
        for axis, low, step in ((2, low_z, dz), (1, low_y, dy)):
            if step:
                mask = mask & near(arrays, axis, low, step)[0]
        return mask & (arrays[3] > 0.0), arrays

    beside_edge = [(dz, dy) for dz in (-1, 0, 1) for dy in (-1, 0, 1) if dz or dy]
    ((edge_z, count_e),) = pack([[near_edge(dz, dy) for dz, dy in beside_edge]], tri)
    edge_own = around(0, 0)
    empty = jnp.zeros((8, TILE), F32)
    edge_y = [empty, empty, empty, empty + ABSENT]

    low_x = TILE_BOX_EDGE * (iota((NB, TILE), 0) & 7).astype(F32)
    in_box_x = iota((4, 8, TILE), 1)

    def along_x(arrays, edges, step):
        found = []
        for value, rim in zip(arrays, edges):
            moved = pltpu.roll(value.reshape(4, 8, TILE), 1 if step < 0 else 7, 1)
            rim = rim[:4] if step < 0 else rim[4:]
            at_edge = in_box_x == (0 if step < 0 else 7)
            found.append(jnp.where(at_edge, rim[:, None, :], moved).reshape(NB, TILE))
        return near(found, 0, low_x, step)

    own = [grains_ref[c * NB : (c + 1) * NB, :] for c in range(4)]
    list_z = [lists_ref[c] for c in range(4)]
    list_y = [lists_ref[4 + c] for c in range(4)]
    (beside, count_x), (beside_rest, count_w) = pack(
        [
            [along_x(own, edge_own, -1), along_x(own, edge_own, 1)],
            [
                along_x(list_z, edge_z, -1),
                along_x(list_y, edge_y, -1),
                along_x(list_z, edge_z, 1),
                along_x(list_y, edge_y, 1),
            ],
        ],
        tri,
    )
    keep_chunks([beside, beside_rest], feature_far_ref, moment_far_ref)
    overflow = jnp.maximum(
        excess_ref[...], excess((count_e, count_x, count_w), (TILE // 8,) + CAPS[3:])
    )
    overflow = jnp.max(overflow)

    def table(near_ref, far_ref, k):
        return (near_ref, k) if k < 3 else (far_ref, k - 3)

    at_z = iota((8, TILE), 0)
    centres_inner = centres(at_z + 4)
    if two_along_z():
        centres_rim = centres((at_z & 3) + jnp.where(lax.axis_index("gz") == 0, 12, 0))
    else:
        centres_rim = centres(jnp.where(at_z < 4, at_z, at_z + 8))

    def put_height(t):
        rows = [grains_ref[pl.ds(r * NB + t, 1), :] for r in range(2, 7)]
        wz_inner = weights(rows[0], centres_inner)
        wz_rim = weights(rows[0], centres_rim)
        masses = 4.0 * math.pi / 3.0 * rows[1] * rows[1] * rows[1]
        vel = rows[2:]
        cont = [contact_ref[pl.ds(k * NB + t, 1), :] for k in range(6)]
        loads = [masses, masses * vel[0], masses * vel[1], masses * vel[2]]
        for k, (i, j) in enumerate(((0, 0), (1, 1), (2, 2), (0, 1), (0, 2), (1, 2))):
            loads.append(cont[k] + masses * (vel[i] * vel[j]))
        height = [load * wz_inner for load in loads]
        if two_along_z():
            height += [jnp.where(at_z < 4, loads[c], loads[c + 1]) * wz_rim for c in range(0, 10, 2)]
            height.append(jnp.zeros((8, TILE), F32))
        else:
            height += [load * wz_rim for load in loads]
        lanes = pl.ds(pl.multiple_of(t * TILE, TILE), TILE)
        height_ref[:, lanes] = jnp.concatenate(height, axis=0).astype(BF16)

    def own_rows(t):
        return tuple(
            jnp.broadcast_to(grains_ref[pl.ds(c * NB + t, 1), :], (8, TILE)) for c in range(4)
        )

    def group(columns, first, g):
        return tuple(
            jnp.broadcast_to(columns[8 * g : 8 * g + 8, first + c : first + c + 1], (8, TILE)) for c in range(4)
        )

    def put(t, sums):
        for k in range(6):
            contact_ref[pl.ds(k * NB + t, 1), :] = jnp.sum(sums[k], axis=0, keepdims=True)

    zeros = tuple(jnp.zeros((8, TILE), F32) for _ in range(6))

    @pl.when(overflow <= 0.0)
    def _():
        sub = iota((8, TILE), 0)
        starts = [8 * sum(CAPS[:k]) for k in range(5)]

        def own_side(t):
            radii = [own_ref[pl.ds((32 + p) * PITCH_ROWS + t, 1), :] for p in range(3)]
            radii = [jnp.where(sub == 6, jnp.broadcast_to(r, (8, TILE)), 0.0) for r in radii]
            reach = [radii[0], jnp.where(sub >= 5, 1.0, 0.0), radii[1], radii[2]]
            return jnp.concatenate(
                [own_ref[pl.ds(t, 32, stride=PITCH_ROWS), :], jnp.concatenate(reach, axis=0)], axis=1
            ).astype(BF16)

        def measure_pairs(t, k, rhs, ref):
            source, n = table(feature_near_ref, feature_far_ref, k)
            rows = source[pl.ds(16 * n * PITCH_ROWS + t, 16, stride=PITCH_ROWS), :]
            first = rows[:8]
            lhs = jnp.concatenate([rows, first, first], axis=0).T.astype(BF16)
            size = 8 * CAPS[k]
            ref[starts[k] : starts[k] + size, :] = jnp.dot(lhs[:size], rhs, preferred_element_type=F32)

        def forces(k, ref):
            size = 8 * CAPS[k]
            square = jnp.maximum(ref[starts[k] : starts[k] + size, :TILE], 1e-12)
            distance = square * lax.rsqrt(square)
            overlap = jnp.maximum(ref[starts[k] : starts[k] + size, TILE:] - distance, 0.0)
            below = distance + SOFTEN
            guess = pl.reciprocal(below, approx=True)
            force = overlap * (guess * (2.0 - below * guess))
            if k == 0:
                at = iota((TILE, TILE), 0) == iota((TILE, TILE), 1)
                force = jnp.where(at, 0.0, force)
            high = force.astype(BF16)
            low = (force - high.astype(F32)).astype(BF16)
            rest = TILE - size
            if rest:
                none = jnp.zeros((rest, TILE), BF16)
                high, low = (jnp.concatenate([v, none], axis=0) for v in (high, low))
            return high, low

        def add_up(t, parts):
            moments = []
            for k in range(5):
                source, n = table(feature_near_ref, feature_far_ref, k)
                first = source[pl.ds(16 * n * PITCH_ROWS + t, 8, stride=PITCH_ROWS), :]
                source, n = table(moment_near_ref, moment_far_ref, k)
                more = source[pl.ds(16 * n * PITCH_ROWS + t, 16, stride=PITCH_ROWS), :]
                moments.append(jnp.concatenate([first, more, first], axis=0))
            lhs = jnp.concatenate(moments, axis=1).astype(BF16)
            highs = jnp.concatenate([p[0] for p in parts], axis=0)
            lows = jnp.concatenate([p[1] for p in parts], axis=0)
            one = jnp.dot(lhs, highs, preferred_element_type=F32)
            two = jnp.dot(lhs[:16], lows, preferred_element_type=F32)
            sum_ref[pl.ds(t, 8, stride=PITCH_ROWS), :] = one[:8] + two[:8]
            sum_ref[pl.ds(8 * PITCH_ROWS + t, 8, stride=PITCH_ROWS), :] = one[8:16] + (one[16:24] + two[8:])

        def step(t, here_ref, next_t, next_ref):
            rhs = own_side(next_t)
            parts = []
            for k in range(5):
                measure_pairs(next_t, k, rhs, next_ref)
                parts.append(forces(k, here_ref))
            add_up(t, parts)

        first_rhs = own_side(0)
        for k in range(5):
            measure_pairs(0, k, first_rhs, even_ref)

        def eight_tiles(q, carry):
            refs = (even_ref, odd_ref)
            for i in range(8):
                t = 8 * q + i
                step(t, refs[i % 2], t + 1 if i < 7 else jnp.minimum(t + 1, NB - 1), refs[1 - i % 2])
            return carry

        lax.fori_loop(0, NB // 8, eight_tiles, 0)
        total = [sum_ref[m * PITCH_ROWS : m * PITCH_ROWS + NB, :] for m in range(14)]
        first = [total[c] + total[3 + c] for c in range(3)]
        own_mid = [own_ref[(35 + c) * PITCH_ROWS : (35 + c) * PITCH_ROWS + NB, :] for c in range(3)]
        for k, (i, j) in enumerate(((0, 0), (1, 1), (2, 2), (0, 1), (0, 2), (1, 2))):
            a, b = own_mid[i], own_mid[j]
            contact_ref[k * NB : (k + 1) * NB, :] = (0.5 * SPRING) * (
                total[8 + k] - (a * first[j] + b * first[i]) + a * b * total[6]
            )

    @pl.when(overflow > 0.0)
    def _():
        stride = 16 * 8 + 32
        here = in_this_frame(grid_ref)
        for c in range(4):
            all_ref[c * stride : c * stride + 128, :] = here[c]
            all_ref[c * stride + 128 : c * stride + 144, :] = sides[0][c]
            all_ref[c * stride + 144 : c * stride + 160, :] = sides[1][c]
        all_ref[4 * stride : 8 * stride, :] = jnp.zeros((4 * stride, TILE), F32)

        def one_tile(t, carry):
            own = own_rows(t)
            tile_x, tile_y, tile_z = t & 7, (t >> 3) & 1, t >> 4

            def one_near(n, sums):
                n_x = n // 9
                n_y = (n - 9 * n_x) // 3
                n_z = n - 9 * n_x - 3 * n_y
                at_x = tile_x + n_x - 1
                plane = 4 * (tile_z + n_z) + tile_y + n_y
                place = jnp.where(
                    at_x < 0, 128 + plane, jnp.where(at_x > 7, 144 + plane, 8 * plane + at_x)
                )
                columns = all_ref[pl.ds(place, 8, stride=stride), :].T
                for g in range(16):
                    sums = pair_terms(own, group(columns, 0, g), sums)
                return sums

            put(t, lax.fori_loop(0, 27, one_near, zeros))
            return carry

        lax.fori_loop(0, NB, one_tile, 0)

    def four_heights(q, carry):
        for i in range(4):
            put_height(4 * q + i)
        return carry

    lax.fori_loop(0, NB // 4, four_heights, 0)
    wide = lax.dot_general(
        height_ref[...], plane_ref[...], (((1,), (1,)), ((), ())), preferred_element_type=F32
    )
    out_ref[...] = wide[:, TILE:]
    rim = wide[:, :TILE]
    rim = jnp.where(is_even("gx"), pltpu.roll(rim, 64, 1), rim)
    half = field_rows() // 2
    upper, lower = rim[:half], rim[half:]
    left_half = iota((half, TILE), 1) < 64
    rim0_ref[...] = jnp.where(left_half, upper, pltpu.roll(lower, 64, 1))
    rim1_ref[...] = jnp.where(left_half, pltpu.roll(upper, 64, 1), lower)


def stress_and_deposit(grid, side, grains, plane, *tables):
    rows = field_rows()
    return plain_call(
        stress_kernel,
        [on_chip((rows // 2, TILE)), on_chip((rows // 2, TILE)), on_chip((rows, 2 * TILE + COLS))],
        "stress_deposit",
        held(grid),
        held(side),
        held(grains),
        held(plane),
        *(held(v) for v in tables),
        scratch=[
            pltpu.VMEM((8 * 160, TILE), F32),
            pltpu.VMEM((6 * NB, TILE), F32),
            pltpu.VMEM((rows, NB * TILE), BF16),
            pltpu.VMEM((2 * 16 * PITCH_ROWS, TILE), F32),
            pltpu.VMEM((2 * 16 * PITCH_ROWS, TILE), F32),
            pltpu.VMEM((16 * PITCH_ROWS, TILE), F32),
            pltpu.VMEM((8 * sum(CAPS), 2 * TILE), F32),
            pltpu.VMEM((8 * sum(CAPS), 2 * TILE), F32),
        ],
    )


def rim_x_kernel(wide_ref, first_ref, second_ref, rim0_ref, rim1_ref, inner_ref):
    even = is_even("gx")
    right = jnp.where(even, first_ref[...], second_ref[...])
    left = jnp.where(even, second_ref[...], first_ref[...])
    left_half = iota(left.shape, 1) < 64
    got = jnp.concatenate(
        [
            jnp.where(left_half, right, pltpu.roll(left, 64, 1)),
            jnp.where(left_half, pltpu.roll(right, 64, 1), left),
        ],
        axis=0,
    )
    src = iota((TILE, 1), 0)
    x = (src >> 4) & 3
    x = jnp.where(src >= 64, x, x + (CELLS_PER_EDGE * BOXES_DOWNSLOPE - 4))
    y = src & 15
    target = jnp.where(y < 4, y * 32 + x, jnp.where(y >= 12, 128 + (y - 12) * 32 + x, 256 + x * 8 + y - 4))
    onehot = jnp.where(iota((TILE, 512), 1) == target, 1.0, 0.0).astype(BF16)
    total = wide_ref[...] + pick(got, onehot)
    low, high = total[:, :TILE], total[:, TILE : 2 * TILE]
    even = is_even("gy")
    rim0_ref[...] = jnp.where(even, high, low)
    rim1_ref[...] = jnp.where(even, low, high)
    inner_ref[...] = total[:, 2 * TILE :]


def add_rim_y(inner_ref, first_ref, second_ref):
    even = is_even("gy")
    right = jnp.where(even, first_ref[...], second_ref[...])
    left = jnp.where(even, second_ref[...], first_ref[...])
    got = jnp.concatenate([left, right], axis=1)
    src = iota((256, 1), 0)
    target = (src & 31) * 8 + 4 * (src >> 7) + ((src >> 5) & 3)
    onehot = jnp.where(iota((256, 256), 1) == target, 1.0, 0.0).astype(BF16)
    return inner_ref[...] + pick(got, onehot)


def rim_y_kernel(inner_ref, first_ref, second_ref, out_ref):
    out_ref[...] = add_rim_y(inner_ref, first_ref, second_ref)


PROFILED = (0, 1, 4, 5, 6, 8)


def rim_y_two_kernel(inner_ref, first_ref, second_ref, out_ref, send_ref):
    total = add_rim_y(inner_ref, first_ref, second_ref)
    out_ref[...] = total
    lower = lax.axis_index("gz") == 0
    send_ref[:40, :] = total[80:120, :TILE]
    send_ref[40:80, :] = total[80:120, TILE:]
    for i, c in enumerate(PROFILED):
        rows = total[8 * c : 8 * c + 8]
        send_ref[80 + 8 * i : 88 + 8 * i, :] = jnp.where(lower, rows[:, TILE:], rows[:, :TILE])


def finish_two_kernel(total_ref, got_ref, fields_ref, fits_ref, inertial_ref):
    lower = lax.axis_index("gz") == 0
    row = iota((8, COLS), 0)
    from_rim = jnp.where(lower, 7 - row, row)
    ours = from_rim < 4
    theirs = from_rim[:, :TILE] >= 4
    fields = []
    for p in range(5):
        got = jnp.concatenate(
            [got_ref[8 * p : 8 * p + 8, :], got_ref[40 + 8 * p : 48 + 8 * p, :]], axis=1
        )
        turned = pltpu.roll(got, 4, 0)
        for i, add in enumerate(
            (jnp.where(lower, turned, got), jnp.where(lower, got, turned))
        ):
            c = 2 * p + i
            fields.append(total_ref[8 * c : 8 * c + 8, :] + jnp.where(ours, add, 0.0))
            fields_ref[0, 0, 0, c] = fields[c]
    column = {}
    for i, c in enumerate(PROFILED):
        mine = jnp.where(lower, fields[c][:, :TILE], fields[c][:, TILE:])
        rim = total_ref[80 + 8 * (c // 2) : 88 + 8 * (c // 2), :]
        rim = jnp.where(lower, rim[:, :TILE], rim[:, TILE:])
        rim = jnp.where(lower == (c % 2 == 0), rim, pltpu.roll(rim, 4, 0))
        other = got_ref[80 + 8 * i : 88 + 8 * i, :] + jnp.where(theirs, rim, 0.0)
        column[c] = jnp.concatenate(
            [jnp.where(lower, mine, other), jnp.where(lower, other, mine)], axis=0
        )
    density = column[0]
    velocity = column[1] / (density + FLOOR_LEVEL)
    press = (column[4] + column[5] + column[6]) / 3.0
    fitted, inertial = column_fit(density, velocity, column[8], press)
    fits_ref[0, 0] = fitted
    inertial_ref[0, 0] = inertial


def held(array):
    return pltpu.with_memory_space_constraint(array, pltpu.VMEM)


def on_chip(shape, dtype=F32):
    return pltpu.VMEM(shape, dtype)


def plain_call(kernel, shapes, name, *args, scratch=()):
    vmem = pl.BlockSpec(memory_space=pltpu.VMEM)
    return pl.pallas_call(
        kernel,
        out_shape=shapes,
        in_specs=[vmem] * len(args),
        out_specs=jax.tree.map(lambda _: vmem, shapes),
        scratch_shapes=scratch,
        compiler_params=pltpu.CompilerParams(vmem_limit_bytes=KERNEL_VMEM),
        name=name,
    )(*args)


def column_fit(density, velocity, shear, press):
    upper = jnp.concatenate([velocity[1:, :], velocity[-1:, :]], axis=0)
    lower = jnp.concatenate([velocity[:1, :], velocity[:-1, :]], axis=0)
    rate = (upper - lower) / (2.0 * PITCH)
    inertial = rate * 1.0 / jnp.sqrt((press + FLOOR_LEVEL) / (density + FLOOR_LEVEL))
    friction = shear / (press + FLOOR_LEVEL)
    weight = density + FLOOR_LEVEL
    add = lambda v: jnp.sum(v, axis=0, keepdims=True)
    sum_zero = add(weight)
    sum_one = add(weight * inertial)
    sum_two = add(weight * inertial * inertial) + RIDGE_SHARE * sum_zero
    mix_zero = add(weight * friction)
    mix_one = add(weight * friction * inertial)
    determ = sum_zero * sum_two - sum_one * sum_one
    fitted = jnp.concatenate(
        [
            (mix_zero * sum_two - sum_one * mix_one) / determ,
            (sum_zero * mix_one - sum_one * mix_zero) / determ,
        ],
        axis=0,
    )
    return fitted, inertial


def swaps(first, second, axis):
    count = lax.axis_size(axis)
    got = []
    for start, value in ((0, first), (1, second)):
        links = []
        for i in range(start, count - 1, 2):
            links += [(i, i + 1), (i + 1, i)]
        got.append(lax.ppermute(value, axis, links) if links else jnp.zeros_like(value))
    return got


def exchange(low, high, axis):
    even = is_even(axis)
    one, two = swaps(jnp.where(even, high, low), jnp.where(even, low, high), axis)
    return jnp.where(even, two, one), jnp.where(even, one, two)


def local(grains, pairs):
    own, near = box_sort(grains, pairs)
    cube = near.reshape(4, 2, 2, 8, TILE)
    below, above = exchange(cube[:, 0], cube[:, 1], "gz")
    cube = jnp.concatenate([below[:, None], cube, above[:, None]], axis=1)
    sends = (cube[:, :, 0], cube[:, :, 1])
    sends, placed = lax.optimization_barrier((sends, own))
    plane = plain_call(
        plane_kernel, on_chip((3 * TILE + COLS, NB * TILE), BF16), "plane", held(placed)
    )
    below, above = exchange(*sends, "gy")
    cube = jnp.concatenate([below[:, :, None], cube, above[:, :, None]], axis=2)
    cube, plane = lax.optimization_barrier((cube, plane))
    sends = (cube[:, :, :, 0], cube[:, :, :, 7])
    sends, placed = lax.optimization_barrier((sends, cube))
    tables = find_near(placed.reshape(4, 128, TILE))
    below, above = exchange(*sends, "gx")
    side = jnp.stack([below, above]).reshape(2, 4, 16, TILE)
    rim0, rim1, wide = stress_and_deposit(cube.reshape(4, 128, TILE), side, own.reshape(7 * NB, TILE), plane, *tables)
    first, second = swaps(rim0, rim1, "gx")
    rows = field_rows()
    block, square = on_chip((rows, TILE)), on_chip((rows, COLS))
    rim0, rim1, inner = plain_call(
        rim_x_kernel, [block, block, square], "rim_x", held(wide), held(first), held(second)
    )
    first, second = swaps(rim0, rim1, "gy")
    if two_along_z():
        sends = on_chip((128, TILE))
        total, send = plain_call(
            rim_y_two_kernel, [square, sends], "rim_y", held(inner), held(first), held(second)
        )
        got, _ = swaps(send, send, "gz")
        outs = [(1, 1, 1, 10, 8, COLS), (1, 1, 2, TILE), (1, 1, 16, TILE)]
        outs = [jax.ShapeDtypeStruct(shape, F32) for shape in outs]
        return tuple(plain_call(finish_two_kernel, outs, "finish", held(total), held(got)))
    total = plain_call(rim_y_kernel, square, "rim_y", held(inner), held(first), held(second))
    fields = total[:80].reshape(10, 8, COLS)
    rim = total[80:].reshape(10, 8, COLS)
    from_below, from_above = exchange(rim[:, :4], rim[:, 4:], "gz")
    fields = fields + jnp.concatenate([from_below, from_above], axis=1)
    share = COLS // lax.axis_size("gz")
    start = lax.axis_index("gz") * share
    density = fields[0]
    velocity = fields[1] / (density + FLOOR_LEVEL)
    shear = fields[8]
    press = (fields[4] + fields[5] + fields[6]) / 3.0
    profile = jnp.stack([density, velocity, shear, press])
    whole = lax.all_gather(profile, "gz", axis=1, tiled=True)
    whole = lax.dynamic_slice_in_dim(whole, start, share, 2)
    fitted, inertial = column_fit(*whole)
    return (fields[None, None, None], fitted[None, None], inertial[None, None])


def solution(mesh):
    in_specs = (P("gx", "gy", "gz", None, None), P("gx", "gy", "gz", None, None))
    out_specs = (
        P("gx", "gy", "gz", None, None, None),
        P("gx", "gy", None, "gz"),
        P("gx", "gy", None, "gz"),
    )
    return jax.shard_map(local, mesh=mesh, in_specs=in_specs, out_specs=out_specs, check_vma=False)
```

```python
import math

import jax
import jax.numpy as jnp
from jax import lax
from jax.experimental import pallas as pl
from jax.experimental.pallas import tpu as pltpu
from jax.sharding import PartitionSpec as P

TILE = 128
BOXES_DOWNSLOPE = 8
BOXES_SPANWISE = 2
BOXES_NORMAL = 2
CELLS_PER_EDGE = 4

TILE_BOX_EDGE = 5.0
SPRING = 2.0
SOFTEN = 0.05
FLOOR_LEVEL = 0.1
RIDGE_SHARE = 0.1
CUT_LEVEL = math.exp(-12.5)
NORM_ONE = 1.0 / math.sqrt(2.0 * math.pi)

PITCH = TILE_BOX_EDGE / CELLS_PER_EDGE
REACH = 1.21
ABSENT = -10.0

NB = BOXES_DOWNSLOPE * BOXES_SPANWISE * BOXES_NORMAL
PITCH_ROWS = NB + 8
COLS = CELLS_PER_EDGE * BOXES_DOWNSLOPE * CELLS_PER_EDGE * BOXES_SPANWISE
CAPS = (16, 12, 16, 12, 14)

KERNEL_VMEM = 32 * 1024 * 1024

F32 = jnp.float32
BF16 = jnp.bfloat16


def iota(shape, dim):
    return lax.broadcasted_iota(jnp.int32, shape, dim)


def split3(value):
    high = value.astype(BF16)
    rest = value - high.astype(F32)
    mid = rest.astype(BF16)
    low = (rest - mid.astype(F32)).astype(BF16)
    return high, mid, low


def pick(value, onehot):
    high, mid, low = split3(value)
    dot = lambda part: jnp.dot(part, onehot, preferred_element_type=F32)
    return (dot(low) + dot(mid)) + dot(high)


def is_last(axis):
    return lax.axis_index(axis) == lax.axis_size(axis) - 1


def is_even(axis):
    return lax.axis_index(axis) % 2 == 0


def sort_kernel(grains_ref, pairs_ref, own_ref, near_ref):
    flags = {(part, value): jnp.zeros((1, NB), F32) for part in "yz" for value in (0, 2)}
    for n in range(pairs_ref.shape[0]):
        pair = pairs_ref[n]
        hood = jnp.where(pair >= 0, pair, 13 * NB) >> 5
        third = (hood * 11) >> 5
        parts = {"y": third - 3 * ((third * 11) >> 5), "z": hood - 3 * third}
        flags = {k: jnp.where(parts[k[0]] == k[1], 1.0, f) for k, f in flags.items()}

    def upper(part, axis):
        alone = jnp.where(is_last(axis), 1.0 - flags[part, 0], 0.0)
        return jnp.maximum(flags[part, 2], alone)

    group = 64.0 * upper("y", "gy") + 128.0 * upper("z", "gz")
    rows = [grains_ref[r] for r in range(7)]
    centre = 0.5 * (jnp.min(rows[0], axis=1, keepdims=True) + jnp.max(rows[0], axis=1, keepdims=True))
    sub = iota((NB, TILE), 0)
    lane = iota((NB, TILE), 1)
    same = sub == lane
    group = jnp.concatenate([group, jnp.zeros((1, TILE - NB), F32)], axis=1)
    key = centre + jnp.sum(jnp.where(same, group, 0.0), axis=1, keepdims=True)
    wide = jnp.broadcast_to(key, (NB, TILE))
    key_row = jnp.sum(jnp.where(same, wide, 0.0), axis=0, keepdims=True)
    before = (wide < key_row) | ((wide == key_row) & (sub < lane))
    rank = jnp.sum(jnp.where(before, 1.0, 0.0), axis=0, keepdims=True)
    onehot = jnp.where((rank == sub.astype(F32)) & (lane < NB), 1.0, 0.0).astype(BF16)[:, :NB]
    for r in range(7):
        high, mid, low = split3(rows[r])
        dot = lambda part: jnp.dot(onehot, part, preferred_element_type=F32)
        value = (dot(low) + dot(mid)) + dot(high)
        own_ref[r] = value
        if r < 4:
            near_ref[r] = value


def box_sort(grains, pairs):
    shapes = [on_chip((7, NB, TILE)), on_chip((4, NB, TILE))]
    listed = pairs.transpose(0, 1, 2, 4, 3).reshape(pairs.shape[4], 1, NB)
    arrays = (pltpu.with_memory_space_constraint(a, pltpu.HBM) for a in (grains.reshape(7, NB, TILE), listed))
    return plain_call(sort_kernel, shapes, "box_sort", *arrays)


def lane_take(value, index):
    dims = lax.GatherDimensionNumbers(
        offset_dims=(),
        collapsed_slice_dims=(1,),
        start_index_map=(1,),
        operand_batching_dims=(0,),
        start_indices_batching_dims=(0,),
    )
    return lax.gather(
        value, index[..., None], dims, (1, 1), mode=lax.GatherScatterMode.PROMISE_IN_BOUNDS
    )


def pack(groups, tri):
    masks = [jnp.where(mask, 1.0, 0.0).astype(BF16) for lists in groups for mask, _ in lists]
    both = jnp.dot(jnp.concatenate(masks, axis=0), tri, preferred_element_type=F32)
    rows = masks[0].shape[0]
    ranks = both[:, :TILE]
    totals = [both[n * rows : (n + 1) * rows, TILE:] for n in range(len(masks))]
    offsets, ends, at = [], [], 0
    for lists in groups:
        offset = jnp.zeros((rows, TILE), F32)
        for _ in lists:
            offsets.append(offset)
            offset = offset + totals[at]
            at += 1
        ends.append(offset)
    lane_f = iota((rows, TILE), 1).astype(F32)
    wanted = jnp.concatenate([lane_f - offset for offset in offsets], axis=0)
    place = jnp.zeros(wanted.shape, jnp.int32)
    for bit in (64, 32, 16, 8, 4, 2, 1):
        place = jnp.where(lane_take(ranks, place + (bit - 1)) <= wanted, place + bit, place)
    packed, at = [], 0
    for lists, end in zip(groups, ends):
        outs = [jnp.zeros((rows, TILE), F32)] * 3 + [jnp.full((rows, TILE), ABSENT, F32)]
        for _, arrays in lists:
            here = slice(at * rows, (at + 1) * rows)
            ours = (wanted[here] >= 0.0) & (wanted[here] < totals[at])
            outs = [jnp.where(ours, lane_take(v, place[here]), o) for v, o in zip(arrays, outs)]
            at += 1
        packed.append((outs, end))
    return packed


def pair_terms(own, cand, sums):
    own_x, own_y, own_z, own_r = own
    cand_x, cand_y, cand_z, cand_r = cand
    dx, dy, dz = own_x - cand_x, own_y - cand_y, own_z - cand_z
    square = dx * dx + dy * dy + dz * dz
    distance = square * lax.rsqrt(jnp.maximum(square, 1e-30))
    overlap = jnp.maximum(own_r + cand_r - distance, 0.0)
    below = distance + SOFTEN
    guess = pl.reciprocal(below, approx=True)
    force = (0.5 * SPRING) * overlap * (guess * (2.0 - below * guess))
    fx, fy, fz = force * dx, force * dy, force * dz
    terms = (fx * dx, fy * dy, fz * dz, fx * dy, fx * dz, fy * dz)
    return tuple(s + t for s, t in zip(sums, terms))


def weights(coords, centres):
    diff = coords - centres
    return jnp.maximum(jnp.exp(-0.5 * diff * diff) - CUT_LEVEL, 0.0) * NORM_ONE


def centres(places):
    return (places.astype(F32) - CELLS_PER_EDGE + 0.5) * PITCH


def plane_kernel(own_ref, plane_ref):
    nx = CELLS_PER_EDGE * (BOXES_DOWNSLOPE + 2)
    ny = CELLS_PER_EDGE * (BOXES_SPANWISE + 2)

    def put_plane(t):
        wx = weights(own_ref[0, pl.ds(t, 1), :], centres(iota((nx, TILE), 0)))
        wy = weights(own_ref[1, pl.ds(t, 1), :], centres(iota((ny, TILE), 0)))
        parts = [wx[x : x + 1] * wy for x in list(range(4)) + list(range(nx - 4, nx))]
        inner_x = wx[4 : nx - 4]
        parts += [inner_x * wy[y : y + 1] for y in list(range(4)) + list(range(ny - 4, ny))]
        inner_y = wy[4 : ny - 4]
        parts += [wx[x : x + 1] * inner_y for x in range(4, nx - 4)]
        lanes = pl.ds(pl.multiple_of(t * TILE, TILE), TILE)
        plane_ref[:, lanes] = jnp.concatenate(parts, axis=0).astype(BF16)

    def four_planes(q, carry):
        for i in range(4):
            put_plane(4 * q + i)
        return carry

    lax.fori_loop(0, NB // 4, four_planes, 0)


SPAN_X = BOXES_DOWNSLOPE * TILE_BOX_EDGE
SPAN_Y = BOXES_SPANWISE * TILE_BOX_EDGE
SPAN_Z = BOXES_NORMAL * TILE_BOX_EDGE


def running_sums():
    row, col = iota((TILE, 2 * TILE), 0), iota((TILE, 2 * TILE), 1)
    return jnp.where((row <= col) | (col >= TILE), 1.0, 0.0).astype(BF16)


def shifts(place, span):
    return jnp.where(place == 0, -span, jnp.where(place == 3, span, 0.0))


def alive(radius):
    return jnp.where(radius == 0.0, ABSENT, radius)


def near(arrays, axis, low, step):
    limit = arrays[axis] >= low - REACH if step < 0 else arrays[axis] <= low + (TILE_BOX_EDGE + REACH)
    return limit & (arrays[3] > 0.0), arrays


def in_this_frame(grid_ref):
    row = iota((128, TILE), 0)
    return [
        grid_ref[0],
        grid_ref[1] + shifts((row >> 3) & 3, SPAN_Y),
        grid_ref[2] + shifts(row >> 5, SPAN_Z),
        alive(grid_ref[3]),
    ]


def beside_in_this_frame(side_ref):
    row = iota((16, TILE), 0)
    return [
        [
            side_ref[k, 0] + shift_x,
            side_ref[k, 1] + shifts(row & 3, SPAN_Y),
            side_ref[k, 2] + shifts(row >> 2, SPAN_Z),
            alive(side_ref[k, 3]),
        ]
        for k, shift_x in ((0, -SPAN_X), (1, SPAN_X))
    ]


def parts(value):
    return [p.astype(F32) for p in split3(value)]


def keep(ref, first, values):
    for f, value in enumerate(values):
        at = (first + f) * PITCH_ROWS
        ref[at : at + NB, :] = value


def keep_chunks(chunks, feature_ref, moment_ref, own_ref=None):
    half_box = 0.5 * TILE_BOX_EDGE
    ones = jnp.ones((NB, TILE), F32)
    none = jnp.zeros((NB, TILE), F32)
    tile = iota((NB, TILE), 0)
    middle = [
        TILE_BOX_EDGE * (tile & 7).astype(F32) + half_box,
        TILE_BOX_EDGE * ((tile >> 3) & 1).astype(F32) + half_box,
        TILE_BOX_EDGE * (tile >> 4).astype(F32) + half_box,
    ]
    for k, chunk in enumerate(chunks):
        x, y, z = (chunk[c] - middle[c] for c in range(3))
        squares = [x * x, y * y, z * z]
        norm = squares[0] + squares[1] + squares[2]
        xs, ys, zs, ns, rs = (parts(v) for v in (x, y, z, norm, chunk[3]))
        keep(
            feature_ref, 16 * k,
            [xs[0], ys[0], zs[0], xs[1], ys[1], zs[1], ones, ns[0]]
            + [xs[2], ys[2], zs[2], ns[1], ns[2]] + rs,
        )
        products = squares + [x * y, x * z, y * z]
        highs = [v.astype(BF16).astype(F32) for v in products]
        lows = [v - h for v, h in zip(products, highs)]
        keep(moment_ref, 16 * k, highs + [none] * 2 + lows + [none] * 2)
        if own_ref is not None and k == 0:
            xi, yi, zi = ([-2.0 * p for p in v] for v in (xs, ys, zs))
            keep(
                own_ref, 0,
                [xi[0], yi[0], zi[0], xi[0], yi[0], zi[0], ns[0], ones]
                + [xi[0], yi[0], zi[0], ones, ones] + [none] * 3
                + [xi[1], yi[1], zi[1], xi[1], yi[1], zi[1], ns[1], none]
                + [xi[2], yi[2], zi[2], none, none, none, ns[2], none]
                + rs + [x, y, z],
            )


def excess(counts, caps):
    worst = [jnp.max(n, axis=0, keepdims=True) - 8.0 * cap for n, cap in zip(counts, caps)]
    while len(worst) > 1:
        worst = [jnp.maximum(worst[0], worst[1])] + worst[2:]
    return worst[0]


def pick_rows(arrays, starts, size):
    return [jnp.concatenate([v[at : at + size] for at in starts], axis=0) for v in arrays]


def pair_loop(chunks, first_chunk, own_ref, sum_ref, even_ref, odd_ref):
    caps = CAPS[first_chunk : first_chunk + len(chunks)]
    starts = [8 * sum(caps[:k]) for k in range(len(caps))]
    sub = iota((8, TILE), 0)

    def own_side(t):
        radii = [own_ref[pl.ds((32 + p) * PITCH_ROWS + t, 1), :] for p in range(3)]
        radii = [jnp.where(sub == 6, jnp.broadcast_to(r, (8, TILE)), 0.0) for r in radii]
        reach = [radii[0], jnp.where(sub >= 5, 1.0, 0.0), radii[1], radii[2]]
        return jnp.concatenate(
            [own_ref[pl.ds(t, 32, stride=PITCH_ROWS), :], jnp.concatenate(reach, axis=0)], axis=1
        ).astype(BF16)

    def measure_pairs(t, k, rhs, ref):
        source, _, n = chunks[k]
        rows = source[pl.ds(16 * n * PITCH_ROWS + t, 16, stride=PITCH_ROWS), :]
        first = rows[:8]
        lhs = jnp.concatenate([rows, first, first], axis=0).T.astype(BF16)
        size = 8 * caps[k]
        ref[starts[k] : starts[k] + size, :] = jnp.dot(lhs[:size], rhs, preferred_element_type=F32)

    def forces(k, ref):
        size = 8 * caps[k]
        square = jnp.maximum(ref[starts[k] : starts[k] + size, :TILE], 1e-12)
        distance = square * lax.rsqrt(square)
        overlap = jnp.maximum(ref[starts[k] : starts[k] + size, TILE:] - distance, 0.0)
        below = distance + SOFTEN
        guess = pl.reciprocal(below, approx=True)
        force = overlap * (guess * (2.0 - below * guess))
        if first_chunk + k == 0:
            at = iota((TILE, TILE), 0) == iota((TILE, TILE), 1)
            force = jnp.where(at, 0.0, force)
        high = force.astype(BF16)
        low = (force - high.astype(F32)).astype(BF16)
        rest = TILE - size
        if rest:
            none = jnp.zeros((rest, TILE), BF16)
            high, low = (jnp.concatenate([v, none], axis=0) for v in (high, low))
        return high, low

    def add_up(t, found):
        moments = []
        for features, products, n in chunks:
            first = features[pl.ds(16 * n * PITCH_ROWS + t, 8, stride=PITCH_ROWS), :]
            more = products[pl.ds(16 * n * PITCH_ROWS + t, 16, stride=PITCH_ROWS), :]
            moments.append(jnp.concatenate([first, more, first], axis=0))
        lhs = jnp.concatenate(moments, axis=1).astype(BF16)
        highs = jnp.concatenate([p[0] for p in found], axis=0)
        lows = jnp.concatenate([p[1] for p in found], axis=0)
        one = jnp.dot(lhs, highs, preferred_element_type=F32)
        two = jnp.dot(lhs[:16], lows, preferred_element_type=F32)
        sum_ref[pl.ds(t, 8, stride=PITCH_ROWS), :] = one[:8] + two[:8]
        sum_ref[pl.ds(8 * PITCH_ROWS + t, 8, stride=PITCH_ROWS), :] = one[8:16] + (one[16:24] + two[8:])

    def step(t, here_ref, next_t, next_ref):
        rhs = own_side(next_t)
        found = []
        for k in range(len(chunks)):
            measure_pairs(next_t, k, rhs, next_ref)
            found.append(forces(k, here_ref))
        add_up(t, found)

    first_rhs = own_side(0)
    for k in range(len(chunks)):
        measure_pairs(0, k, first_rhs, even_ref)

    def eight_tiles(q, carry):
        refs = (even_ref, odd_ref)
        for i in range(8):
            t = 8 * q + i
            step(t, refs[i % 2], t + 1 if i < 7 else jnp.minimum(t + 1, NB - 1), refs[1 - i % 2])
        return carry

    lax.fori_loop(0, NB // 8, eight_tiles, 0)


def table(rows):
    return on_chip((rows * PITCH_ROWS, TILE))


def pair_space(chunks, groups):
    return [table(16 * chunks), table(16 * chunks)] + [pltpu.VMEM((8 * groups, 2 * TILE), F32)] * 2


def own_kernel(grains_ref, own_ref, sum_ref, feature_ref, moment_ref, even_ref, odd_ref):
    keep_chunks([[grains_ref[c] for c in range(4)]], feature_ref, moment_ref, own_ref)
    pair_loop([(feature_ref, moment_ref, 0)], 0, own_ref, sum_ref, even_ref, odd_ref)


def pair_own(grains):
    return plain_call(own_kernel, [table(38), table(16)], "own", held(grains), scratch=pair_space(1, CAPS[0]))


def near_kernel(grid_ref, lists_ref, excess_ref, feature_ref, moment_ref):
    tri = running_sums()
    here = in_this_frame(grid_ref)
    low_z = TILE_BOX_EDGE * (iota((64, TILE), 0) >> 5).astype(F32)
    low_y = TILE_BOX_EDGE * ((iota((32, TILE), 0) >> 3) & 1).astype(F32)
    cut_z = lambda start: [v[32 * start : 32 * start + 64] for v in here]
    cut_y = lambda arrays, start: pick_rows(arrays, (8 * start, 32 + 8 * start), 16)
    level = cut_z(1)
    ((beside_z, count_z),) = pack([[near(cut_z(0), 2, low_z, -1), near(cut_z(2), 2, low_z, 1)]], tri)
    ((beside_y, count_y),) = pack(
        [
            [
                near(cut_y(level, 0), 1, low_y, -1),
                near(cut_y(beside_z, 0), 1, low_y, -1),
                near(cut_y(level, 2), 1, low_y, 1),
                near(cut_y(beside_z, 2), 1, low_y, 1),
            ]
        ],
        tri,
    )
    excess_ref[...] = excess((count_z, count_y), CAPS[1:3])
    chunks = [cut_y(beside_z, 1), beside_y]
    for k in range(2):
        for c in range(4):
            lists_ref[4 * k + c] = chunks[k][c]
    keep_chunks(chunks, feature_ref, moment_ref)


def find_near(grid):
    shapes = [on_chip((8, NB, TILE)), on_chip((1, TILE)), table(2 * 16), table(2 * 16)]
    return plain_call(near_kernel, shapes, "near", held(grid))


def two_along_z():
    return lax.axis_size("gz") == 2


def field_rows():
    return 80 + (48 if two_along_z() else 80)


def stress_kernel(
    grid_ref, side_ref, grains_ref, plane_ref, own_ref, own_sum_ref,
    lists_ref, excess_ref, feature_near_ref, moment_near_ref,
    rim0_ref, rim1_ref, out_ref,
    all_ref, contact_ref, height_ref, feature_far_ref, moment_far_ref, sum_ref, even_ref, odd_ref,
):
    tri = running_sums()
    sides = beside_in_this_frame(side_ref)

    edge = [jnp.concatenate([low, high], axis=0) for low, high in zip(*sides)]
    row = iota((8, TILE), 0)
    low_z = TILE_BOX_EDGE * ((row >> 1) & 1).astype(F32)
    low_y = TILE_BOX_EDGE * (row & 1).astype(F32)

    def around(dz, dy):
        return pick_rows(edge, [16 * s + 4 * (z + 1 + dz) + 1 + dy for s in range(2) for z in range(2)], 2)

    def near_edge(dz, dy):
        arrays = around(dz, dy)
        mask = jnp.where(row < 4, arrays[0], SPAN_X - arrays[0]) >= -REACH
        for axis, low, step in ((2, low_z, dz), (1, low_y, dy)):
            if step:
                mask = mask & near(arrays, axis, low, step)[0]
        return mask & (arrays[3] > 0.0), arrays

    beside_edge = [(dz, dy) for dz in (-1, 0, 1) for dy in (-1, 0, 1) if dz or dy]
    ((edge_z, count_e),) = pack([[near_edge(dz, dy) for dz, dy in beside_edge]], tri)
    edge_own = around(0, 0)
    empty = jnp.zeros((8, TILE), F32)
    edge_y = [empty, empty, empty, empty + ABSENT]

    low_x = TILE_BOX_EDGE * (iota((NB, TILE), 0) & 7).astype(F32)
    in_box_x = iota((4, 8, TILE), 1)

    def along_x(arrays, edges, step):
        found = []
        for value, rim in zip(arrays, edges):
            moved = pltpu.roll(value.reshape(4, 8, TILE), 1 if step < 0 else 7, 1)
            rim = rim[:4] if step < 0 else rim[4:]
            at_edge = in_box_x == (0 if step < 0 else 7)
            found.append(jnp.where(at_edge, rim[:, None, :], moved).reshape(NB, TILE))
        return near(found, 0, low_x, step)

    own = [grains_ref[c * NB : (c + 1) * NB, :] for c in range(4)]
    list_z = [lists_ref[c] for c in range(4)]
    list_y = [lists_ref[4 + c] for c in range(4)]
    (beside, count_x), (beside_rest, count_w) = pack(
        [
            [along_x(own, edge_own, -1), along_x(own, edge_own, 1)],
            [
                along_x(list_z, edge_z, -1),
                along_x(list_y, edge_y, -1),
                along_x(list_z, edge_z, 1),
                along_x(list_y, edge_y, 1),
            ],
        ],
        tri,
    )
    keep_chunks([beside, beside_rest], feature_far_ref, moment_far_ref)
    overflow = jnp.maximum(
        excess_ref[...], excess((count_e, count_x, count_w), (TILE // 8,) + CAPS[3:])
    )
    overflow = jnp.max(overflow)

    at_z = iota((8, TILE), 0)
    centres_inner = centres(at_z + 4)
    if two_along_z():
        centres_rim = centres((at_z & 3) + jnp.where(lax.axis_index("gz") == 0, 12, 0))
    else:
        centres_rim = centres(jnp.where(at_z < 4, at_z, at_z + 8))

    def put_height(t):
        rows = [grains_ref[pl.ds(r * NB + t, 1), :] for r in range(2, 7)]
        wz_inner = weights(rows[0], centres_inner)
        wz_rim = weights(rows[0], centres_rim)
        masses = 4.0 * math.pi / 3.0 * rows[1] * rows[1] * rows[1]
        vel = rows[2:]
        cont = [contact_ref[pl.ds(k * NB + t, 1), :] for k in range(6)]
        loads = [masses, masses * vel[0], masses * vel[1], masses * vel[2]]
        for k, (i, j) in enumerate(((0, 0), (1, 1), (2, 2), (0, 1), (0, 2), (1, 2))):
            loads.append(cont[k] + masses * (vel[i] * vel[j]))
        height = [load * wz_inner for load in loads]
        if two_along_z():
            height += [jnp.where(at_z < 4, loads[c], loads[c + 1]) * wz_rim for c in range(0, 10, 2)]
            height.append(jnp.zeros((8, TILE), F32))
        else:
            height += [load * wz_rim for load in loads]
        lanes = pl.ds(pl.multiple_of(t * TILE, TILE), TILE)
        height_ref[:, lanes] = jnp.concatenate(height, axis=0).astype(BF16)

    def own_rows(t):
        return tuple(
            jnp.broadcast_to(grains_ref[pl.ds(c * NB + t, 1), :], (8, TILE)) for c in range(4)
        )

    def group(columns, first, g):
        return tuple(
            jnp.broadcast_to(columns[8 * g : 8 * g + 8, first + c : first + c + 1], (8, TILE)) for c in range(4)
        )

    def put(t, sums):
        for k in range(6):
            contact_ref[pl.ds(k * NB + t, 1), :] = jnp.sum(sums[k], axis=0, keepdims=True)

    zeros = tuple(jnp.zeros((8, TILE), F32) for _ in range(6))

    @pl.when(overflow <= 0.0)
    def _():
        tables = [(feature_near_ref, moment_near_ref, k) for k in range(2)]
        tables += [(feature_far_ref, moment_far_ref, k) for k in range(2)]
        pair_loop(tables, 1, own_ref, sum_ref, even_ref, odd_ref)
        rows = lambda ref, m: ref[m * PITCH_ROWS : m * PITCH_ROWS + NB, :]
        total = [rows(sum_ref, m) + rows(own_sum_ref, m) for m in range(14)]
        first = [total[c] + total[3 + c] for c in range(3)]
        own_mid = [own_ref[(35 + c) * PITCH_ROWS : (35 + c) * PITCH_ROWS + NB, :] for c in range(3)]
        for k, (i, j) in enumerate(((0, 0), (1, 1), (2, 2), (0, 1), (0, 2), (1, 2))):
            a, b = own_mid[i], own_mid[j]
            contact_ref[k * NB : (k + 1) * NB, :] = (0.5 * SPRING) * (
                total[8 + k] - (a * first[j] + b * first[i]) + a * b * total[6]
            )

    @pl.when(overflow > 0.0)
    def _():
        stride = 16 * 8 + 32
        here = in_this_frame(grid_ref)
        for c in range(4):
            all_ref[c * stride : c * stride + 128, :] = here[c]
            all_ref[c * stride + 128 : c * stride + 144, :] = sides[0][c]
            all_ref[c * stride + 144 : c * stride + 160, :] = sides[1][c]
        all_ref[4 * stride : 8 * stride, :] = jnp.zeros((4 * stride, TILE), F32)

        def one_tile(t, carry):
            own = own_rows(t)
            tile_x, tile_y, tile_z = t & 7, (t >> 3) & 1, t >> 4

            def one_near(n, sums):
                n_x = n // 9
                n_y = (n - 9 * n_x) // 3
                n_z = n - 9 * n_x - 3 * n_y
                at_x = tile_x + n_x - 1
                plane = 4 * (tile_z + n_z) + tile_y + n_y
                place = jnp.where(
                    at_x < 0, 128 + plane, jnp.where(at_x > 7, 144 + plane, 8 * plane + at_x)
                )
                columns = all_ref[pl.ds(place, 8, stride=stride), :].T
                for g in range(16):
                    sums = pair_terms(own, group(columns, 0, g), sums)
                return sums

            put(t, lax.fori_loop(0, 27, one_near, zeros))
            return carry

        lax.fori_loop(0, NB, one_tile, 0)

    def four_heights(q, carry):
        for i in range(4):
            put_height(4 * q + i)
        return carry

    lax.fori_loop(0, NB // 4, four_heights, 0)
    wide = lax.dot_general(
        height_ref[...], plane_ref[...], (((1,), (1,)), ((), ())), preferred_element_type=F32
    )
    out_ref[...] = wide[:, TILE:]
    rim = wide[:, :TILE]
    rim = jnp.where(is_even("gx"), pltpu.roll(rim, 64, 1), rim)
    half = field_rows() // 2
    upper, lower = rim[:half], rim[half:]
    left_half = iota((half, TILE), 1) < 64
    rim0_ref[...] = jnp.where(left_half, upper, pltpu.roll(lower, 64, 1))
    rim1_ref[...] = jnp.where(left_half, pltpu.roll(upper, 64, 1), lower)


def stress_and_deposit(grid, side, grains, plane, *tables):
    rows = field_rows()
    return plain_call(
        stress_kernel,
        [on_chip((rows // 2, TILE)), on_chip((rows // 2, TILE)), on_chip((rows, 2 * TILE + COLS))],
        "stress_deposit",
        held(grid),
        held(side),
        held(grains),
        held(plane),
        *(held(v) for v in tables),
        scratch=[
            pltpu.VMEM((8 * 160, TILE), F32),
            pltpu.VMEM((6 * NB, TILE), F32),
            pltpu.VMEM((rows, NB * TILE), BF16),
            pltpu.VMEM((2 * 16 * PITCH_ROWS, TILE), F32),
            pltpu.VMEM((2 * 16 * PITCH_ROWS, TILE), F32),
            pltpu.VMEM((16 * PITCH_ROWS, TILE), F32),
            pltpu.VMEM((8 * sum(CAPS[1:]), 2 * TILE), F32),
            pltpu.VMEM((8 * sum(CAPS[1:]), 2 * TILE), F32),
        ],
    )


def rim_x_kernel(wide_ref, first_ref, second_ref, rim0_ref, rim1_ref, inner_ref):
    even = is_even("gx")
    right = jnp.where(even, first_ref[...], second_ref[...])
    left = jnp.where(even, second_ref[...], first_ref[...])
    left_half = iota(left.shape, 1) < 64
    got = jnp.concatenate(
        [
            jnp.where(left_half, right, pltpu.roll(left, 64, 1)),
            jnp.where(left_half, pltpu.roll(right, 64, 1), left),
        ],
        axis=0,
    )
    src = iota((TILE, 1), 0)
    x = (src >> 4) & 3
    x = jnp.where(src >= 64, x, x + (CELLS_PER_EDGE * BOXES_DOWNSLOPE - 4))
    y = src & 15
    target = jnp.where(y < 4, y * 32 + x, jnp.where(y >= 12, 128 + (y - 12) * 32 + x, 256 + x * 8 + y - 4))
    onehot = jnp.where(iota((TILE, 512), 1) == target, 1.0, 0.0).astype(BF16)
    total = wide_ref[...] + pick(got, onehot)
    low, high = total[:, :TILE], total[:, TILE : 2 * TILE]
    even = is_even("gy")
    rim0_ref[...] = jnp.where(even, high, low)
    rim1_ref[...] = jnp.where(even, low, high)
    inner_ref[...] = total[:, 2 * TILE :]


def add_rim_y(inner_ref, first_ref, second_ref):
    even = is_even("gy")
    right = jnp.where(even, first_ref[...], second_ref[...])
    left = jnp.where(even, second_ref[...], first_ref[...])
    got = jnp.concatenate([left, right], axis=1)
    src = iota((256, 1), 0)
    target = (src & 31) * 8 + 4 * (src >> 7) + ((src >> 5) & 3)
    onehot = jnp.where(iota((256, 256), 1) == target, 1.0, 0.0).astype(BF16)
    return inner_ref[...] + pick(got, onehot)


def rim_y_kernel(inner_ref, first_ref, second_ref, out_ref):
    out_ref[...] = add_rim_y(inner_ref, first_ref, second_ref)


PROFILED = (0, 1, 4, 5, 6, 8)


def rim_y_two_kernel(inner_ref, first_ref, second_ref, out_ref, send_ref):
    total = add_rim_y(inner_ref, first_ref, second_ref)
    out_ref[...] = total
    lower = lax.axis_index("gz") == 0
    send_ref[:40, :] = total[80:120, :TILE]
    send_ref[40:80, :] = total[80:120, TILE:]
    for i, c in enumerate(PROFILED):
        rows = total[8 * c : 8 * c + 8]
        send_ref[80 + 8 * i : 88 + 8 * i, :] = jnp.where(lower, rows[:, TILE:], rows[:, :TILE])


def finish_two_kernel(total_ref, got_ref, fields_ref, fits_ref, inertial_ref):
    lower = lax.axis_index("gz") == 0
    row = iota((8, COLS), 0)
    from_rim = jnp.where(lower, 7 - row, row)
    ours = from_rim < 4
    theirs = from_rim[:, :TILE] >= 4
    fields = []
    for p in range(5):
        got = jnp.concatenate(
            [got_ref[8 * p : 8 * p + 8, :], got_ref[40 + 8 * p : 48 + 8 * p, :]], axis=1
        )
        turned = pltpu.roll(got, 4, 0)
        for i, add in enumerate(
            (jnp.where(lower, turned, got), jnp.where(lower, got, turned))
        ):
            c = 2 * p + i
            fields.append(total_ref[8 * c : 8 * c + 8, :] + jnp.where(ours, add, 0.0))
            fields_ref[0, 0, 0, c] = fields[c]
    column = {}
    for i, c in enumerate(PROFILED):
        mine = jnp.where(lower, fields[c][:, :TILE], fields[c][:, TILE:])
        rim = total_ref[80 + 8 * (c // 2) : 88 + 8 * (c // 2), :]
        rim = jnp.where(lower, rim[:, :TILE], rim[:, TILE:])
        rim = jnp.where(lower == (c % 2 == 0), rim, pltpu.roll(rim, 4, 0))
        other = got_ref[80 + 8 * i : 88 + 8 * i, :] + jnp.where(theirs, rim, 0.0)
        column[c] = jnp.concatenate(
            [jnp.where(lower, mine, other), jnp.where(lower, other, mine)], axis=0
        )
    density = column[0]
    velocity = column[1] / (density + FLOOR_LEVEL)
    press = (column[4] + column[5] + column[6]) / 3.0
    fitted, inertial = column_fit(density, velocity, column[8], press)
    fits_ref[0, 0] = fitted
    inertial_ref[0, 0] = inertial


def held(array):
    return pltpu.with_memory_space_constraint(array, pltpu.VMEM)


def on_chip(shape, dtype=F32):
    return pltpu.VMEM(shape, dtype)


def plain_call(kernel, shapes, name, *args, scratch=()):
    vmem = pl.BlockSpec(memory_space=pltpu.VMEM)
    return pl.pallas_call(
        kernel,
        out_shape=shapes,
        in_specs=[vmem] * len(args),
        out_specs=jax.tree.map(lambda _: vmem, shapes),
        scratch_shapes=scratch,
        compiler_params=pltpu.CompilerParams(vmem_limit_bytes=KERNEL_VMEM),
        name=name,
    )(*args)


def column_fit(density, velocity, shear, press):
    upper = jnp.concatenate([velocity[1:, :], velocity[-1:, :]], axis=0)
    lower = jnp.concatenate([velocity[:1, :], velocity[:-1, :]], axis=0)
    rate = (upper - lower) / (2.0 * PITCH)
    inertial = rate * 1.0 / jnp.sqrt((press + FLOOR_LEVEL) / (density + FLOOR_LEVEL))
    friction = shear / (press + FLOOR_LEVEL)
    weight = density + FLOOR_LEVEL
    add = lambda v: jnp.sum(v, axis=0, keepdims=True)
    sum_zero = add(weight)
    sum_one = add(weight * inertial)
    sum_two = add(weight * inertial * inertial) + RIDGE_SHARE * sum_zero
    mix_zero = add(weight * friction)
    mix_one = add(weight * friction * inertial)
    determ = sum_zero * sum_two - sum_one * sum_one
    fitted = jnp.concatenate(
        [
            (mix_zero * sum_two - sum_one * mix_one) / determ,
            (sum_zero * mix_one - sum_one * mix_zero) / determ,
        ],
        axis=0,
    )
    return fitted, inertial


def swaps(first, second, axis):
    count = lax.axis_size(axis)
    got = []
    for start, value in ((0, first), (1, second)):
        links = []
        for i in range(start, count - 1, 2):
            links += [(i, i + 1), (i + 1, i)]
        got.append(lax.ppermute(value, axis, links) if links else jnp.zeros_like(value))
    return got


def exchange(low, high, axis):
    even = is_even(axis)
    one, two = swaps(jnp.where(even, high, low), jnp.where(even, low, high), axis)
    return jnp.where(even, two, one), jnp.where(even, one, two)


def local(grains, pairs):
    own, near = box_sort(grains, pairs)
    cube = near.reshape(4, 2, 2, 8, TILE)
    sends, placed = lax.optimization_barrier(((cube[:, 0], cube[:, 1]), own))
    own_table, own_sums = pair_own(placed)
    below, above = exchange(*sends, "gz")
    cube = jnp.concatenate([below[:, None], cube, above[:, None]], axis=1)
    sends = (cube[:, :, 0], cube[:, :, 1])
    sends, placed, own_table, own_sums = lax.optimization_barrier((sends, own, own_table, own_sums))
    plane = plain_call(
        plane_kernel, on_chip((3 * TILE + COLS, NB * TILE), BF16), "plane", held(placed)
    )
    below, above = exchange(*sends, "gy")
    cube = jnp.concatenate([below[:, :, None], cube, above[:, :, None]], axis=2)
    cube, plane = lax.optimization_barrier((cube, plane))
    sends = (cube[:, :, :, 0], cube[:, :, :, 7])
    sends, placed = lax.optimization_barrier((sends, cube))
    tables = find_near(placed.reshape(4, 128, TILE))
    below, above = exchange(*sends, "gx")
    side = jnp.stack([below, above]).reshape(2, 4, 16, TILE)
    rim0, rim1, wide = stress_and_deposit(
        cube.reshape(4, 128, TILE), side, own.reshape(7 * NB, TILE), plane, own_table, own_sums, *tables
    )
    first, second = swaps(rim0, rim1, "gx")
    rows = field_rows()
    block, square = on_chip((rows, TILE)), on_chip((rows, COLS))
    rim0, rim1, inner = plain_call(
        rim_x_kernel, [block, block, square], "rim_x", held(wide), held(first), held(second)
    )
    first, second = swaps(rim0, rim1, "gy")
    if two_along_z():
        sends = on_chip((128, TILE))
        total, send = plain_call(
            rim_y_two_kernel, [square, sends], "rim_y", held(inner), held(first), held(second)
        )
        got, _ = swaps(send, send, "gz")
        outs = [(1, 1, 1, 10, 8, COLS), (1, 1, 2, TILE), (1, 1, 16, TILE)]
        outs = [jax.ShapeDtypeStruct(shape, F32) for shape in outs]
        return tuple(plain_call(finish_two_kernel, outs, "finish", held(total), held(got)))
    total = plain_call(rim_y_kernel, square, "rim_y", held(inner), held(first), held(second))
    fields = total[:80].reshape(10, 8, COLS)
    rim = total[80:].reshape(10, 8, COLS)
    from_below, from_above = exchange(rim[:, :4], rim[:, 4:], "gz")
    fields = fields + jnp.concatenate([from_below, from_above], axis=1)
    share = COLS // lax.axis_size("gz")
    start = lax.axis_index("gz") * share
    density = fields[0]
    velocity = fields[1] / (density + FLOOR_LEVEL)
    shear = fields[8]
    press = (fields[4] + fields[5] + fields[6]) / 3.0
    profile = jnp.stack([density, velocity, shear, press])
    whole = lax.all_gather(profile, "gz", axis=1, tiled=True)
    whole = lax.dynamic_slice_in_dim(whole, start, share, 2)
    fitted, inertial = column_fit(*whole)
    return (fields[None, None, None], fitted[None, None], inertial[None, None])


def solution(mesh):
    in_specs = (P("gx", "gy", "gz", None, None), P("gx", "gy", "gz", None, None))
    out_specs = (
        P("gx", "gy", "gz", None, None, None),
        P("gx", "gy", None, "gz"),
        P("gx", "gy", None, "gz"),
    )
    return jax.shard_map(local, mesh=mesh, in_specs=in_specs, out_specs=out_specs, check_vma=False)
```

```python
import math

import jax
import jax.numpy as jnp
from jax import lax
from jax.experimental import pallas as pl
from jax.experimental.pallas import tpu as pltpu
from jax.sharding import PartitionSpec as P

TILE = 128
BOXES_DOWNSLOPE = 8
BOXES_SPANWISE = 2
BOXES_NORMAL = 2
CELLS_PER_EDGE = 4

TILE_BOX_EDGE = 5.0
SPRING = 2.0
SOFTEN = 0.05
FLOOR_LEVEL = 0.1
RIDGE_SHARE = 0.1
CUT_LEVEL = math.exp(-12.5)
NORM_ONE = 1.0 / math.sqrt(2.0 * math.pi)

PITCH = TILE_BOX_EDGE / CELLS_PER_EDGE
REACH = 1.21
ABSENT = -10.0

NB = BOXES_DOWNSLOPE * BOXES_SPANWISE * BOXES_NORMAL
PITCH_ROWS = NB + 8
COLS = CELLS_PER_EDGE * BOXES_DOWNSLOPE * CELLS_PER_EDGE * BOXES_SPANWISE
CAPS = (16, 12, 16, 12, 14)

KERNEL_VMEM = 32 * 1024 * 1024

F32 = jnp.float32
BF16 = jnp.bfloat16


def iota(shape, dim):
    return lax.broadcasted_iota(jnp.int32, shape, dim)


def split3(value):
    high = value.astype(BF16)
    rest = value - high.astype(F32)
    mid = rest.astype(BF16)
    low = (rest - mid.astype(F32)).astype(BF16)
    return high, mid, low


def pick(value, onehot):
    high, mid, low = split3(value)
    dot = lambda part: jnp.dot(part, onehot, preferred_element_type=F32)
    return (dot(low) + dot(mid)) + dot(high)


def is_last(axis):
    return lax.axis_index(axis) == lax.axis_size(axis) - 1


def is_even(axis):
    return lax.axis_index(axis) % 2 == 0


def sort_kernel(grains_ref, pairs_ref, own_ref, near_ref):
    flags = {(part, value): jnp.zeros((1, NB), F32) for part in "yz" for value in (0, 2)}
    for n in range(pairs_ref.shape[0]):
        pair = pairs_ref[n]
        hood = jnp.where(pair >= 0, pair, 13 * NB) >> 5
        third = (hood * 11) >> 5
        parts = {"y": third - 3 * ((third * 11) >> 5), "z": hood - 3 * third}
        flags = {k: jnp.where(parts[k[0]] == k[1], 1.0, f) for k, f in flags.items()}

    def upper(part, axis):
        alone = jnp.where(is_last(axis), 1.0 - flags[part, 0], 0.0)
        return jnp.maximum(flags[part, 2], alone)

    group = 64.0 * upper("y", "gy") + 128.0 * upper("z", "gz")
    rows = [grains_ref[r] for r in range(7)]
    centre = 0.5 * (jnp.min(rows[0], axis=1, keepdims=True) + jnp.max(rows[0], axis=1, keepdims=True))
    sub = iota((NB, TILE), 0)
    lane = iota((NB, TILE), 1)
    same = sub == lane
    group = jnp.concatenate([group, jnp.zeros((1, TILE - NB), F32)], axis=1)
    key = centre + jnp.sum(jnp.where(same, group, 0.0), axis=1, keepdims=True)
    wide = jnp.broadcast_to(key, (NB, TILE))
    key_row = jnp.sum(jnp.where(same, wide, 0.0), axis=0, keepdims=True)
    before = (wide < key_row) | ((wide == key_row) & (sub < lane))
    rank = jnp.sum(jnp.where(before, 1.0, 0.0), axis=0, keepdims=True)
    onehot = jnp.where((rank == sub.astype(F32)) & (lane < NB), 1.0, 0.0).astype(BF16)[:, :NB]
    for r in range(7):
        high, mid, low = split3(rows[r])
        dot = lambda part: jnp.dot(onehot, part, preferred_element_type=F32)
        value = (dot(low) + dot(mid)) + dot(high)
        own_ref[r] = value
        if r < 4:
            near_ref[r] = value


def box_sort(grains, pairs):
    shapes = [on_chip((7, NB, TILE)), on_chip((4, NB, TILE))]
    listed = pairs.transpose(0, 1, 2, 4, 3).reshape(pairs.shape[4], 1, NB)
    arrays = (pltpu.with_memory_space_constraint(a, pltpu.HBM) for a in (grains.reshape(7, NB, TILE), listed))
    return plain_call(sort_kernel, shapes, "box_sort", *arrays)


def lane_take(value, index):
    dims = lax.GatherDimensionNumbers(
        offset_dims=(),
        collapsed_slice_dims=(1,),
        start_index_map=(1,),
        operand_batching_dims=(0,),
        start_indices_batching_dims=(0,),
    )
    return lax.gather(
        value, index[..., None], dims, (1, 1), mode=lax.GatherScatterMode.PROMISE_IN_BOUNDS
    )


def pack(groups, tri):
    masks = [jnp.where(mask, 1.0, 0.0).astype(BF16) for lists in groups for mask, _ in lists]
    both = jnp.dot(jnp.concatenate(masks, axis=0), tri, preferred_element_type=F32)
    rows = masks[0].shape[0]
    ranks = both[:, :TILE]
    totals = [both[n * rows : (n + 1) * rows, TILE : 2 * TILE] for n in range(len(masks))]
    upto = {m: both[:, (2 + i) * TILE : (3 + i) * TILE] for i, m in enumerate(LANDMARKS)}
    offsets, ends, at = [], [], 0
    for lists in groups:
        offset = jnp.zeros((rows, TILE), F32)
        for _ in lists:
            offsets.append(offset)
            offset = offset + totals[at]
            at += 1
        ends.append(offset)
    lane_f = iota((rows, TILE), 1).astype(F32)
    wanted = jnp.concatenate([lane_f - offset for offset in offsets], axis=0)
    by_64 = upto[63] <= wanted
    by_32 = jnp.where(by_64, upto[95], upto[31]) <= wanted
    probe = jnp.where(by_64, jnp.where(by_32, upto[111], upto[79]), jnp.where(by_32, upto[47], upto[15]))
    place = jnp.where(by_64, 64, 0) + jnp.where(by_32, 32, 0) + jnp.where(probe <= wanted, 16, 0)
    for bit in (8, 4, 2, 1):
        place = jnp.where(lane_take(ranks, place + (bit - 1)) <= wanted, place + bit, place)
    packed, at = [], 0
    for lists, end in zip(groups, ends):
        outs = [jnp.zeros((rows, TILE), F32)] * 3 + [jnp.full((rows, TILE), ABSENT, F32)]
        for _, arrays in lists:
            here = slice(at * rows, (at + 1) * rows)
            ours = (wanted[here] >= 0.0) & (wanted[here] < totals[at])
            outs = [jnp.where(ours, lane_take(v, place[here]), o) for v, o in zip(arrays, outs)]
            at += 1
        packed.append((outs, end))
    return packed


def pair_terms(own, cand, sums):
    own_x, own_y, own_z, own_r = own
    cand_x, cand_y, cand_z, cand_r = cand
    dx, dy, dz = own_x - cand_x, own_y - cand_y, own_z - cand_z
    square = dx * dx + dy * dy + dz * dz
    distance = square * lax.rsqrt(jnp.maximum(square, 1e-30))
    overlap = jnp.maximum(own_r + cand_r - distance, 0.0)
    below = distance + SOFTEN
    guess = pl.reciprocal(below, approx=True)
    force = (0.5 * SPRING) * overlap * (guess * (2.0 - below * guess))
    fx, fy, fz = force * dx, force * dy, force * dz
    terms = (fx * dx, fy * dy, fz * dz, fx * dy, fx * dz, fy * dz)
    return tuple(s + t for s, t in zip(sums, terms))


def weights(coords, centres):
    diff = coords - centres
    return jnp.maximum(jnp.exp(-0.5 * diff * diff) - CUT_LEVEL, 0.0) * NORM_ONE


def centres(places):
    return (places.astype(F32) - CELLS_PER_EDGE + 0.5) * PITCH


def plane_kernel(own_ref, plane_ref):
    nx = CELLS_PER_EDGE * (BOXES_DOWNSLOPE + 2)
    ny = CELLS_PER_EDGE * (BOXES_SPANWISE + 2)

    def put_plane(t):
        wx = weights(own_ref[0, pl.ds(t, 1), :], centres(iota((nx, TILE), 0)))
        wy = weights(own_ref[1, pl.ds(t, 1), :], centres(iota((ny, TILE), 0)))
        parts = [wx[x : x + 1] * wy for x in list(range(4)) + list(range(nx - 4, nx))]
        inner_x = wx[4 : nx - 4]
        parts += [inner_x * wy[y : y + 1] for y in list(range(4)) + list(range(ny - 4, ny))]
        inner_y = wy[4 : ny - 4]
        parts += [wx[x : x + 1] * inner_y for x in range(4, nx - 4)]
        lanes = pl.ds(pl.multiple_of(t * TILE, TILE), TILE)
        plane_ref[:, lanes] = jnp.concatenate(parts, axis=0).astype(BF16)

    def four_planes(q, carry):
        for i in range(4):
            put_plane(4 * q + i)
        return carry

    lax.fori_loop(0, NB // 4, four_planes, 0)


SPAN_X = BOXES_DOWNSLOPE * TILE_BOX_EDGE
SPAN_Y = BOXES_SPANWISE * TILE_BOX_EDGE
SPAN_Z = BOXES_NORMAL * TILE_BOX_EDGE


LANDMARKS = (15, 31, 47, 63, 79, 95, 111)


def running_sums():
    row, col = iota((TILE, TILE), 0), iota((TILE, TILE), 1)
    blocks = [row <= col] + [row <= last for last in (TILE - 1,) + LANDMARKS]
    return jnp.concatenate([jnp.where(b, 1.0, 0.0) for b in blocks], axis=1).astype(BF16)


def shifts(place, span):
    return jnp.where(place == 0, -span, jnp.where(place == 3, span, 0.0))


def alive(radius):
    return jnp.where(radius == 0.0, ABSENT, radius)


def near(arrays, axis, low, step):
    limit = arrays[axis] >= low - REACH if step < 0 else arrays[axis] <= low + (TILE_BOX_EDGE + REACH)
    return limit & (arrays[3] > 0.0), arrays


def in_this_frame(grid_ref):
    row = iota((128, TILE), 0)
    return [
        grid_ref[0],
        grid_ref[1] + shifts((row >> 3) & 3, SPAN_Y),
        grid_ref[2] + shifts(row >> 5, SPAN_Z),
        alive(grid_ref[3]),
    ]


def beside_in_this_frame(side_ref):
    row = iota((16, TILE), 0)
    return [
        [
            side_ref[k, 0] + shift_x,
            side_ref[k, 1] + shifts(row & 3, SPAN_Y),
            side_ref[k, 2] + shifts(row >> 2, SPAN_Z),
            alive(side_ref[k, 3]),
        ]
        for k, shift_x in ((0, -SPAN_X), (1, SPAN_X))
    ]


def parts(value):
    return [p.astype(F32) for p in split3(value)]


def keep(ref, first, values):
    for f, value in enumerate(values):
        at = (first + f) * PITCH_ROWS
        ref[at : at + NB, :] = value


def keep_chunks(chunks, feature_ref, moment_ref, own_ref=None):
    half_box = 0.5 * TILE_BOX_EDGE
    ones = jnp.ones((NB, TILE), F32)
    none = jnp.zeros((NB, TILE), F32)
    tile = iota((NB, TILE), 0)
    middle = [
        TILE_BOX_EDGE * (tile & 7).astype(F32) + half_box,
        TILE_BOX_EDGE * ((tile >> 3) & 1).astype(F32) + half_box,
        TILE_BOX_EDGE * (tile >> 4).astype(F32) + half_box,
    ]
    for k, chunk in enumerate(chunks):
        x, y, z = (chunk[c] - middle[c] for c in range(3))
        squares = [x * x, y * y, z * z]
        norm = squares[0] + squares[1] + squares[2]
        xs, ys, zs, ns, rs = (parts(v) for v in (x, y, z, norm, chunk[3]))
        keep(
            feature_ref, 16 * k,
            [xs[0], ys[0], zs[0], xs[1], ys[1], zs[1], ones, ns[0]]
            + [xs[2], ys[2], zs[2], ns[1], ns[2]] + rs,
        )
        products = squares + [x * y, x * z, y * z]
        highs = [v.astype(BF16).astype(F32) for v in products]
        lows = [v - h for v, h in zip(products, highs)]
        keep(moment_ref, 16 * k, highs + [none] * 2 + lows + [none] * 2)
        if own_ref is not None and k == 0:
            xi, yi, zi = ([-2.0 * p for p in v] for v in (xs, ys, zs))
            keep(
                own_ref, 0,
                [xi[0], yi[0], zi[0], xi[0], yi[0], zi[0], ns[0], ones]
                + [xi[0], yi[0], zi[0], ones, ones] + [none] * 3
                + [xi[1], yi[1], zi[1], xi[1], yi[1], zi[1], ns[1], none]
                + [xi[2], yi[2], zi[2], none, none, none, ns[2], none]
                + rs + [x, y, z],
            )


def excess(counts, caps):
    worst = [jnp.max(n, axis=0, keepdims=True) - 8.0 * cap for n, cap in zip(counts, caps)]
    while len(worst) > 1:
        worst = [jnp.maximum(worst[0], worst[1])] + worst[2:]
    return worst[0]


def pick_rows(arrays, starts, size):
    return [jnp.concatenate([v[at : at + size] for at in starts], axis=0) for v in arrays]


def pair_loop(chunks, first_chunk, own_ref, sum_ref, even_ref, odd_ref):
    caps = CAPS[first_chunk : first_chunk + len(chunks)]
    starts = [8 * sum(caps[:k]) for k in range(len(caps))]
    sub = iota((8, TILE), 0)

    def own_side(t):
        radii = [own_ref[pl.ds((32 + p) * PITCH_ROWS + t, 1), :] for p in range(3)]
        radii = [jnp.where(sub == 6, jnp.broadcast_to(r, (8, TILE)), 0.0) for r in radii]
        reach = [radii[0], jnp.where(sub >= 5, 1.0, 0.0), radii[1], radii[2]]
        return jnp.concatenate(
            [own_ref[pl.ds(t, 32, stride=PITCH_ROWS), :], jnp.concatenate(reach, axis=0)], axis=1
        ).astype(BF16)

    def measure_pairs(t, k, rhs, ref):
        source, _, n = chunks[k]
        rows = source[pl.ds(16 * n * PITCH_ROWS + t, 16, stride=PITCH_ROWS), :]
        first = rows[:8]
        lhs = jnp.concatenate([rows, first, first], axis=0).T.astype(BF16)
        size = 8 * caps[k]
        ref[starts[k] : starts[k] + size, :] = jnp.dot(lhs[:size], rhs, preferred_element_type=F32)

    def forces(k, ref):
        size = 8 * caps[k]
        square = jnp.maximum(ref[starts[k] : starts[k] + size, :TILE], 1e-12)
        distance = square * lax.rsqrt(square)
        overlap = jnp.maximum(ref[starts[k] : starts[k] + size, TILE:] - distance, 0.0)
        below = distance + SOFTEN
        guess = pl.reciprocal(below, approx=True)
        force = overlap * (guess * (2.0 - below * guess))
        if first_chunk + k == 0:
            at = iota((TILE, TILE), 0) == iota((TILE, TILE), 1)
            force = jnp.where(at, 0.0, force)
        high = force.astype(BF16)
        low = (force - high.astype(F32)).astype(BF16)
        rest = TILE - size
        if rest:
            none = jnp.zeros((rest, TILE), BF16)
            high, low = (jnp.concatenate([v, none], axis=0) for v in (high, low))
        return high, low

    def add_up(t, found):
        moments = []
        for features, products, n in chunks:
            first = features[pl.ds(16 * n * PITCH_ROWS + t, 8, stride=PITCH_ROWS), :]
            more = products[pl.ds(16 * n * PITCH_ROWS + t, 16, stride=PITCH_ROWS), :]
            moments.append(jnp.concatenate([first, more, first], axis=0))
        lhs = jnp.concatenate(moments, axis=1).astype(BF16)
        highs = jnp.concatenate([p[0] for p in found], axis=0)
        lows = jnp.concatenate([p[1] for p in found], axis=0)
        one = jnp.dot(lhs, highs, preferred_element_type=F32)
        two = jnp.dot(lhs[:16], lows, preferred_element_type=F32)
        sum_ref[pl.ds(t, 8, stride=PITCH_ROWS), :] = one[:8] + two[:8]
        sum_ref[pl.ds(8 * PITCH_ROWS + t, 8, stride=PITCH_ROWS), :] = one[8:16] + (one[16:24] + two[8:])

    def step(t, here_ref, next_t, next_ref):
        rhs = own_side(next_t)
        found = []
        for k in range(len(chunks)):
            measure_pairs(next_t, k, rhs, next_ref)
            found.append(forces(k, here_ref))
        add_up(t, found)

    first_rhs = own_side(0)
    for k in range(len(chunks)):
        measure_pairs(0, k, first_rhs, even_ref)

    def eight_tiles(q, carry):
        refs = (even_ref, odd_ref)
        for i in range(8):
            t = 8 * q + i
            step(t, refs[i % 2], t + 1 if i < 7 else jnp.minimum(t + 1, NB - 1), refs[1 - i % 2])
        return carry

    lax.fori_loop(0, NB // 8, eight_tiles, 0)


def table(rows):
    return on_chip((rows * PITCH_ROWS, TILE))


def pair_space(chunks, groups):
    return [table(16 * chunks), table(16 * chunks)] + [pltpu.VMEM((8 * groups, 2 * TILE), F32)] * 2


def own_kernel(grains_ref, own_ref, sum_ref, feature_ref, moment_ref, even_ref, odd_ref):
    keep_chunks([[grains_ref[c] for c in range(4)]], feature_ref, moment_ref, own_ref)
    pair_loop([(feature_ref, moment_ref, 0)], 0, own_ref, sum_ref, even_ref, odd_ref)


def pair_own(grains):
    return plain_call(own_kernel, [table(38), table(16)], "own", held(grains), scratch=pair_space(1, CAPS[0]))


def near_kernel(grid_ref, lists_ref, excess_ref, feature_ref, moment_ref):
    tri = running_sums()
    here = in_this_frame(grid_ref)
    low_z = TILE_BOX_EDGE * (iota((64, TILE), 0) >> 5).astype(F32)
    low_y = TILE_BOX_EDGE * ((iota((32, TILE), 0) >> 3) & 1).astype(F32)
    cut_z = lambda start: [v[32 * start : 32 * start + 64] for v in here]
    cut_y = lambda arrays, start: pick_rows(arrays, (8 * start, 32 + 8 * start), 16)
    level = cut_z(1)
    ((beside_z, count_z),) = pack([[near(cut_z(0), 2, low_z, -1), near(cut_z(2), 2, low_z, 1)]], tri)
    ((beside_y, count_y),) = pack(
        [
            [
                near(cut_y(level, 0), 1, low_y, -1),
                near(cut_y(beside_z, 0), 1, low_y, -1),
                near(cut_y(level, 2), 1, low_y, 1),
                near(cut_y(beside_z, 2), 1, low_y, 1),
            ]
        ],
        tri,
    )
    excess_ref[...] = excess((count_z, count_y), CAPS[1:3])
    chunks = [cut_y(beside_z, 1), beside_y]
    for k in range(2):
        for c in range(4):
            lists_ref[4 * k + c] = chunks[k][c]
    keep_chunks(chunks, feature_ref, moment_ref)


def find_near(grid):
    shapes = [on_chip((8, NB, TILE)), on_chip((1, TILE)), table(2 * 16), table(2 * 16)]
    return plain_call(near_kernel, shapes, "near", held(grid))


def two_along_z():
    return lax.axis_size("gz") == 2


def field_rows():
    return 80 + (48 if two_along_z() else 80)


def stress_kernel(
    grid_ref, side_ref, grains_ref, plane_ref, own_ref, own_sum_ref,
    lists_ref, excess_ref, feature_near_ref, moment_near_ref,
    rim0_ref, rim1_ref, out_ref,
    all_ref, contact_ref, height_ref, feature_far_ref, moment_far_ref, sum_ref, even_ref, odd_ref,
):
    tri = running_sums()
    sides = beside_in_this_frame(side_ref)

    edge = [jnp.concatenate([low, high], axis=0) for low, high in zip(*sides)]
    row = iota((8, TILE), 0)
    low_z = TILE_BOX_EDGE * ((row >> 1) & 1).astype(F32)
    low_y = TILE_BOX_EDGE * (row & 1).astype(F32)

    def around(dz, dy):
        return pick_rows(edge, [16 * s + 4 * (z + 1 + dz) + 1 + dy for s in range(2) for z in range(2)], 2)

    def near_edge(dz, dy):
        arrays = around(dz, dy)
        mask = jnp.where(row < 4, arrays[0], SPAN_X - arrays[0]) >= -REACH
        for axis, low, step in ((2, low_z, dz), (1, low_y, dy)):
            if step:
                mask = mask & near(arrays, axis, low, step)[0]
        return mask & (arrays[3] > 0.0), arrays

    beside_edge = [(dz, dy) for dz in (-1, 0, 1) for dy in (-1, 0, 1) if dz or dy]
    ((edge_z, count_e),) = pack([[near_edge(dz, dy) for dz, dy in beside_edge]], tri)
    edge_own = around(0, 0)
    empty = jnp.zeros((8, TILE), F32)
    edge_y = [empty, empty, empty, empty + ABSENT]

    low_x = TILE_BOX_EDGE * (iota((NB, TILE), 0) & 7).astype(F32)
    in_box_x = iota((4, 8, TILE), 1)

    def along_x(arrays, edges, step):
        found = []
        for value, rim in zip(arrays, edges):
            moved = pltpu.roll(value.reshape(4, 8, TILE), 1 if step < 0 else 7, 1)
            rim = rim[:4] if step < 0 else rim[4:]
            at_edge = in_box_x == (0 if step < 0 else 7)
            found.append(jnp.where(at_edge, rim[:, None, :], moved).reshape(NB, TILE))
        return near(found, 0, low_x, step)

    own = [grains_ref[c * NB : (c + 1) * NB, :] for c in range(4)]
    list_z = [lists_ref[c] for c in range(4)]
    list_y = [lists_ref[4 + c] for c in range(4)]
    (beside, count_x), (beside_rest, count_w) = pack(
        [
            [along_x(own, edge_own, -1), along_x(own, edge_own, 1)],
            [
                along_x(list_z, edge_z, -1),
                along_x(list_y, edge_y, -1),
                along_x(list_z, edge_z, 1),
                along_x(list_y, edge_y, 1),
            ],
        ],
        tri,
    )
    keep_chunks([beside, beside_rest], feature_far_ref, moment_far_ref)
    overflow = jnp.maximum(
        excess_ref[...], excess((count_e, count_x, count_w), (TILE // 8,) + CAPS[3:])
    )
    overflow = jnp.max(overflow)

    at_z = iota((8, TILE), 0)
    centres_inner = centres(at_z + 4)
    if two_along_z():
        centres_rim = centres((at_z & 3) + jnp.where(lax.axis_index("gz") == 0, 12, 0))
    else:
        centres_rim = centres(jnp.where(at_z < 4, at_z, at_z + 8))

    def put_height(t):
        rows = [grains_ref[pl.ds(r * NB + t, 1), :] for r in range(2, 7)]
        wz_inner = weights(rows[0], centres_inner)
        wz_rim = weights(rows[0], centres_rim)
        masses = 4.0 * math.pi / 3.0 * rows[1] * rows[1] * rows[1]
        vel = rows[2:]
        cont = [contact_ref[pl.ds(k * NB + t, 1), :] for k in range(6)]
        loads = [masses, masses * vel[0], masses * vel[1], masses * vel[2]]
        for k, (i, j) in enumerate(((0, 0), (1, 1), (2, 2), (0, 1), (0, 2), (1, 2))):
            loads.append(cont[k] + masses * (vel[i] * vel[j]))
        height = [load * wz_inner for load in loads]
        if two_along_z():
            height += [jnp.where(at_z < 4, loads[c], loads[c + 1]) * wz_rim for c in range(0, 10, 2)]
            height.append(jnp.zeros((8, TILE), F32))
        else:
            height += [load * wz_rim for load in loads]
        lanes = pl.ds(pl.multiple_of(t * TILE, TILE), TILE)
        height_ref[:, lanes] = jnp.concatenate(height, axis=0).astype(BF16)

    def own_rows(t):
        return tuple(
            jnp.broadcast_to(grains_ref[pl.ds(c * NB + t, 1), :], (8, TILE)) for c in range(4)
        )

    def group(columns, first, g):
        return tuple(
            jnp.broadcast_to(columns[8 * g : 8 * g + 8, first + c : first + c + 1], (8, TILE)) for c in range(4)
        )

    def put(t, sums):
        for k in range(6):
            contact_ref[pl.ds(k * NB + t, 1), :] = jnp.sum(sums[k], axis=0, keepdims=True)

    zeros = tuple(jnp.zeros((8, TILE), F32) for _ in range(6))

    @pl.when(overflow <= 0.0)
    def _():
        tables = [(feature_near_ref, moment_near_ref, k) for k in range(2)]
        tables += [(feature_far_ref, moment_far_ref, k) for k in range(2)]
        pair_loop(tables, 1, own_ref, sum_ref, even_ref, odd_ref)
        rows = lambda ref, m: ref[m * PITCH_ROWS : m * PITCH_ROWS + NB, :]
        total = [rows(sum_ref, m) + rows(own_sum_ref, m) for m in range(14)]
        first = [total[c] + total[3 + c] for c in range(3)]
        own_mid = [own_ref[(35 + c) * PITCH_ROWS : (35 + c) * PITCH_ROWS + NB, :] for c in range(3)]
        for k, (i, j) in enumerate(((0, 0), (1, 1), (2, 2), (0, 1), (0, 2), (1, 2))):
            a, b = own_mid[i], own_mid[j]
            contact_ref[k * NB : (k + 1) * NB, :] = (0.5 * SPRING) * (
                total[8 + k] - (a * first[j] + b * first[i]) + a * b * total[6]
            )

    @pl.when(overflow > 0.0)
    def _():
        stride = 16 * 8 + 32
        here = in_this_frame(grid_ref)
        for c in range(4):
            all_ref[c * stride : c * stride + 128, :] = here[c]
            all_ref[c * stride + 128 : c * stride + 144, :] = sides[0][c]
            all_ref[c * stride + 144 : c * stride + 160, :] = sides[1][c]
        all_ref[4 * stride : 8 * stride, :] = jnp.zeros((4 * stride, TILE), F32)

        def one_tile(t, carry):
            own = own_rows(t)
            tile_x, tile_y, tile_z = t & 7, (t >> 3) & 1, t >> 4

            def one_near(n, sums):
                n_x = n // 9
                n_y = (n - 9 * n_x) // 3
                n_z = n - 9 * n_x - 3 * n_y
                at_x = tile_x + n_x - 1
                plane = 4 * (tile_z + n_z) + tile_y + n_y
                place = jnp.where(
                    at_x < 0, 128 + plane, jnp.where(at_x > 7, 144 + plane, 8 * plane + at_x)
                )
                columns = all_ref[pl.ds(place, 8, stride=stride), :].T
                for g in range(16):
                    sums = pair_terms(own, group(columns, 0, g), sums)
                return sums

            put(t, lax.fori_loop(0, 27, one_near, zeros))
            return carry

        lax.fori_loop(0, NB, one_tile, 0)

    def four_heights(q, carry):
        for i in range(4):
            put_height(4 * q + i)
        return carry

    lax.fori_loop(0, NB // 4, four_heights, 0)
    wide = lax.dot_general(
        height_ref[...], plane_ref[...], (((1,), (1,)), ((), ())), preferred_element_type=F32
    )
    out_ref[...] = wide[:, TILE:]
    rim = wide[:, :TILE]
    rim = jnp.where(is_even("gx"), pltpu.roll(rim, 64, 1), rim)
    half = field_rows() // 2
    upper, lower = rim[:half], rim[half:]
    left_half = iota((half, TILE), 1) < 64
    rim0_ref[...] = jnp.where(left_half, upper, pltpu.roll(lower, 64, 1))
    rim1_ref[...] = jnp.where(left_half, pltpu.roll(upper, 64, 1), lower)


def stress_and_deposit(grid, side, grains, plane, *tables):
    rows = field_rows()
    return plain_call(
        stress_kernel,
        [on_chip((rows // 2, TILE)), on_chip((rows // 2, TILE)), on_chip((rows, 2 * TILE + COLS))],
        "stress_deposit",
        held(grid),
        held(side),
        held(grains),
        held(plane),
        *(held(v) for v in tables),
        scratch=[
            pltpu.VMEM((8 * 160, TILE), F32),
            pltpu.VMEM((6 * NB, TILE), F32),
            pltpu.VMEM((rows, NB * TILE), BF16),
            pltpu.VMEM((2 * 16 * PITCH_ROWS, TILE), F32),
            pltpu.VMEM((2 * 16 * PITCH_ROWS, TILE), F32),
            pltpu.VMEM((16 * PITCH_ROWS, TILE), F32),
            pltpu.VMEM((8 * sum(CAPS[1:]), 2 * TILE), F32),
            pltpu.VMEM((8 * sum(CAPS[1:]), 2 * TILE), F32),
        ],
    )


def rim_x_kernel(wide_ref, first_ref, second_ref, rim0_ref, rim1_ref, inner_ref):
    even = is_even("gx")
    right = jnp.where(even, first_ref[...], second_ref[...])
    left = jnp.where(even, second_ref[...], first_ref[...])
    left_half = iota(left.shape, 1) < 64
    got = jnp.concatenate(
        [
            jnp.where(left_half, right, pltpu.roll(left, 64, 1)),
            jnp.where(left_half, pltpu.roll(right, 64, 1), left),
        ],
        axis=0,
    )
    src = iota((TILE, 1), 0)
    x = (src >> 4) & 3
    x = jnp.where(src >= 64, x, x + (CELLS_PER_EDGE * BOXES_DOWNSLOPE - 4))
    y = src & 15
    target = jnp.where(y < 4, y * 32 + x, jnp.where(y >= 12, 128 + (y - 12) * 32 + x, 256 + x * 8 + y - 4))
    onehot = jnp.where(iota((TILE, 512), 1) == target, 1.0, 0.0).astype(BF16)
    total = wide_ref[...] + pick(got, onehot)
    low, high = total[:, :TILE], total[:, TILE : 2 * TILE]
    even = is_even("gy")
    rim0_ref[...] = jnp.where(even, high, low)
    rim1_ref[...] = jnp.where(even, low, high)
    inner_ref[...] = total[:, 2 * TILE :]


def add_rim_y(inner_ref, first_ref, second_ref):
    even = is_even("gy")
    right = jnp.where(even, first_ref[...], second_ref[...])
    left = jnp.where(even, second_ref[...], first_ref[...])
    got = jnp.concatenate([left, right], axis=1)
    src = iota((256, 1), 0)
    target = (src & 31) * 8 + 4 * (src >> 7) + ((src >> 5) & 3)
    onehot = jnp.where(iota((256, 256), 1) == target, 1.0, 0.0).astype(BF16)
    return inner_ref[...] + pick(got, onehot)


def rim_y_kernel(inner_ref, first_ref, second_ref, out_ref):
    out_ref[...] = add_rim_y(inner_ref, first_ref, second_ref)


PROFILED = (0, 1, 4, 5, 6, 8)


def rim_y_two_kernel(inner_ref, first_ref, second_ref, out_ref, send_ref):
    total = add_rim_y(inner_ref, first_ref, second_ref)
    out_ref[...] = total
    lower = lax.axis_index("gz") == 0
    send_ref[:40, :] = total[80:120, :TILE]
    send_ref[40:80, :] = total[80:120, TILE:]
    for i, c in enumerate(PROFILED):
        rows = total[8 * c : 8 * c + 8]
        send_ref[80 + 8 * i : 88 + 8 * i, :] = jnp.where(lower, rows[:, TILE:], rows[:, :TILE])


def finish_two_kernel(total_ref, got_ref, fields_ref, fits_ref, inertial_ref):
    lower = lax.axis_index("gz") == 0
    row = iota((8, COLS), 0)
    from_rim = jnp.where(lower, 7 - row, row)
    ours = from_rim < 4
    theirs = from_rim[:, :TILE] >= 4
    fields = []
    for p in range(5):
        got = jnp.concatenate(
            [got_ref[8 * p : 8 * p + 8, :], got_ref[40 + 8 * p : 48 + 8 * p, :]], axis=1
        )
        turned = pltpu.roll(got, 4, 0)
        for i, add in enumerate(
            (jnp.where(lower, turned, got), jnp.where(lower, got, turned))
        ):
            c = 2 * p + i
            fields.append(total_ref[8 * c : 8 * c + 8, :] + jnp.where(ours, add, 0.0))
            fields_ref[0, 0, 0, c] = fields[c]
    column = {}
    for i, c in enumerate(PROFILED):
        mine = jnp.where(lower, fields[c][:, :TILE], fields[c][:, TILE:])
        rim = total_ref[80 + 8 * (c // 2) : 88 + 8 * (c // 2), :]
        rim = jnp.where(lower, rim[:, :TILE], rim[:, TILE:])
        rim = jnp.where(lower == (c % 2 == 0), rim, pltpu.roll(rim, 4, 0))
        other = got_ref[80 + 8 * i : 88 + 8 * i, :] + jnp.where(theirs, rim, 0.0)
        column[c] = jnp.concatenate(
            [jnp.where(lower, mine, other), jnp.where(lower, other, mine)], axis=0
        )
    density = column[0]
    velocity = column[1] / (density + FLOOR_LEVEL)
    press = (column[4] + column[5] + column[6]) / 3.0
    fitted, inertial = column_fit(density, velocity, column[8], press)
    fits_ref[0, 0] = fitted
    inertial_ref[0, 0] = inertial


def held(array):
    return pltpu.with_memory_space_constraint(array, pltpu.VMEM)


def on_chip(shape, dtype=F32):
    return pltpu.VMEM(shape, dtype)


def plain_call(kernel, shapes, name, *args, scratch=()):
    vmem = pl.BlockSpec(memory_space=pltpu.VMEM)
    return pl.pallas_call(
        kernel,
        out_shape=shapes,
        in_specs=[vmem] * len(args),
        out_specs=jax.tree.map(lambda _: vmem, shapes),
        scratch_shapes=scratch,
        compiler_params=pltpu.CompilerParams(vmem_limit_bytes=KERNEL_VMEM),
        name=name,
    )(*args)


def column_fit(density, velocity, shear, press):
    upper = jnp.concatenate([velocity[1:, :], velocity[-1:, :]], axis=0)
    lower = jnp.concatenate([velocity[:1, :], velocity[:-1, :]], axis=0)
    rate = (upper - lower) / (2.0 * PITCH)
    inertial = rate * 1.0 / jnp.sqrt((press + FLOOR_LEVEL) / (density + FLOOR_LEVEL))
    friction = shear / (press + FLOOR_LEVEL)
    weight = density + FLOOR_LEVEL
    add = lambda v: jnp.sum(v, axis=0, keepdims=True)
    sum_zero = add(weight)
    sum_one = add(weight * inertial)
    sum_two = add(weight * inertial * inertial) + RIDGE_SHARE * sum_zero
    mix_zero = add(weight * friction)
    mix_one = add(weight * friction * inertial)
    determ = sum_zero * sum_two - sum_one * sum_one
    fitted = jnp.concatenate(
        [
            (mix_zero * sum_two - sum_one * mix_one) / determ,
            (sum_zero * mix_one - sum_one * mix_zero) / determ,
        ],
        axis=0,
    )
    return fitted, inertial


def swaps(first, second, axis):
    count = lax.axis_size(axis)
    got = []
    for start, value in ((0, first), (1, second)):
        links = []
        for i in range(start, count - 1, 2):
            links += [(i, i + 1), (i + 1, i)]
        got.append(lax.ppermute(value, axis, links) if links else jnp.zeros_like(value))
    return got


def exchange(low, high, axis):
    even = is_even(axis)
    one, two = swaps(jnp.where(even, high, low), jnp.where(even, low, high), axis)
    return jnp.where(even, two, one), jnp.where(even, one, two)


def local(grains, pairs):
    own, near = box_sort(grains, pairs)
    cube = near.reshape(4, 2, 2, 8, TILE)
    sends, placed = lax.optimization_barrier(((cube[:, 0], cube[:, 1]), own))
    own_table, own_sums = pair_own(placed)
    below, above = exchange(*sends, "gz")
    cube = jnp.concatenate([below[:, None], cube, above[:, None]], axis=1)
    sends = (cube[:, :, 0], cube[:, :, 1])
    sends, placed, own_table, own_sums = lax.optimization_barrier((sends, own, own_table, own_sums))
    plane = plain_call(
        plane_kernel, on_chip((3 * TILE + COLS, NB * TILE), BF16), "plane", held(placed)
    )
    below, above = exchange(*sends, "gy")
    cube = jnp.concatenate([below[:, :, None], cube, above[:, :, None]], axis=2)
    cube, plane = lax.optimization_barrier((cube, plane))
    sends = (cube[:, :, :, 0], cube[:, :, :, 7])
    sends, placed = lax.optimization_barrier((sends, cube))
    tables = find_near(placed.reshape(4, 128, TILE))
    below, above = exchange(*sends, "gx")
    side = jnp.stack([below, above]).reshape(2, 4, 16, TILE)
    rim0, rim1, wide = stress_and_deposit(
        cube.reshape(4, 128, TILE), side, own.reshape(7 * NB, TILE), plane, own_table, own_sums, *tables
    )
    first, second = swaps(rim0, rim1, "gx")
    rows = field_rows()
    block, square = on_chip((rows, TILE)), on_chip((rows, COLS))
    rim0, rim1, inner = plain_call(
        rim_x_kernel, [block, block, square], "rim_x", held(wide), held(first), held(second)
    )
    first, second = swaps(rim0, rim1, "gy")
    if two_along_z():
        sends = on_chip((128, TILE))
        total, send = plain_call(
            rim_y_two_kernel, [square, sends], "rim_y", held(inner), held(first), held(second)
        )
        got, _ = swaps(send, send, "gz")
        outs = [(1, 1, 1, 10, 8, COLS), (1, 1, 2, TILE), (1, 1, 16, TILE)]
        outs = [jax.ShapeDtypeStruct(shape, F32) for shape in outs]
        return tuple(plain_call(finish_two_kernel, outs, "finish", held(total), held(got)))
    total = plain_call(rim_y_kernel, square, "rim_y", held(inner), held(first), held(second))
    fields = total[:80].reshape(10, 8, COLS)
    rim = total[80:].reshape(10, 8, COLS)
    from_below, from_above = exchange(rim[:, :4], rim[:, 4:], "gz")
    fields = fields + jnp.concatenate([from_below, from_above], axis=1)
    share = COLS // lax.axis_size("gz")
    start = lax.axis_index("gz") * share
    density = fields[0]
    velocity = fields[1] / (density + FLOOR_LEVEL)
    shear = fields[8]
    press = (fields[4] + fields[5] + fields[6]) / 3.0
    profile = jnp.stack([density, velocity, shear, press])
    whole = lax.all_gather(profile, "gz", axis=1, tiled=True)
    whole = lax.dynamic_slice_in_dim(whole, start, share, 2)
    fitted, inertial = column_fit(*whole)
    return (fields[None, None, None], fitted[None, None], inertial[None, None])


def solution(mesh):
    in_specs = (P("gx", "gy", "gz", None, None), P("gx", "gy", "gz", None, None))
    out_specs = (
        P("gx", "gy", "gz", None, None, None),
        P("gx", "gy", None, "gz"),
        P("gx", "gy", None, "gz"),
    )
    return jax.shard_map(local, mesh=mesh, in_specs=in_specs, out_specs=out_specs, check_vma=False)
```

```python
import math

import jax
import jax.numpy as jnp
from jax import lax
from jax.experimental import pallas as pl
from jax.experimental.pallas import tpu as pltpu
from jax.sharding import PartitionSpec as P

TILE = 128
BOXES_DOWNSLOPE = 8
BOXES_SPANWISE = 2
BOXES_NORMAL = 2
CELLS_PER_EDGE = 4

TILE_BOX_EDGE = 5.0
SPRING = 2.0
SOFTEN = 0.05
FLOOR_LEVEL = 0.1
RIDGE_SHARE = 0.1
CUT_LEVEL = math.exp(-12.5)
NORM_ONE = 1.0 / math.sqrt(2.0 * math.pi)

PITCH = TILE_BOX_EDGE / CELLS_PER_EDGE
REACH = 1.21
ABSENT = -10.0

NB = BOXES_DOWNSLOPE * BOXES_SPANWISE * BOXES_NORMAL
PITCH_ROWS = NB + 8
COLS = CELLS_PER_EDGE * BOXES_DOWNSLOPE * CELLS_PER_EDGE * BOXES_SPANWISE
CAPS = (16, 12, 16, 12, 14)

KERNEL_VMEM = 32 * 1024 * 1024

F32 = jnp.float32
BF16 = jnp.bfloat16


def iota(shape, dim):
    return lax.broadcasted_iota(jnp.int32, shape, dim)


def split3(value):
    high = value.astype(BF16)
    rest = value - high.astype(F32)
    mid = rest.astype(BF16)
    low = (rest - mid.astype(F32)).astype(BF16)
    return high, mid, low


def pick(value, onehot):
    high, mid, low = split3(value)
    dot = lambda part: jnp.dot(part, onehot, preferred_element_type=F32)
    return (dot(low) + dot(mid)) + dot(high)


def is_last(axis):
    return lax.axis_index(axis) == lax.axis_size(axis) - 1


def is_even(axis):
    return lax.axis_index(axis) % 2 == 0


def sort_kernel(grains_ref, pairs_ref, own_ref, near_ref):
    flags = {(part, value): jnp.zeros((1, NB), F32) for part in "yz" for value in (0, 2)}
    for n in range(pairs_ref.shape[0]):
        pair = pairs_ref[n]
        hood = jnp.where(pair >= 0, pair, 13 * NB) >> 5
        third = (hood * 11) >> 5
        parts = {"y": third - 3 * ((third * 11) >> 5), "z": hood - 3 * third}
        flags = {k: jnp.where(parts[k[0]] == k[1], 1.0, f) for k, f in flags.items()}

    def upper(part, axis):
        alone = jnp.where(is_last(axis), 1.0 - flags[part, 0], 0.0)
        return jnp.maximum(flags[part, 2], alone)

    group = 64.0 * upper("y", "gy") + 128.0 * upper("z", "gz")
    rows = [grains_ref[r] for r in range(7)]
    centre = 0.5 * (jnp.min(rows[0], axis=1, keepdims=True) + jnp.max(rows[0], axis=1, keepdims=True))
    sub = iota((NB, TILE), 0)
    lane = iota((NB, TILE), 1)
    same = sub == lane
    group = jnp.concatenate([group, jnp.zeros((1, TILE - NB), F32)], axis=1)
    key = centre + jnp.sum(jnp.where(same, group, 0.0), axis=1, keepdims=True)
    wide = jnp.broadcast_to(key, (NB, TILE))
    key_row = jnp.sum(jnp.where(same, wide, 0.0), axis=0, keepdims=True)
    before = (wide < key_row) | ((wide == key_row) & (sub < lane))
    rank = jnp.sum(jnp.where(before, 1.0, 0.0), axis=0, keepdims=True)
    onehot = jnp.where((rank == sub.astype(F32)) & (lane < NB), 1.0, 0.0).astype(BF16)[:, :NB]
    for r in range(7):
        high, mid, low = split3(rows[r])
        dot = lambda part: jnp.dot(onehot, part, preferred_element_type=F32)
        value = (dot(low) + dot(mid)) + dot(high)
        own_ref[r] = value
        if r < 4:
            near_ref[r] = value


def box_sort(grains, pairs):
    shapes = [on_chip((7, NB, TILE)), on_chip((4, NB, TILE))]
    listed = pairs.transpose(0, 1, 2, 4, 3).reshape(pairs.shape[4], 1, NB)
    arrays = (pltpu.with_memory_space_constraint(a, pltpu.HBM) for a in (grains.reshape(7, NB, TILE), listed))
    return plain_call(sort_kernel, shapes, "box_sort", *arrays)


def lane_take(value, index):
    dims = lax.GatherDimensionNumbers(
        offset_dims=(),
        collapsed_slice_dims=(1,),
        start_index_map=(1,),
        operand_batching_dims=(0,),
        start_indices_batching_dims=(0,),
    )
    return lax.gather(
        value, index[..., None], dims, (1, 1), mode=lax.GatherScatterMode.PROMISE_IN_BOUNDS
    )


def pack(groups, tri):
    masks = [jnp.where(mask, 1.0, 0.0).astype(BF16) for lists in groups for mask, _ in lists]
    both = jnp.dot(jnp.concatenate(masks, axis=0), tri, preferred_element_type=F32)
    rows = masks[0].shape[0]
    ranks = both[:, :TILE]
    totals = [both[n * rows : (n + 1) * rows, TILE : 2 * TILE] for n in range(len(masks))]
    upto = {m: both[:, (2 + i) * TILE : (3 + i) * TILE] for i, m in enumerate(LANDMARKS)}
    offsets, ends, at = [], [], 0
    for lists in groups:
        offset = jnp.zeros((rows, TILE), F32)
        for _ in lists:
            offsets.append(offset)
            offset = offset + totals[at]
            at += 1
        ends.append(offset)
    lane_f = iota((rows, TILE), 1).astype(F32)
    wanted = jnp.concatenate([lane_f - offset for offset in offsets], axis=0)
    by_64 = upto[63] <= wanted
    by_32 = jnp.where(by_64, upto[95], upto[31]) <= wanted
    probe = jnp.where(by_64, jnp.where(by_32, upto[111], upto[79]), jnp.where(by_32, upto[47], upto[15]))
    place = jnp.where(by_64, 64, 0) + jnp.where(by_32, 32, 0) + jnp.where(probe <= wanted, 16, 0)
    for bit in (8, 4, 2, 1):
        place = jnp.where(lane_take(ranks, place + (bit - 1)) <= wanted, place + bit, place)
    packed, at = [], 0
    for lists, end in zip(groups, ends):
        outs = [jnp.zeros((rows, TILE), F32)] * 3 + [jnp.full((rows, TILE), ABSENT, F32)]
        for _, arrays in lists:
            here = slice(at * rows, (at + 1) * rows)
            ours = (wanted[here] >= 0.0) & (wanted[here] < totals[at])
            outs = [jnp.where(ours, lane_take(v, place[here]), o) for v, o in zip(arrays, outs)]
            at += 1
        packed.append((outs, end))
    return packed


def pair_terms(own, cand, sums):
    own_x, own_y, own_z, own_r = own
    cand_x, cand_y, cand_z, cand_r = cand
    dx, dy, dz = own_x - cand_x, own_y - cand_y, own_z - cand_z
    square = dx * dx + dy * dy + dz * dz
    distance = square * lax.rsqrt(jnp.maximum(square, 1e-30))
    overlap = jnp.maximum(own_r + cand_r - distance, 0.0)
    below = distance + SOFTEN
    guess = pl.reciprocal(below, approx=True)
    force = (0.5 * SPRING) * overlap * (guess * (2.0 - below * guess))
    fx, fy, fz = force * dx, force * dy, force * dz
    terms = (fx * dx, fy * dy, fz * dz, fx * dy, fx * dz, fy * dz)
    return tuple(s + t for s, t in zip(sums, terms))


def weights(coords, centres):
    diff = coords - centres
    return jnp.maximum(jnp.exp(-0.5 * diff * diff) - CUT_LEVEL, 0.0) * NORM_ONE


def centres(places):
    return (places.astype(F32) - CELLS_PER_EDGE + 0.5) * PITCH


def plane_kernel(own_ref, plane_ref):
    nx = CELLS_PER_EDGE * (BOXES_DOWNSLOPE + 2)
    ny = CELLS_PER_EDGE * (BOXES_SPANWISE + 2)

    def put_plane(t):
        wx = weights(own_ref[0, pl.ds(t, 1), :], centres(iota((nx, TILE), 0)))
        wy = weights(own_ref[1, pl.ds(t, 1), :], centres(iota((ny, TILE), 0)))
        parts = [wx[x : x + 1] * wy for x in list(range(4)) + list(range(nx - 4, nx))]
        inner_x = wx[4 : nx - 4]
        parts += [inner_x * wy[y : y + 1] for y in list(range(4)) + list(range(ny - 4, ny))]
        inner_y = wy[4 : ny - 4]
        parts += [wx[x : x + 1] * inner_y for x in range(4, nx - 4)]
        lanes = pl.ds(pl.multiple_of(t * TILE, TILE), TILE)
        plane_ref[:, lanes] = jnp.concatenate(parts, axis=0).astype(BF16)

    def four_planes(q, carry):
        for i in range(4):
            put_plane(4 * q + i)
        return carry

    lax.fori_loop(0, NB // 4, four_planes, 0)


SPAN_X = BOXES_DOWNSLOPE * TILE_BOX_EDGE
SPAN_Y = BOXES_SPANWISE * TILE_BOX_EDGE
SPAN_Z = BOXES_NORMAL * TILE_BOX_EDGE


LANDMARKS = (15, 31, 47, 63, 79, 95, 111)


def running_sums():
    row, col = iota((TILE, TILE), 0), iota((TILE, TILE), 1)
    blocks = [row <= col] + [row <= last for last in (TILE - 1,) + LANDMARKS]
    return jnp.concatenate([jnp.where(b, 1.0, 0.0) for b in blocks], axis=1).astype(BF16)


def shifts(place, span):
    return jnp.where(place == 0, -span, jnp.where(place == 3, span, 0.0))


def alive(radius):
    return jnp.where(radius == 0.0, ABSENT, radius)


def near(arrays, axis, low, step):
    limit = arrays[axis] >= low - REACH if step < 0 else arrays[axis] <= low + (TILE_BOX_EDGE + REACH)
    return limit & (arrays[3] > 0.0), arrays


def in_this_frame(grid_ref):
    row = iota((128, TILE), 0)
    return [
        grid_ref[0],
        grid_ref[1] + shifts((row >> 3) & 3, SPAN_Y),
        grid_ref[2] + shifts(row >> 5, SPAN_Z),
        alive(grid_ref[3]),
    ]


def beside_in_this_frame(side_ref):
    row = iota((16, TILE), 0)
    return [
        [
            side_ref[k, 0] + shift_x,
            side_ref[k, 1] + shifts(row & 3, SPAN_Y),
            side_ref[k, 2] + shifts(row >> 2, SPAN_Z),
            alive(side_ref[k, 3]),
        ]
        for k, shift_x in ((0, -SPAN_X), (1, SPAN_X))
    ]


def parts(value):
    return [p.astype(F32) for p in split3(value)]


def keep(ref, first, values):
    for f, value in enumerate(values):
        at = (first + f) * PITCH_ROWS
        ref[at : at + NB, :] = value


def keep_chunks(chunks, feature_ref, moment_ref, own_ref=None):
    half_box = 0.5 * TILE_BOX_EDGE
    ones = jnp.ones((NB, TILE), F32)
    none = jnp.zeros((NB, TILE), F32)
    tile = iota((NB, TILE), 0)
    middle = [
        TILE_BOX_EDGE * (tile & 7).astype(F32) + half_box,
        TILE_BOX_EDGE * ((tile >> 3) & 1).astype(F32) + half_box,
        TILE_BOX_EDGE * (tile >> 4).astype(F32) + half_box,
    ]
    for k, chunk in enumerate(chunks):
        x, y, z = (chunk[c] - middle[c] for c in range(3))
        squares = [x * x, y * y, z * z]
        norm = squares[0] + squares[1] + squares[2]
        xs, ys, zs, ns, rs = (parts(v) for v in (x, y, z, norm, chunk[3]))
        keep(
            feature_ref, 16 * k,
            [xs[0], ys[0], zs[0], xs[1], ys[1], zs[1], ones, ns[0]]
            + [xs[2], ys[2], zs[2], ns[1], ns[2]] + rs,
        )
        products = squares + [x * y, x * z, y * z]
        highs = [v.astype(BF16).astype(F32) for v in products]
        lows = [v - h for v, h in zip(products, highs)]
        keep(moment_ref, 16 * k, highs + [none] * 2 + lows + [none] * 2)
        if own_ref is not None and k == 0:
            xi, yi, zi = ([-2.0 * p for p in v] for v in (xs, ys, zs))
            keep(
                own_ref, 0,
                [xi[0], yi[0], zi[0], xi[0], yi[0], zi[0], ns[0], ones]
                + [xi[0], yi[0], zi[0], ones, ones] + [none] * 3
                + [xi[1], yi[1], zi[1], xi[1], yi[1], zi[1], ns[1], none]
                + [xi[2], yi[2], zi[2], none, none, none, ns[2], none]
                + rs + [x, y, z],
            )


def excess(counts, caps):
    worst = [jnp.max(n, axis=0, keepdims=True) - 8.0 * cap for n, cap in zip(counts, caps)]
    while len(worst) > 1:
        worst = [jnp.maximum(worst[0], worst[1])] + worst[2:]
    return worst[0]


def pick_rows(arrays, starts, size):
    return [jnp.concatenate([v[at : at + size] for at in starts], axis=0) for v in arrays]


def pair_loop(chunks, first_chunk, own_ref, sum_ref, even_ref, odd_ref):
    caps = CAPS[first_chunk : first_chunk + len(chunks)]
    starts = [8 * sum(caps[:k]) for k in range(len(caps))]
    sub = iota((8, TILE), 0)

    def own_side(t):
        radii = [own_ref[pl.ds((32 + p) * PITCH_ROWS + t, 1), :] for p in range(3)]
        radii = [jnp.where(sub == 6, jnp.broadcast_to(r, (8, TILE)), 0.0) for r in radii]
        reach = [radii[0], jnp.where(sub >= 5, 1.0, 0.0), radii[1], radii[2]]
        return jnp.concatenate(
            [own_ref[pl.ds(t, 32, stride=PITCH_ROWS), :], jnp.concatenate(reach, axis=0)], axis=1
        ).astype(BF16)

    def measure_pairs(t, k, rhs, ref):
        source, _, n = chunks[k]
        rows = source[pl.ds(16 * n * PITCH_ROWS + t, 16, stride=PITCH_ROWS), :]
        first = rows[:8]
        lhs = jnp.concatenate([rows, first, first], axis=0).T.astype(BF16)
        size = 8 * caps[k]
        ref[starts[k] : starts[k] + size, :] = jnp.dot(lhs[:size], rhs, preferred_element_type=F32)

    def forces(k, ref):
        size = 8 * caps[k]
        square = jnp.maximum(ref[starts[k] : starts[k] + size, :TILE], 1e-12)
        distance = square * lax.rsqrt(square)
        overlap = jnp.maximum(ref[starts[k] : starts[k] + size, TILE:] - distance, 0.0)
        below = distance + SOFTEN
        guess = pl.reciprocal(below, approx=True)
        force = overlap * (guess * (2.0 - below * guess))
        if first_chunk + k == 0:
            at = iota((TILE, TILE), 0) == iota((TILE, TILE), 1)
            force = jnp.where(at, 0.0, force)
        high = force.astype(BF16)
        low = (force - high.astype(F32)).astype(BF16)
        rest = TILE - size
        if rest:
            none = jnp.zeros((rest, TILE), BF16)
            high, low = (jnp.concatenate([v, none], axis=0) for v in (high, low))
        return high, low

    def add_up(t, found):
        moments = []
        for features, products, n in chunks:
            first = features[pl.ds(16 * n * PITCH_ROWS + t, 8, stride=PITCH_ROWS), :]
            more = products[pl.ds(16 * n * PITCH_ROWS + t, 16, stride=PITCH_ROWS), :]
            moments.append(jnp.concatenate([first, more, first], axis=0))
        lhs = jnp.concatenate(moments, axis=1).astype(BF16)
        highs = jnp.concatenate([p[0] for p in found], axis=0)
        lows = jnp.concatenate([p[1] for p in found], axis=0)
        one = jnp.dot(lhs, highs, preferred_element_type=F32)
        two = jnp.dot(lhs[:16], lows, preferred_element_type=F32)
        sum_ref[pl.ds(t, 8, stride=PITCH_ROWS), :] = one[:8] + two[:8]
        sum_ref[pl.ds(8 * PITCH_ROWS + t, 8, stride=PITCH_ROWS), :] = one[8:16] + (one[16:24] + two[8:])

    def step(t, here_ref, next_t, next_ref):
        rhs = own_side(next_t)
        found = []
        for k in range(len(chunks)):
            measure_pairs(next_t, k, rhs, next_ref)
            found.append(forces(k, here_ref))
        add_up(t, found)

    first_rhs = own_side(0)
    for k in range(len(chunks)):
        measure_pairs(0, k, first_rhs, even_ref)

    def eight_tiles(q, carry):
        refs = (even_ref, odd_ref)
        for i in range(8):
            t = 8 * q + i
            step(t, refs[i % 2], t + 1 if i < 7 else jnp.minimum(t + 1, NB - 1), refs[1 - i % 2])
        return carry

    lax.fori_loop(0, NB // 8, eight_tiles, 0)


def table(rows):
    return on_chip((rows * PITCH_ROWS, TILE))


def pair_space(chunks, groups):
    return [table(16 * chunks), table(16 * chunks)] + [pltpu.VMEM((8 * groups, 2 * TILE), F32)] * 2


def own_kernel(grains_ref, own_ref, sum_ref, feature_ref, moment_ref, even_ref, odd_ref):
    keep_chunks([[grains_ref[c] for c in range(4)]], feature_ref, moment_ref, own_ref)
    pair_loop([(feature_ref, moment_ref, 0)], 0, own_ref, sum_ref, even_ref, odd_ref)


def pair_own(grains):
    return plain_call(own_kernel, [table(38), table(16)], "own", held(grains), scratch=pair_space(1, CAPS[0]))


def near_kernel(grid_ref, lists_ref, excess_ref, feature_ref, moment_ref):
    tri = running_sums()
    here = in_this_frame(grid_ref)
    low_z = TILE_BOX_EDGE * (iota((64, TILE), 0) >> 5).astype(F32)
    low_y = TILE_BOX_EDGE * ((iota((32, TILE), 0) >> 3) & 1).astype(F32)
    cut_z = lambda start: [v[32 * start : 32 * start + 64] for v in here]
    cut_y = lambda arrays, start: pick_rows(arrays, (8 * start, 32 + 8 * start), 16)
    level = cut_z(1)
    ((beside_z, count_z),) = pack([[near(cut_z(0), 2, low_z, -1), near(cut_z(2), 2, low_z, 1)]], tri)
    ((beside_y, count_y),) = pack(
        [
            [
                near(cut_y(level, 0), 1, low_y, -1),
                near(cut_y(beside_z, 0), 1, low_y, -1),
                near(cut_y(level, 2), 1, low_y, 1),
                near(cut_y(beside_z, 2), 1, low_y, 1),
            ]
        ],
        tri,
    )
    excess_ref[...] = excess((count_z, count_y), CAPS[1:3])
    chunks = [cut_y(beside_z, 1), beside_y]
    for k in range(2):
        for c in range(4):
            lists_ref[4 * k + c] = chunks[k][c]
    keep_chunks(chunks, feature_ref, moment_ref)


def find_near(grid):
    shapes = [on_chip((8, NB, TILE)), on_chip((1, TILE)), table(2 * 16), table(2 * 16)]
    return plain_call(near_kernel, shapes, "near", held(grid))


def two_along_z():
    return lax.axis_size("gz") == 2


def field_rows():
    return 80 + (48 if two_along_z() else 80)


def stress_kernel(
    grid_ref, side_ref, grains_ref, plane_ref, own_ref, own_sum_ref,
    lists_ref, excess_ref, feature_near_ref, moment_near_ref,
    rim0_ref, rim1_ref, out_ref,
    all_ref, contact_ref, height_ref, wide_ref, feature_far_ref, moment_far_ref, sum_ref, even_ref, odd_ref,
):
    tri = running_sums()
    sides = beside_in_this_frame(side_ref)

    edge = [jnp.concatenate([low, high], axis=0) for low, high in zip(*sides)]
    row = iota((8, TILE), 0)
    low_z = TILE_BOX_EDGE * ((row >> 1) & 1).astype(F32)
    low_y = TILE_BOX_EDGE * (row & 1).astype(F32)

    def around(dz, dy):
        return pick_rows(edge, [16 * s + 4 * (z + 1 + dz) + 1 + dy for s in range(2) for z in range(2)], 2)

    def near_edge(dz, dy):
        arrays = around(dz, dy)
        mask = jnp.where(row < 4, arrays[0], SPAN_X - arrays[0]) >= -REACH
        for axis, low, step in ((2, low_z, dz), (1, low_y, dy)):
            if step:
                mask = mask & near(arrays, axis, low, step)[0]
        return mask & (arrays[3] > 0.0), arrays

    beside_edge = [(dz, dy) for dz in (-1, 0, 1) for dy in (-1, 0, 1) if dz or dy]
    ((edge_z, count_e),) = pack([[near_edge(dz, dy) for dz, dy in beside_edge]], tri)
    edge_own = around(0, 0)
    empty = jnp.zeros((8, TILE), F32)
    edge_y = [empty, empty, empty, empty + ABSENT]

    low_x = TILE_BOX_EDGE * (iota((NB, TILE), 0) & 7).astype(F32)
    in_box_x = iota((4, 8, TILE), 1)

    def along_x(arrays, edges, step):
        found = []
        for value, rim in zip(arrays, edges):
            moved = pltpu.roll(value.reshape(4, 8, TILE), 1 if step < 0 else 7, 1)
            rim = rim[:4] if step < 0 else rim[4:]
            at_edge = in_box_x == (0 if step < 0 else 7)
            found.append(jnp.where(at_edge, rim[:, None, :], moved).reshape(NB, TILE))
        return near(found, 0, low_x, step)

    own = [grains_ref[c * NB : (c + 1) * NB, :] for c in range(4)]
    list_z = [lists_ref[c] for c in range(4)]
    list_y = [lists_ref[4 + c] for c in range(4)]
    (beside, count_x), (beside_rest, count_w) = pack(
        [
            [along_x(own, edge_own, -1), along_x(own, edge_own, 1)],
            [
                along_x(list_z, edge_z, -1),
                along_x(list_y, edge_y, -1),
                along_x(list_z, edge_z, 1),
                along_x(list_y, edge_y, 1),
            ],
        ],
        tri,
    )
    keep_chunks([beside, beside_rest], feature_far_ref, moment_far_ref)
    overflow = jnp.maximum(
        excess_ref[...], excess((count_e, count_x, count_w), (TILE // 8,) + CAPS[3:])
    )
    overflow = jnp.max(overflow)

    at_z = iota((8, TILE), 0)
    centres_inner = centres(at_z + 4)
    if two_along_z():
        centres_rim = centres((at_z & 3) + jnp.where(lax.axis_index("gz") == 0, 12, 0))
    else:
        centres_rim = centres(jnp.where(at_z < 4, at_z, at_z + 8))

    def put_height(t):
        rows = [grains_ref[pl.ds(r * NB + t, 1), :] for r in range(2, 7)]
        wz_inner = weights(rows[0], centres_inner)
        wz_rim = weights(rows[0], centres_rim)
        masses = 4.0 * math.pi / 3.0 * rows[1] * rows[1] * rows[1]
        vel = rows[2:]
        cont = [contact_ref[pl.ds(k * NB + t, 1), :] for k in range(6)]
        loads = [masses, masses * vel[0], masses * vel[1], masses * vel[2]]
        for k, (i, j) in enumerate(((0, 0), (1, 1), (2, 2), (0, 1), (0, 2), (1, 2))):
            loads.append(cont[k] + masses * (vel[i] * vel[j]))
        height = [load * wz_inner for load in loads]
        if two_along_z():
            height += [jnp.where(at_z < 4, loads[c], loads[c + 1]) * wz_rim for c in range(0, 10, 2)]
            height.append(jnp.zeros((8, TILE), F32))
        else:
            height += [load * wz_rim for load in loads]
        lanes = pl.ds(pl.multiple_of(t * TILE, TILE), TILE)
        height_ref[:, lanes] = jnp.concatenate(height, axis=0).astype(BF16)

    def own_rows(t):
        return tuple(
            jnp.broadcast_to(grains_ref[pl.ds(c * NB + t, 1), :], (8, TILE)) for c in range(4)
        )

    def group(columns, first, g):
        return tuple(
            jnp.broadcast_to(columns[8 * g : 8 * g + 8, first + c : first + c + 1], (8, TILE)) for c in range(4)
        )

    def put(t, sums):
        for k in range(6):
            contact_ref[pl.ds(k * NB + t, 1), :] = jnp.sum(sums[k], axis=0, keepdims=True)

    zeros = tuple(jnp.zeros((8, TILE), F32) for _ in range(6))

    @pl.when(overflow <= 0.0)
    def _():
        tables = [(feature_near_ref, moment_near_ref, k) for k in range(2)]
        tables += [(feature_far_ref, moment_far_ref, k) for k in range(2)]
        pair_loop(tables, 1, own_ref, sum_ref, even_ref, odd_ref)
        rows = lambda ref, m: ref[m * PITCH_ROWS : m * PITCH_ROWS + NB, :]
        total = [rows(sum_ref, m) + rows(own_sum_ref, m) for m in range(14)]
        first = [total[c] + total[3 + c] for c in range(3)]
        own_mid = [own_ref[(35 + c) * PITCH_ROWS : (35 + c) * PITCH_ROWS + NB, :] for c in range(3)]
        for k, (i, j) in enumerate(((0, 0), (1, 1), (2, 2), (0, 1), (0, 2), (1, 2))):
            a, b = own_mid[i], own_mid[j]
            contact_ref[k * NB : (k + 1) * NB, :] = (0.5 * SPRING) * (
                total[8 + k] - (a * first[j] + b * first[i]) + a * b * total[6]
            )

    @pl.when(overflow > 0.0)
    def _():
        stride = 16 * 8 + 32
        here = in_this_frame(grid_ref)
        for c in range(4):
            all_ref[c * stride : c * stride + 128, :] = here[c]
            all_ref[c * stride + 128 : c * stride + 144, :] = sides[0][c]
            all_ref[c * stride + 144 : c * stride + 160, :] = sides[1][c]
        all_ref[4 * stride : 8 * stride, :] = jnp.zeros((4 * stride, TILE), F32)

        def one_tile(t, carry):
            own = own_rows(t)
            tile_x, tile_y, tile_z = t & 7, (t >> 3) & 1, t >> 4

            def one_near(n, sums):
                n_x = n // 9
                n_y = (n - 9 * n_x) // 3
                n_z = n - 9 * n_x - 3 * n_y
                at_x = tile_x + n_x - 1
                plane = 4 * (tile_z + n_z) + tile_y + n_y
                place = jnp.where(
                    at_x < 0, 128 + plane, jnp.where(at_x > 7, 144 + plane, 8 * plane + at_x)
                )
                columns = all_ref[pl.ds(place, 8, stride=stride), :].T
                for g in range(16):
                    sums = pair_terms(own, group(columns, 0, g), sums)
                return sums

            put(t, lax.fori_loop(0, 27, one_near, zeros))
            return carry

        lax.fori_loop(0, NB, one_tile, 0)

    def four_heights(q, carry):
        for i in range(4):
            put_height(4 * q + i)
        return carry

    lax.fori_loop(0, NB // 4, four_heights, 0)
    wide_ref[...] = jnp.zeros(wide_ref.shape, F32)
    for pair in range(BOXES_DOWNSLOPE // 2):
        first, last = max(0, 8 * pair - 4), min(32, 8 * pair + 12)
        begin, end = first // 16 * 16, -(-last // 16) * 16
        spans = [(64 * side, 64) for side, at in ((0, 0), (1, BOXES_DOWNSLOPE // 2 - 1)) if pair == at]
        spans += [(TILE + 32 * y + begin, end - begin) for y in range(8)]
        spans.append((3 * TILE + 8 * first, 8 * (last - first)))
        found = 0.0
        for row in range(NB // BOXES_DOWNSLOPE):
            lanes = slice(TILE * (BOXES_DOWNSLOPE * row + 2 * pair), TILE * (BOXES_DOWNSLOPE * row + 2 * pair + 2))
            planes = jnp.concatenate([plane_ref[at : at + size, lanes] for at, size in spans], axis=0)
            found = found + lax.dot_general(
                planes, height_ref[:, lanes], (((1,), (1,)), ((), ())), preferred_element_type=F32
            )
        done = 0
        for at, size in spans:
            wide_ref[at : at + size, :] += found[done : done + size]
            done += size
    wide = wide_ref[...].T
    out_ref[...] = wide[:, TILE:]
    rim = wide[:, :TILE]
    rim = jnp.where(is_even("gx"), pltpu.roll(rim, 64, 1), rim)
    half = field_rows() // 2
    upper, lower = rim[:half], rim[half:]
    left_half = iota((half, TILE), 1) < 64
    rim0_ref[...] = jnp.where(left_half, upper, pltpu.roll(lower, 64, 1))
    rim1_ref[...] = jnp.where(left_half, pltpu.roll(upper, 64, 1), lower)


def stress_and_deposit(grid, side, grains, plane, *tables):
    rows = field_rows()
    return plain_call(
        stress_kernel,
        [on_chip((rows // 2, TILE)), on_chip((rows // 2, TILE)), on_chip((rows, 2 * TILE + COLS))],
        "stress_deposit",
        held(grid),
        held(side),
        held(grains),
        held(plane),
        *(held(v) for v in tables),
        scratch=[
            pltpu.VMEM((8 * 160, TILE), F32),
            pltpu.VMEM((6 * NB, TILE), F32),
            pltpu.VMEM((rows, NB * TILE), BF16),
            pltpu.VMEM((3 * TILE + COLS, rows), F32),
            pltpu.VMEM((2 * 16 * PITCH_ROWS, TILE), F32),
            pltpu.VMEM((2 * 16 * PITCH_ROWS, TILE), F32),
            pltpu.VMEM((16 * PITCH_ROWS, TILE), F32),
            pltpu.VMEM((8 * sum(CAPS[1:]), 2 * TILE), F32),
            pltpu.VMEM((8 * sum(CAPS[1:]), 2 * TILE), F32),
        ],
    )


def rim_x_kernel(wide_ref, first_ref, second_ref, rim0_ref, rim1_ref, inner_ref):
    even = is_even("gx")
    right = jnp.where(even, first_ref[...], second_ref[...])
    left = jnp.where(even, second_ref[...], first_ref[...])
    left_half = iota(left.shape, 1) < 64
    got = jnp.concatenate(
        [
            jnp.where(left_half, right, pltpu.roll(left, 64, 1)),
            jnp.where(left_half, pltpu.roll(right, 64, 1), left),
        ],
        axis=0,
    )
    src = iota((TILE, 1), 0)
    x = (src >> 4) & 3
    x = jnp.where(src >= 64, x, x + (CELLS_PER_EDGE * BOXES_DOWNSLOPE - 4))
    y = src & 15
    target = jnp.where(y < 4, y * 32 + x, jnp.where(y >= 12, 128 + (y - 12) * 32 + x, 256 + x * 8 + y - 4))
    onehot = jnp.where(iota((TILE, 512), 1) == target, 1.0, 0.0).astype(BF16)
    total = wide_ref[...] + pick(got, onehot)
    low, high = total[:, :TILE], total[:, TILE : 2 * TILE]
    even = is_even("gy")
    rim0_ref[...] = jnp.where(even, high, low)
    rim1_ref[...] = jnp.where(even, low, high)
    inner_ref[...] = total[:, 2 * TILE :]


def add_rim_y(inner_ref, first_ref, second_ref):
    even = is_even("gy")
    right = jnp.where(even, first_ref[...], second_ref[...])
    left = jnp.where(even, second_ref[...], first_ref[...])
    got = jnp.concatenate([left, right], axis=1)
    src = iota((256, 1), 0)
    target = (src & 31) * 8 + 4 * (src >> 7) + ((src >> 5) & 3)
    onehot = jnp.where(iota((256, 256), 1) == target, 1.0, 0.0).astype(BF16)
    return inner_ref[...] + pick(got, onehot)


def rim_y_kernel(inner_ref, first_ref, second_ref, out_ref):
    out_ref[...] = add_rim_y(inner_ref, first_ref, second_ref)


PROFILED = (0, 1, 4, 5, 6, 8)


def rim_y_two_kernel(inner_ref, first_ref, second_ref, out_ref, send_ref):
    total = add_rim_y(inner_ref, first_ref, second_ref)
    out_ref[...] = total
    lower = lax.axis_index("gz") == 0
    send_ref[:40, :] = total[80:120, :TILE]
    send_ref[40:80, :] = total[80:120, TILE:]
    for i, c in enumerate(PROFILED):
        rows = total[8 * c : 8 * c + 8]
        send_ref[80 + 8 * i : 88 + 8 * i, :] = jnp.where(lower, rows[:, TILE:], rows[:, :TILE])


def finish_two_kernel(total_ref, got_ref, fields_ref, fits_ref, inertial_ref):
    lower = lax.axis_index("gz") == 0
    row = iota((8, COLS), 0)
    from_rim = jnp.where(lower, 7 - row, row)
    ours = from_rim < 4
    theirs = from_rim[:, :TILE] >= 4
    fields = []
    for p in range(5):
        got = jnp.concatenate(
            [got_ref[8 * p : 8 * p + 8, :], got_ref[40 + 8 * p : 48 + 8 * p, :]], axis=1
        )
        turned = pltpu.roll(got, 4, 0)
        for i, add in enumerate(
            (jnp.where(lower, turned, got), jnp.where(lower, got, turned))
        ):
            c = 2 * p + i
            fields.append(total_ref[8 * c : 8 * c + 8, :] + jnp.where(ours, add, 0.0))
            fields_ref[0, 0, 0, c] = fields[c]
    column = {}
    for i, c in enumerate(PROFILED):
        mine = jnp.where(lower, fields[c][:, :TILE], fields[c][:, TILE:])
        rim = total_ref[80 + 8 * (c // 2) : 88 + 8 * (c // 2), :]
        rim = jnp.where(lower, rim[:, :TILE], rim[:, TILE:])
        rim = jnp.where(lower == (c % 2 == 0), rim, pltpu.roll(rim, 4, 0))
        other = got_ref[80 + 8 * i : 88 + 8 * i, :] + jnp.where(theirs, rim, 0.0)
        column[c] = jnp.concatenate(
            [jnp.where(lower, mine, other), jnp.where(lower, other, mine)], axis=0
        )
    density = column[0]
    velocity = column[1] / (density + FLOOR_LEVEL)
    press = (column[4] + column[5] + column[6]) / 3.0
    fitted, inertial = column_fit(density, velocity, column[8], press)
    fits_ref[0, 0] = fitted
    inertial_ref[0, 0] = inertial


def held(array):
    return pltpu.with_memory_space_constraint(array, pltpu.VMEM)


def on_chip(shape, dtype=F32):
    return pltpu.VMEM(shape, dtype)


def plain_call(kernel, shapes, name, *args, scratch=()):
    vmem = pl.BlockSpec(memory_space=pltpu.VMEM)
    return pl.pallas_call(
        kernel,
        out_shape=shapes,
        in_specs=[vmem] * len(args),
        out_specs=jax.tree.map(lambda _: vmem, shapes),
        scratch_shapes=scratch,
        compiler_params=pltpu.CompilerParams(vmem_limit_bytes=KERNEL_VMEM),
        name=name,
    )(*args)


def column_fit(density, velocity, shear, press):
    upper = jnp.concatenate([velocity[1:, :], velocity[-1:, :]], axis=0)
    lower = jnp.concatenate([velocity[:1, :], velocity[:-1, :]], axis=0)
    rate = (upper - lower) / (2.0 * PITCH)
    inertial = rate * 1.0 / jnp.sqrt((press + FLOOR_LEVEL) / (density + FLOOR_LEVEL))
    friction = shear / (press + FLOOR_LEVEL)
    weight = density + FLOOR_LEVEL
    add = lambda v: jnp.sum(v, axis=0, keepdims=True)
    sum_zero = add(weight)
    sum_one = add(weight * inertial)
    sum_two = add(weight * inertial * inertial) + RIDGE_SHARE * sum_zero
    mix_zero = add(weight * friction)
    mix_one = add(weight * friction * inertial)
    determ = sum_zero * sum_two - sum_one * sum_one
    fitted = jnp.concatenate(
        [
            (mix_zero * sum_two - sum_one * mix_one) / determ,
            (sum_zero * mix_one - sum_one * mix_zero) / determ,
        ],
        axis=0,
    )
    return fitted, inertial


def swaps(first, second, axis):
    count = lax.axis_size(axis)
    got = []
    for start, value in ((0, first), (1, second)):
        links = []
        for i in range(start, count - 1, 2):
            links += [(i, i + 1), (i + 1, i)]
        got.append(lax.ppermute(value, axis, links) if links else jnp.zeros_like(value))
    return got


def exchange(low, high, axis):
    even = is_even(axis)
    one, two = swaps(jnp.where(even, high, low), jnp.where(even, low, high), axis)
    return jnp.where(even, two, one), jnp.where(even, one, two)


def local(grains, pairs):
    own, near = box_sort(grains, pairs)
    cube = near.reshape(4, 2, 2, 8, TILE)
    sends, placed = lax.optimization_barrier(((cube[:, 0], cube[:, 1]), own))
    own_table, own_sums = pair_own(placed)
    below, above = exchange(*sends, "gz")
    cube = jnp.concatenate([below[:, None], cube, above[:, None]], axis=1)
    sends = (cube[:, :, 0], cube[:, :, 1])
    sends, placed, own_table, own_sums = lax.optimization_barrier((sends, own, own_table, own_sums))
    plane = plain_call(
        plane_kernel, on_chip((3 * TILE + COLS, NB * TILE), BF16), "plane", held(placed)
    )
    below, above = exchange(*sends, "gy")
    cube = jnp.concatenate([below[:, :, None], cube, above[:, :, None]], axis=2)
    cube, plane = lax.optimization_barrier((cube, plane))
    sends = (cube[:, :, :, 0], cube[:, :, :, 7])
    sends, placed = lax.optimization_barrier((sends, cube))
    tables = find_near(placed.reshape(4, 128, TILE))
    below, above = exchange(*sends, "gx")
    side = jnp.stack([below, above]).reshape(2, 4, 16, TILE)
    rim0, rim1, wide = stress_and_deposit(
        cube.reshape(4, 128, TILE), side, own.reshape(7 * NB, TILE), plane, own_table, own_sums, *tables
    )
    first, second = swaps(rim0, rim1, "gx")
    rows = field_rows()
    block, square = on_chip((rows, TILE)), on_chip((rows, COLS))
    rim0, rim1, inner = plain_call(
        rim_x_kernel, [block, block, square], "rim_x", held(wide), held(first), held(second)
    )
    first, second = swaps(rim0, rim1, "gy")
    if two_along_z():
        sends = on_chip((128, TILE))
        total, send = plain_call(
            rim_y_two_kernel, [square, sends], "rim_y", held(inner), held(first), held(second)
        )
        got, _ = swaps(send, send, "gz")
        outs = [(1, 1, 1, 10, 8, COLS), (1, 1, 2, TILE), (1, 1, 16, TILE)]
        outs = [jax.ShapeDtypeStruct(shape, F32) for shape in outs]
        return tuple(plain_call(finish_two_kernel, outs, "finish", held(total), held(got)))
    total = plain_call(rim_y_kernel, square, "rim_y", held(inner), held(first), held(second))
    fields = total[:80].reshape(10, 8, COLS)
    rim = total[80:].reshape(10, 8, COLS)
    from_below, from_above = exchange(rim[:, :4], rim[:, 4:], "gz")
    fields = fields + jnp.concatenate([from_below, from_above], axis=1)
    share = COLS // lax.axis_size("gz")
    start = lax.axis_index("gz") * share
    density = fields[0]
    velocity = fields[1] / (density + FLOOR_LEVEL)
    shear = fields[8]
    press = (fields[4] + fields[5] + fields[6]) / 3.0
    profile = jnp.stack([density, velocity, shear, press])
    whole = lax.all_gather(profile, "gz", axis=1, tiled=True)
    whole = lax.dynamic_slice_in_dim(whole, start, share, 2)
    fitted, inertial = column_fit(*whole)
    return (fields[None, None, None], fitted[None, None], inertial[None, None])


def solution(mesh):
    in_specs = (P("gx", "gy", "gz", None, None), P("gx", "gy", "gz", None, None))
    out_specs = (
        P("gx", "gy", "gz", None, None, None),
        P("gx", "gy", None, "gz"),
        P("gx", "gy", None, "gz"),
    )
    return jax.shard_map(local, mesh=mesh, in_specs=in_specs, out_specs=out_specs, check_vma=False)
```

```python
import math

import jax
import jax.numpy as jnp
from jax import lax
from jax.experimental import pallas as pl
from jax.experimental.pallas import tpu as pltpu
from jax.sharding import PartitionSpec as P

TILE = 128
BOXES_DOWNSLOPE = 8
BOXES_SPANWISE = 2
BOXES_NORMAL = 2
CELLS_PER_EDGE = 4

TILE_BOX_EDGE = 5.0
SPRING = 2.0
SOFTEN = 0.05
FLOOR_LEVEL = 0.1
RIDGE_SHARE = 0.1
CUT_LEVEL = math.exp(-12.5)
NORM_ONE = 1.0 / math.sqrt(2.0 * math.pi)

PITCH = TILE_BOX_EDGE / CELLS_PER_EDGE
REACH = 1.21
ABSENT = -10.0

NB = BOXES_DOWNSLOPE * BOXES_SPANWISE * BOXES_NORMAL
PITCH_ROWS = NB + 8
COLS = CELLS_PER_EDGE * BOXES_DOWNSLOPE * CELLS_PER_EDGE * BOXES_SPANWISE
CAPS = (16, 12, 16, 12, 14)

KERNEL_VMEM = 32 * 1024 * 1024

F32 = jnp.float32
BF16 = jnp.bfloat16


def iota(shape, dim):
    return lax.broadcasted_iota(jnp.int32, shape, dim)


def split3(value):
    high = value.astype(BF16)
    rest = value - high.astype(F32)
    mid = rest.astype(BF16)
    low = (rest - mid.astype(F32)).astype(BF16)
    return high, mid, low


def pick(value, onehot):
    high, mid, low = split3(value)
    dot = lambda part: jnp.dot(part, onehot, preferred_element_type=F32)
    return (dot(low) + dot(mid)) + dot(high)


def is_last(axis):
    return lax.axis_index(axis) == lax.axis_size(axis) - 1


def is_even(axis):
    return lax.axis_index(axis) % 2 == 0


def sort_kernel(grains_ref, pairs_ref, own_ref, near_ref):
    flags = {(part, value): jnp.zeros((1, NB), F32) for part in "yz" for value in (0, 2)}
    for n in range(pairs_ref.shape[0]):
        pair = pairs_ref[n]
        hood = jnp.where(pair >= 0, pair, 13 * NB) >> 5
        third = (hood * 11) >> 5
        parts = {"y": third - 3 * ((third * 11) >> 5), "z": hood - 3 * third}
        flags = {k: jnp.where(parts[k[0]] == k[1], 1.0, f) for k, f in flags.items()}

    def upper(part, axis):
        alone = jnp.where(is_last(axis), 1.0 - flags[part, 0], 0.0)
        return jnp.maximum(flags[part, 2], alone)

    group = 64.0 * upper("y", "gy") + 128.0 * upper("z", "gz")
    rows = [grains_ref[r] for r in range(7)]
    centre = 0.5 * (jnp.min(rows[0], axis=1, keepdims=True) + jnp.max(rows[0], axis=1, keepdims=True))
    sub = iota((NB, TILE), 0)
    lane = iota((NB, TILE), 1)
    same = sub == lane
    group = jnp.concatenate([group, jnp.zeros((1, TILE - NB), F32)], axis=1)
    key = centre + jnp.sum(jnp.where(same, group, 0.0), axis=1, keepdims=True)
    wide = jnp.broadcast_to(key, (NB, TILE))
    key_row = jnp.sum(jnp.where(same, wide, 0.0), axis=0, keepdims=True)
    before = (wide < key_row) | ((wide == key_row) & (sub < lane))
    rank = jnp.sum(jnp.where(before, 1.0, 0.0), axis=0, keepdims=True)
    onehot = jnp.where((rank == sub.astype(F32)) & (lane < NB), 1.0, 0.0).astype(BF16)[:, :NB]
    for r in range(7):
        high, mid, low = split3(rows[r])
        dot = lambda part: jnp.dot(onehot, part, preferred_element_type=F32)
        value = (dot(low) + dot(mid)) + dot(high)
        own_ref[r] = value
        if r < 4:
            near_ref[r] = value


def box_sort(grains, pairs):
    shapes = [on_chip((7, NB, TILE)), on_chip((4, NB, TILE))]
    listed = pairs.transpose(0, 1, 2, 4, 3).reshape(pairs.shape[4], 1, NB)
    arrays = (pltpu.with_memory_space_constraint(a, pltpu.HBM) for a in (grains.reshape(7, NB, TILE), listed))
    return plain_call(sort_kernel, shapes, "box_sort", *arrays)


def lane_take(value, index):
    dims = lax.GatherDimensionNumbers(
        offset_dims=(),
        collapsed_slice_dims=(1,),
        start_index_map=(1,),
        operand_batching_dims=(0,),
        start_indices_batching_dims=(0,),
    )
    return lax.gather(
        value, index[..., None], dims, (1, 1), mode=lax.GatherScatterMode.PROMISE_IN_BOUNDS
    )


def pack(groups, tri):
    masks = [jnp.where(mask, 1.0, 0.0).astype(BF16) for lists in groups for mask, _ in lists]
    both = jnp.dot(jnp.concatenate(masks, axis=0), tri, preferred_element_type=F32)
    rows = masks[0].shape[0]
    ranks = both[:, :TILE]
    totals = [both[n * rows : (n + 1) * rows, TILE : 2 * TILE] for n in range(len(masks))]
    upto = {m: both[:, (2 + i) * TILE : (3 + i) * TILE] for i, m in enumerate(LANDMARKS)}
    offsets, ends, at = [], [], 0
    for lists in groups:
        offset = jnp.zeros((rows, TILE), F32)
        for _ in lists:
            offsets.append(offset)
            offset = offset + totals[at]
            at += 1
        ends.append(offset)
    lane_f = iota((rows, TILE), 1).astype(F32)
    wanted = jnp.concatenate([lane_f - offset for offset in offsets], axis=0)
    by_64 = upto[63] <= wanted
    by_32 = jnp.where(by_64, upto[95], upto[31]) <= wanted
    probe = jnp.where(by_64, jnp.where(by_32, upto[111], upto[79]), jnp.where(by_32, upto[47], upto[15]))
    place = jnp.where(by_64, 64, 0) + jnp.where(by_32, 32, 0) + jnp.where(probe <= wanted, 16, 0)
    for bit in (8, 4, 2, 1):
        place = jnp.where(lane_take(ranks, place + (bit - 1)) <= wanted, place + bit, place)
    packed, at = [], 0
    for lists, end in zip(groups, ends):
        outs = [jnp.zeros((rows, TILE), F32)] * 3 + [jnp.full((rows, TILE), ABSENT, F32)]
        for _, arrays in lists:
            here = slice(at * rows, (at + 1) * rows)
            ours = (wanted[here] >= 0.0) & (wanted[here] < totals[at])
            outs = [jnp.where(ours, lane_take(v, place[here]), o) for v, o in zip(arrays, outs)]
            at += 1
        packed.append((outs, end))
    return packed


def pair_terms(own, cand, sums):
    own_x, own_y, own_z, own_r = own
    cand_x, cand_y, cand_z, cand_r = cand
    dx, dy, dz = own_x - cand_x, own_y - cand_y, own_z - cand_z
    square = dx * dx + dy * dy + dz * dz
    distance = square * lax.rsqrt(jnp.maximum(square, 1e-30))
    overlap = jnp.maximum(own_r + cand_r - distance, 0.0)
    below = distance + SOFTEN
    guess = pl.reciprocal(below, approx=True)
    force = (0.5 * SPRING) * overlap * (guess * (2.0 - below * guess))
    fx, fy, fz = force * dx, force * dy, force * dz
    terms = (fx * dx, fy * dy, fz * dz, fx * dy, fx * dz, fy * dz)
    return tuple(s + t for s, t in zip(sums, terms))


def weights(coords, centres):
    diff = coords - centres
    return jnp.maximum(jnp.exp(-0.5 * diff * diff) - CUT_LEVEL, 0.0) * NORM_ONE


def centres(places):
    return (places.astype(F32) - CELLS_PER_EDGE + 0.5) * PITCH


def plane_kernel(own_ref, plane_ref):
    nx = CELLS_PER_EDGE * (BOXES_DOWNSLOPE + 2)
    ny = CELLS_PER_EDGE * (BOXES_SPANWISE + 2)

    def put_plane(t):
        wx = weights(own_ref[0, pl.ds(t, 1), :], centres(iota((nx, TILE), 0)))
        wy = weights(own_ref[1, pl.ds(t, 1), :], centres(iota((ny, TILE), 0)))
        parts = [wx[x : x + 1] * wy for x in list(range(4)) + list(range(nx - 4, nx))]
        inner_x = wx[4 : nx - 4]
        parts += [inner_x * wy[y : y + 1] for y in list(range(4)) + list(range(ny - 4, ny))]
        inner_y = wy[4 : ny - 4]
        parts += [wx[x : x + 1] * inner_y for x in range(4, nx - 4)]
        lanes = pl.ds(pl.multiple_of(t * TILE, TILE), TILE)
        plane_ref[:, lanes] = jnp.concatenate(parts, axis=0).astype(BF16)

    def four_planes(q, carry):
        for i in range(4):
            put_plane(4 * q + i)
        return carry

    lax.fori_loop(0, NB // 4, four_planes, 0)


SPAN_X = BOXES_DOWNSLOPE * TILE_BOX_EDGE
SPAN_Y = BOXES_SPANWISE * TILE_BOX_EDGE
SPAN_Z = BOXES_NORMAL * TILE_BOX_EDGE


LANDMARKS = (15, 31, 47, 63, 79, 95, 111)


def running_sums():
    row, col = iota((TILE, TILE), 0), iota((TILE, TILE), 1)
    blocks = [row <= col] + [row <= last for last in (TILE - 1,) + LANDMARKS]
    return jnp.concatenate([jnp.where(b, 1.0, 0.0) for b in blocks], axis=1).astype(BF16)


def shifts(place, span):
    return jnp.where(place == 0, -span, jnp.where(place == 3, span, 0.0))


def alive(radius):
    return jnp.where(radius == 0.0, ABSENT, radius)


def near(arrays, axis, low, step):
    limit = arrays[axis] >= low - REACH if step < 0 else arrays[axis] <= low + (TILE_BOX_EDGE + REACH)
    return limit & (arrays[3] > 0.0), arrays


def in_this_frame(grid_ref):
    row = iota((128, TILE), 0)
    return [
        grid_ref[0],
        grid_ref[1] + shifts((row >> 3) & 3, SPAN_Y),
        grid_ref[2] + shifts(row >> 5, SPAN_Z),
        alive(grid_ref[3]),
    ]


def beside_in_this_frame(side_ref):
    row = iota((16, TILE), 0)
    return [
        [
            side_ref[k, 0] + shift_x,
            side_ref[k, 1] + shifts(row & 3, SPAN_Y),
            side_ref[k, 2] + shifts(row >> 2, SPAN_Z),
            alive(side_ref[k, 3]),
        ]
        for k, shift_x in ((0, -SPAN_X), (1, SPAN_X))
    ]


def parts(value):
    return [p.astype(F32) for p in split3(value)]


def keep(ref, first, values):
    for f, value in enumerate(values):
        at = (first + f) * PITCH_ROWS
        ref[at : at + NB, :] = value


def keep_chunks(chunks, feature_ref, moment_ref, own_ref=None):
    half_box = 0.5 * TILE_BOX_EDGE
    ones = jnp.ones((NB, TILE), F32)
    none = jnp.zeros((NB, TILE), F32)
    tile = iota((NB, TILE), 0)
    middle = [
        TILE_BOX_EDGE * (tile & 7).astype(F32) + half_box,
        TILE_BOX_EDGE * ((tile >> 3) & 1).astype(F32) + half_box,
        TILE_BOX_EDGE * (tile >> 4).astype(F32) + half_box,
    ]
    for k, chunk in enumerate(chunks):
        x, y, z = (chunk[c] - middle[c] for c in range(3))
        squares = [x * x, y * y, z * z]
        norm = squares[0] + squares[1] + squares[2]
        xs, ys, zs, ns, rs = (parts(v) for v in (x, y, z, norm, chunk[3]))
        keep(
            feature_ref, 16 * k,
            [xs[0], ys[0], zs[0], xs[1], ys[1], zs[1], ones, ns[0]]
            + [xs[2], ys[2], zs[2], ns[1], ns[2]] + rs,
        )
        products = squares + [x * y, x * z, y * z]
        highs = [v.astype(BF16).astype(F32) for v in products]
        lows = [v - h for v, h in zip(products, highs)]
        keep(moment_ref, 16 * k, highs + [none] * 2 + lows + [none] * 2)
        if own_ref is not None and k == 0:
            xi, yi, zi = ([-2.0 * p for p in v] for v in (xs, ys, zs))
            keep(
                own_ref, 0,
                [xi[0], yi[0], zi[0], xi[0], yi[0], zi[0], ns[0], ones]
                + [xi[0], yi[0], zi[0], ones, ones] + [none] * 3
                + [xi[1], yi[1], zi[1], xi[1], yi[1], zi[1], ns[1], none]
                + [xi[2], yi[2], zi[2], none, none, none, ns[2], none]
                + rs + [x, y, z],
            )


def excess(counts, caps):
    worst = [jnp.max(n, axis=0, keepdims=True) - 8.0 * cap for n, cap in zip(counts, caps)]
    while len(worst) > 1:
        worst = [jnp.maximum(worst[0], worst[1])] + worst[2:]
    return worst[0]


def pick_rows(arrays, starts, size):
    return [jnp.concatenate([v[at : at + size] for at in starts], axis=0) for v in arrays]


def pair_loop(chunks, first_chunk, own_ref, sum_ref, even_ref, odd_ref):
    caps = CAPS[first_chunk : first_chunk + len(chunks)]
    starts = [8 * sum(caps[:k]) for k in range(len(caps))]
    sub = iota((8, TILE), 0)

    def own_side(t):
        radii = [own_ref[pl.ds((32 + p) * PITCH_ROWS + t, 1), :] for p in range(3)]
        radii = [jnp.where(sub == 6, jnp.broadcast_to(r, (8, TILE)), 0.0) for r in radii]
        reach = [radii[0], jnp.where(sub >= 5, 1.0, 0.0), radii[1], radii[2]]
        return jnp.concatenate(
            [own_ref[pl.ds(t, 32, stride=PITCH_ROWS), :], jnp.concatenate(reach, axis=0)], axis=1
        ).astype(BF16)

    def measure_pairs(t, k, rhs, ref):
        source, _, n = chunks[k]
        rows = source[pl.ds(16 * n * PITCH_ROWS + t, 16, stride=PITCH_ROWS), :]
        first = rows[:8]
        lhs = jnp.concatenate([rows, first, first], axis=0).T.astype(BF16)
        size = 8 * caps[k]
        ref[starts[k] : starts[k] + size, :] = jnp.dot(lhs[:size], rhs, preferred_element_type=F32)

    def forces(k, ref):
        size = 8 * caps[k]
        square = jnp.maximum(ref[starts[k] : starts[k] + size, :TILE], 1e-12)
        distance = square * lax.rsqrt(square)
        overlap = jnp.maximum(ref[starts[k] : starts[k] + size, TILE:] - distance, 0.0)
        below = distance + SOFTEN
        guess = pl.reciprocal(below, approx=True)
        force = overlap * (guess * (2.0 - below * guess))
        if first_chunk + k == 0:
            at = iota((TILE, TILE), 0) == iota((TILE, TILE), 1)
            force = jnp.where(at, 0.0, force)
        high = force.astype(BF16)
        low = (force - high.astype(F32)).astype(BF16)
        rest = TILE - size
        if rest:
            none = jnp.zeros((rest, TILE), BF16)
            high, low = (jnp.concatenate([v, none], axis=0) for v in (high, low))
        return high, low

    def add_up(t, found):
        moments = []
        for features, products, n in chunks:
            first = features[pl.ds(16 * n * PITCH_ROWS + t, 8, stride=PITCH_ROWS), :]
            more = products[pl.ds(16 * n * PITCH_ROWS + t, 16, stride=PITCH_ROWS), :]
            moments.append(jnp.concatenate([first, more, first], axis=0))
        lhs = jnp.concatenate(moments, axis=1).astype(BF16)
        highs = jnp.concatenate([p[0] for p in found], axis=0)
        lows = jnp.concatenate([p[1] for p in found], axis=0)
        one = jnp.dot(lhs, highs, preferred_element_type=F32)
        two = jnp.dot(lhs[:16], lows, preferred_element_type=F32)
        sum_ref[pl.ds(t, 8, stride=PITCH_ROWS), :] = one[:8] + two[:8]
        sum_ref[pl.ds(8 * PITCH_ROWS + t, 8, stride=PITCH_ROWS), :] = one[8:16] + (one[16:24] + two[8:])

    def step(t, here_ref, next_t, next_ref):
        rhs = own_side(next_t)
        found = []
        for k in range(len(chunks)):
            measure_pairs(next_t, k, rhs, next_ref)
            found.append(forces(k, here_ref))
        add_up(t, found)

    first_rhs = own_side(0)
    for k in range(len(chunks)):
        measure_pairs(0, k, first_rhs, even_ref)

    def eight_tiles(q, carry):
        refs = (even_ref, odd_ref)
        for i in range(8):
            t = 8 * q + i
            step(t, refs[i % 2], t + 1 if i < 7 else jnp.minimum(t + 1, NB - 1), refs[1 - i % 2])
        return carry

    lax.fori_loop(0, NB // 8, eight_tiles, 0)


def table(rows):
    return on_chip((rows * PITCH_ROWS, TILE))


def pair_space(chunks, groups):
    return [table(16 * chunks), table(16 * chunks)] + [pltpu.VMEM((8 * groups, 2 * TILE), F32)] * 2


def own_kernel(grains_ref, own_ref, sum_ref, feature_ref, moment_ref, even_ref, odd_ref):
    keep_chunks([[grains_ref[c] for c in range(4)]], feature_ref, moment_ref, own_ref)
    pair_loop([(feature_ref, moment_ref, 0)], 0, own_ref, sum_ref, even_ref, odd_ref)


def pair_own(grains):
    return plain_call(own_kernel, [table(38), table(16)], "own", held(grains), scratch=pair_space(1, CAPS[0]))


def near_kernel(grid_ref, lists_ref, excess_ref, feature_ref, moment_ref):
    tri = running_sums()
    here = in_this_frame(grid_ref)
    low_z = TILE_BOX_EDGE * (iota((64, TILE), 0) >> 5).astype(F32)
    low_y = TILE_BOX_EDGE * ((iota((32, TILE), 0) >> 3) & 1).astype(F32)
    cut_z = lambda start: [v[32 * start : 32 * start + 64] for v in here]
    cut_y = lambda arrays, start: pick_rows(arrays, (8 * start, 32 + 8 * start), 16)
    level = cut_z(1)
    ((beside_z, count_z),) = pack([[near(cut_z(0), 2, low_z, -1), near(cut_z(2), 2, low_z, 1)]], tri)
    ((beside_y, count_y),) = pack(
        [
            [
                near(cut_y(level, 0), 1, low_y, -1),
                near(cut_y(beside_z, 0), 1, low_y, -1),
                near(cut_y(level, 2), 1, low_y, 1),
                near(cut_y(beside_z, 2), 1, low_y, 1),
            ]
        ],
        tri,
    )
    excess_ref[...] = excess((count_z, count_y), CAPS[1:3])
    chunks = [cut_y(beside_z, 1), beside_y]
    for k in range(2):
        for c in range(4):
            lists_ref[4 * k + c] = chunks[k][c]
    keep_chunks(chunks, feature_ref, moment_ref)


def find_near(grid):
    shapes = [on_chip((8, NB, TILE)), on_chip((1, TILE)), table(2 * 16), table(2 * 16)]
    return plain_call(near_kernel, shapes, "near", held(grid))


def two_along_z():
    return lax.axis_size("gz") == 2


def field_rows():
    return 80 + (48 if two_along_z() else 80)


def stress_kernel(
    grid_ref, side_ref, grains_ref, plane_ref, own_ref, own_sum_ref,
    lists_ref, excess_ref, feature_near_ref, moment_near_ref,
    rim0_ref, rim1_ref, out_ref,
    all_ref, contact_ref, height_ref, wide_ref, feature_far_ref, moment_far_ref, sum_ref, even_ref, odd_ref,
):
    tri = running_sums()
    sides = beside_in_this_frame(side_ref)

    edge = [jnp.concatenate([low, high], axis=0) for low, high in zip(*sides)]
    row = iota((8, TILE), 0)
    low_z = TILE_BOX_EDGE * ((row >> 1) & 1).astype(F32)
    low_y = TILE_BOX_EDGE * (row & 1).astype(F32)

    def around(dz, dy):
        return pick_rows(edge, [16 * s + 4 * (z + 1 + dz) + 1 + dy for s in range(2) for z in range(2)], 2)

    def near_edge(dz, dy):
        arrays = around(dz, dy)
        mask = jnp.where(row < 4, arrays[0], SPAN_X - arrays[0]) >= -REACH
        for axis, low, step in ((2, low_z, dz), (1, low_y, dy)):
            if step:
                mask = mask & near(arrays, axis, low, step)[0]
        return mask & (arrays[3] > 0.0), arrays

    beside_edge = [(dz, dy) for dz in (-1, 0, 1) for dy in (-1, 0, 1) if dz or dy]
    ((edge_z, count_e),) = pack([[near_edge(dz, dy) for dz, dy in beside_edge]], tri)
    edge_own = around(0, 0)
    empty = jnp.zeros((8, TILE), F32)
    edge_y = [empty, empty, empty, empty + ABSENT]

    low_x = TILE_BOX_EDGE * (iota((NB, TILE), 0) & 7).astype(F32)
    in_box_x = iota((4, 8, TILE), 1)

    def along_x(arrays, edges, step):
        found = []
        for value, rim in zip(arrays, edges):
            moved = pltpu.roll(value.reshape(4, 8, TILE), 1 if step < 0 else 7, 1)
            rim = rim[:4] if step < 0 else rim[4:]
            at_edge = in_box_x == (0 if step < 0 else 7)
            found.append(jnp.where(at_edge, rim[:, None, :], moved).reshape(NB, TILE))
        return near(found, 0, low_x, step)

    own = [grains_ref[c * NB : (c + 1) * NB, :] for c in range(4)]
    list_z = [lists_ref[c] for c in range(4)]
    list_y = [lists_ref[4 + c] for c in range(4)]
    (beside, count_x), (beside_rest, count_w) = pack(
        [
            [along_x(own, edge_own, -1), along_x(own, edge_own, 1)],
            [
                along_x(list_z, edge_z, -1),
                along_x(list_y, edge_y, -1),
                along_x(list_z, edge_z, 1),
                along_x(list_y, edge_y, 1),
            ],
        ],
        tri,
    )
    keep_chunks([beside, beside_rest], feature_far_ref, moment_far_ref)
    overflow = jnp.maximum(
        excess_ref[...], excess((count_e, count_x, count_w), (TILE // 8,) + CAPS[3:])
    )
    overflow = jnp.max(overflow)

    at_z = iota((8, TILE), 0)
    centres_inner = centres(at_z + 4)
    if two_along_z():
        centres_rim = centres((at_z & 3) + jnp.where(lax.axis_index("gz") == 0, 12, 0))
    else:
        centres_rim = centres(jnp.where(at_z < 4, at_z, at_z + 8))

    def put_height(t):
        rows = [grains_ref[pl.ds(r * NB + t, 1), :] for r in range(2, 7)]
        wz_inner = weights(rows[0], centres_inner)
        wz_rim = weights(rows[0], centres_rim)
        masses = 4.0 * math.pi / 3.0 * rows[1] * rows[1] * rows[1]
        vel = rows[2:]
        cont = [contact_ref[pl.ds(k * NB + t, 1), :] for k in range(6)]
        loads = [masses, masses * vel[0], masses * vel[1], masses * vel[2]]
        for k, (i, j) in enumerate(((0, 0), (1, 1), (2, 2), (0, 1), (0, 2), (1, 2))):
            loads.append(cont[k] + masses * (vel[i] * vel[j]))
        height = [load * wz_inner for load in loads]
        if two_along_z():
            height += [jnp.where(at_z < 4, loads[c], loads[c + 1]) * wz_rim for c in range(0, 10, 2)]
            height.append(jnp.zeros((8, TILE), F32))
        else:
            height += [load * wz_rim for load in loads]
        lanes = pl.ds(pl.multiple_of(t * TILE, TILE), TILE)
        height_ref[:, lanes] = jnp.concatenate(height, axis=0).astype(BF16)

    def own_rows(t):
        return tuple(
            jnp.broadcast_to(grains_ref[pl.ds(c * NB + t, 1), :], (8, TILE)) for c in range(4)
        )

    def group(columns, first, g):
        return tuple(
            jnp.broadcast_to(columns[8 * g : 8 * g + 8, first + c : first + c + 1], (8, TILE)) for c in range(4)
        )

    def put(t, sums):
        for k in range(6):
            contact_ref[pl.ds(k * NB + t, 1), :] = jnp.sum(sums[k], axis=0, keepdims=True)

    zeros = tuple(jnp.zeros((8, TILE), F32) for _ in range(6))

    @pl.when(overflow <= 0.0)
    def _():
        tables = [(feature_near_ref, moment_near_ref, k) for k in range(2)]
        tables += [(feature_far_ref, moment_far_ref, k) for k in range(2)]
        pair_loop(tables, 1, own_ref, sum_ref, even_ref, odd_ref)
        rows = lambda ref, m: ref[m * PITCH_ROWS : m * PITCH_ROWS + NB, :]
        total = [rows(sum_ref, m) + rows(own_sum_ref, m) for m in range(14)]
        first = [total[c] + total[3 + c] for c in range(3)]
        own_mid = [own_ref[(35 + c) * PITCH_ROWS : (35 + c) * PITCH_ROWS + NB, :] for c in range(3)]
        for k, (i, j) in enumerate(((0, 0), (1, 1), (2, 2), (0, 1), (0, 2), (1, 2))):
            a, b = own_mid[i], own_mid[j]
            contact_ref[k * NB : (k + 1) * NB, :] = (0.5 * SPRING) * (
                total[8 + k] - (a * first[j] + b * first[i]) + a * b * total[6]
            )

    @pl.when(overflow > 0.0)
    def _():
        stride = 16 * 8 + 32
        here = in_this_frame(grid_ref)
        for c in range(4):
            all_ref[c * stride : c * stride + 128, :] = here[c]
            all_ref[c * stride + 128 : c * stride + 144, :] = sides[0][c]
            all_ref[c * stride + 144 : c * stride + 160, :] = sides[1][c]
        all_ref[4 * stride : 8 * stride, :] = jnp.zeros((4 * stride, TILE), F32)

        def one_tile(t, carry):
            own = own_rows(t)
            tile_x, tile_y, tile_z = t & 7, (t >> 3) & 1, t >> 4

            def one_near(n, sums):
                n_x = n // 9
                n_y = (n - 9 * n_x) // 3
                n_z = n - 9 * n_x - 3 * n_y
                at_x = tile_x + n_x - 1
                plane = 4 * (tile_z + n_z) + tile_y + n_y
                place = jnp.where(
                    at_x < 0, 128 + plane, jnp.where(at_x > 7, 144 + plane, 8 * plane + at_x)
                )
                columns = all_ref[pl.ds(place, 8, stride=stride), :].T
                for g in range(16):
                    sums = pair_terms(own, group(columns, 0, g), sums)
                return sums

            put(t, lax.fori_loop(0, 27, one_near, zeros))
            return carry

        lax.fori_loop(0, NB, one_tile, 0)

    def eight_heights(q, carry):
        for i in range(8):
            put_height(8 * q + i)
        return carry

    lax.fori_loop(0, NB // 8, eight_heights, 0)
    wide_ref[...] = jnp.zeros(wide_ref.shape, F32)
    for pair in range(BOXES_DOWNSLOPE // 2):
        first, last = max(0, 8 * pair - 4), min(32, 8 * pair + 12)
        begin, end = first // 16 * 16, -(-last // 16) * 16
        spans = [(64 * side, 64) for side, at in ((0, 0), (1, BOXES_DOWNSLOPE // 2 - 1)) if pair == at]
        spans += [(TILE + 32 * y + begin, end - begin) for y in range(8)]
        spans.append((3 * TILE + 8 * first, 8 * (last - first)))
        found = 0.0
        for row in range(NB // BOXES_DOWNSLOPE):
            lanes = slice(TILE * (BOXES_DOWNSLOPE * row + 2 * pair), TILE * (BOXES_DOWNSLOPE * row + 2 * pair + 2))
            planes = jnp.concatenate([plane_ref[at : at + size, lanes] for at, size in spans], axis=0)
            found = found + lax.dot_general(
                planes, height_ref[:, lanes], (((1,), (1,)), ((), ())), preferred_element_type=F32
            )
        done = 0
        for at, size in spans:
            wide_ref[at : at + size, :] += found[done : done + size]
            done += size
    wide = wide_ref[...].T
    out_ref[...] = wide[:, TILE:]
    rim = wide[:, :TILE]
    rim = jnp.where(is_even("gx"), pltpu.roll(rim, 64, 1), rim)
    half = field_rows() // 2
    upper, lower = rim[:half], rim[half:]
    left_half = iota((half, TILE), 1) < 64
    rim0_ref[...] = jnp.where(left_half, upper, pltpu.roll(lower, 64, 1))
    rim1_ref[...] = jnp.where(left_half, pltpu.roll(upper, 64, 1), lower)


def stress_and_deposit(grid, side, grains, plane, *tables):
    rows = field_rows()
    return plain_call(
        stress_kernel,
        [on_chip((rows // 2, TILE)), on_chip((rows // 2, TILE)), on_chip((rows, 2 * TILE + COLS))],
        "stress_deposit",
        held(grid),
        held(side),
        held(grains),
        held(plane),
        *(held(v) for v in tables),
        scratch=[
            pltpu.VMEM((8 * 160, TILE), F32),
            pltpu.VMEM((6 * NB, TILE), F32),
            pltpu.VMEM((rows, NB * TILE), BF16),
            pltpu.VMEM((3 * TILE + COLS, rows), F32),
            pltpu.VMEM((2 * 16 * PITCH_ROWS, TILE), F32),
            pltpu.VMEM((2 * 16 * PITCH_ROWS, TILE), F32),
            pltpu.VMEM((16 * PITCH_ROWS, TILE), F32),
            pltpu.VMEM((8 * sum(CAPS[1:]), 2 * TILE), F32),
            pltpu.VMEM((8 * sum(CAPS[1:]), 2 * TILE), F32),
        ],
    )


def rim_x_kernel(wide_ref, first_ref, second_ref, rim0_ref, rim1_ref, inner_ref):
    even = is_even("gx")
    right = jnp.where(even, first_ref[...], second_ref[...])
    left = jnp.where(even, second_ref[...], first_ref[...])
    left_half = iota(left.shape, 1) < 64
    got = jnp.concatenate(
        [
            jnp.where(left_half, right, pltpu.roll(left, 64, 1)),
            jnp.where(left_half, pltpu.roll(right, 64, 1), left),
        ],
        axis=0,
    )
    src = iota((TILE, 1), 0)
    x = (src >> 4) & 3
    x = jnp.where(src >= 64, x, x + (CELLS_PER_EDGE * BOXES_DOWNSLOPE - 4))
    y = src & 15
    target = jnp.where(y < 4, y * 32 + x, jnp.where(y >= 12, 128 + (y - 12) * 32 + x, 256 + x * 8 + y - 4))
    onehot = jnp.where(iota((TILE, 512), 1) == target, 1.0, 0.0).astype(BF16)
    total = wide_ref[...] + pick(got, onehot)
    low, high = total[:, :TILE], total[:, TILE : 2 * TILE]
    even = is_even("gy")
    rim0_ref[...] = jnp.where(even, high, low)
    rim1_ref[...] = jnp.where(even, low, high)
    inner_ref[...] = total[:, 2 * TILE :]


def add_rim_y(inner_ref, first_ref, second_ref):
    even = is_even("gy")
    right = jnp.where(even, first_ref[...], second_ref[...])
    left = jnp.where(even, second_ref[...], first_ref[...])
    got = jnp.concatenate([left, right], axis=1)
    src = iota((256, 1), 0)
    target = (src & 31) * 8 + 4 * (src >> 7) + ((src >> 5) & 3)
    onehot = jnp.where(iota((256, 256), 1) == target, 1.0, 0.0).astype(BF16)
    return inner_ref[...] + pick(got, onehot)


def rim_y_kernel(inner_ref, first_ref, second_ref, out_ref):
    out_ref[...] = add_rim_y(inner_ref, first_ref, second_ref)


PROFILED = (0, 1, 4, 5, 6, 8)


def rim_y_two_kernel(inner_ref, first_ref, second_ref, out_ref, send_ref):
    total = add_rim_y(inner_ref, first_ref, second_ref)
    out_ref[...] = total
    lower = lax.axis_index("gz") == 0
    send_ref[:40, :] = total[80:120, :TILE]
    send_ref[40:80, :] = total[80:120, TILE:]
    for i, c in enumerate(PROFILED):
        rows = total[8 * c : 8 * c + 8]
        send_ref[80 + 8 * i : 88 + 8 * i, :] = jnp.where(lower, rows[:, TILE:], rows[:, :TILE])


def finish_two_kernel(total_ref, got_ref, fields_ref, fits_ref, inertial_ref):
    lower = lax.axis_index("gz") == 0
    row = iota((8, COLS), 0)
    from_rim = jnp.where(lower, 7 - row, row)
    ours = from_rim < 4
    theirs = from_rim[:, :TILE] >= 4
    fields = []
    for p in range(5):
        got = jnp.concatenate(
            [got_ref[8 * p : 8 * p + 8, :], got_ref[40 + 8 * p : 48 + 8 * p, :]], axis=1
        )
        turned = pltpu.roll(got, 4, 0)
        for i, add in enumerate(
            (jnp.where(lower, turned, got), jnp.where(lower, got, turned))
        ):
            c = 2 * p + i
            fields.append(total_ref[8 * c : 8 * c + 8, :] + jnp.where(ours, add, 0.0))
            fields_ref[0, 0, 0, c] = fields[c]
    column = {}
    for i, c in enumerate(PROFILED):
        mine = jnp.where(lower, fields[c][:, :TILE], fields[c][:, TILE:])
        rim = total_ref[80 + 8 * (c // 2) : 88 + 8 * (c // 2), :]
        rim = jnp.where(lower, rim[:, :TILE], rim[:, TILE:])
        rim = jnp.where(lower == (c % 2 == 0), rim, pltpu.roll(rim, 4, 0))
        other = got_ref[80 + 8 * i : 88 + 8 * i, :] + jnp.where(theirs, rim, 0.0)
        column[c] = jnp.concatenate(
            [jnp.where(lower, mine, other), jnp.where(lower, other, mine)], axis=0
        )
    density = column[0]
    velocity = column[1] / (density + FLOOR_LEVEL)
    press = (column[4] + column[5] + column[6]) / 3.0
    fitted, inertial = column_fit(density, velocity, column[8], press)
    fits_ref[0, 0] = fitted
    inertial_ref[0, 0] = inertial


def held(array):
    return pltpu.with_memory_space_constraint(array, pltpu.VMEM)


def on_chip(shape, dtype=F32):
    return pltpu.VMEM(shape, dtype)


def plain_call(kernel, shapes, name, *args, scratch=()):
    vmem = pl.BlockSpec(memory_space=pltpu.VMEM)
    return pl.pallas_call(
        kernel,
        out_shape=shapes,
        in_specs=[vmem] * len(args),
        out_specs=jax.tree.map(lambda _: vmem, shapes),
        scratch_shapes=scratch,
        compiler_params=pltpu.CompilerParams(vmem_limit_bytes=KERNEL_VMEM),
        name=name,
    )(*args)


def column_fit(density, velocity, shear, press):
    upper = jnp.concatenate([velocity[1:, :], velocity[-1:, :]], axis=0)
    lower = jnp.concatenate([velocity[:1, :], velocity[:-1, :]], axis=0)
    rate = (upper - lower) / (2.0 * PITCH)
    inertial = rate * 1.0 / jnp.sqrt((press + FLOOR_LEVEL) / (density + FLOOR_LEVEL))
    friction = shear / (press + FLOOR_LEVEL)
    weight = density + FLOOR_LEVEL
    add = lambda v: jnp.sum(v, axis=0, keepdims=True)
    sum_zero = add(weight)
    sum_one = add(weight * inertial)
    sum_two = add(weight * inertial * inertial) + RIDGE_SHARE * sum_zero
    mix_zero = add(weight * friction)
    mix_one = add(weight * friction * inertial)
    determ = sum_zero * sum_two - sum_one * sum_one
    fitted = jnp.concatenate(
        [
            (mix_zero * sum_two - sum_one * mix_one) / determ,
            (sum_zero * mix_one - sum_one * mix_zero) / determ,
        ],
        axis=0,
    )
    return fitted, inertial


def swaps(first, second, axis):
    count = lax.axis_size(axis)
    got = []
    for start, value in ((0, first), (1, second)):
        links = []
        for i in range(start, count - 1, 2):
            links += [(i, i + 1), (i + 1, i)]
        got.append(lax.ppermute(value, axis, links) if links else jnp.zeros_like(value))
    return got


def exchange(low, high, axis):
    even = is_even(axis)
    one, two = swaps(jnp.where(even, high, low), jnp.where(even, low, high), axis)
    return jnp.where(even, two, one), jnp.where(even, one, two)


def local(grains, pairs):
    own, near = box_sort(grains, pairs)
    cube = near.reshape(4, 2, 2, 8, TILE)
    sends, placed = lax.optimization_barrier(((cube[:, 0], cube[:, 1]), own))
    own_table, own_sums = pair_own(placed)
    below, above = exchange(*sends, "gz")
    cube = jnp.concatenate([below[:, None], cube, above[:, None]], axis=1)
    sends = (cube[:, :, 0], cube[:, :, 1])
    sends, placed, own_table, own_sums = lax.optimization_barrier((sends, own, own_table, own_sums))
    plane = plain_call(
        plane_kernel, on_chip((3 * TILE + COLS, NB * TILE), BF16), "plane", held(placed)
    )
    below, above = exchange(*sends, "gy")
    cube = jnp.concatenate([below[:, :, None], cube, above[:, :, None]], axis=2)
    cube, plane = lax.optimization_barrier((cube, plane))
    sends = (cube[:, :, :, 0], cube[:, :, :, 7])
    sends, placed = lax.optimization_barrier((sends, cube))
    tables = find_near(placed.reshape(4, 128, TILE))
    below, above = exchange(*sends, "gx")
    side = jnp.stack([below, above]).reshape(2, 4, 16, TILE)
    rim0, rim1, wide = stress_and_deposit(
        cube.reshape(4, 128, TILE), side, own.reshape(7 * NB, TILE), plane, own_table, own_sums, *tables
    )
    first, second = swaps(rim0, rim1, "gx")
    rows = field_rows()
    block, square = on_chip((rows, TILE)), on_chip((rows, COLS))
    rim0, rim1, inner = plain_call(
        rim_x_kernel, [block, block, square], "rim_x", held(wide), held(first), held(second)
    )
    first, second = swaps(rim0, rim1, "gy")
    if two_along_z():
        sends = on_chip((128, TILE))
        total, send = plain_call(
            rim_y_two_kernel, [square, sends], "rim_y", held(inner), held(first), held(second)
        )
        got, _ = swaps(send, send, "gz")
        outs = [(1, 1, 1, 10, 8, COLS), (1, 1, 2, TILE), (1, 1, 16, TILE)]
        outs = [jax.ShapeDtypeStruct(shape, F32) for shape in outs]
        return tuple(plain_call(finish_two_kernel, outs, "finish", held(total), held(got)))
    total = plain_call(rim_y_kernel, square, "rim_y", held(inner), held(first), held(second))
    fields = total[:80].reshape(10, 8, COLS)
    rim = total[80:].reshape(10, 8, COLS)
    from_below, from_above = exchange(rim[:, :4], rim[:, 4:], "gz")
    fields = fields + jnp.concatenate([from_below, from_above], axis=1)
    share = COLS // lax.axis_size("gz")
    start = lax.axis_index("gz") * share
    density = fields[0]
    velocity = fields[1] / (density + FLOOR_LEVEL)
    shear = fields[8]
    press = (fields[4] + fields[5] + fields[6]) / 3.0
    profile = jnp.stack([density, velocity, shear, press])
    whole = lax.all_gather(profile, "gz", axis=1, tiled=True)
    whole = lax.dynamic_slice_in_dim(whole, start, share, 2)
    fitted, inertial = column_fit(*whole)
    return (fields[None, None, None], fitted[None, None], inertial[None, None])


def solution(mesh):
    in_specs = (P("gx", "gy", "gz", None, None), P("gx", "gy", "gz", None, None))
    out_specs = (
        P("gx", "gy", "gz", None, None, None),
        P("gx", "gy", None, "gz"),
        P("gx", "gy", None, "gz"),
    )
    return jax.shard_map(local, mesh=mesh, in_specs=in_specs, out_specs=out_specs, check_vma=False)
```
